32 devices in a mesh: dp: 8 (over z, x), mp: 4 (over y, core).
Axes of the slice: x: 2, y: 2, z: 4, core: 2. Of those that a mesh axis runs over, the one named last changes fastest.
Arguments:
- tokens: bfloat16 [16, 1024, 1024], P('dp', 'mp'), may hold values from -6 to 6
- lengths: int32 [16], P('dp'), may hold values from 256 to 1024, as said below
- attn_norm: bfloat16 [1024], P('dp'), may hold values from 0.099609375 to 1.8984375
- qkv_weight: bfloat16 [3, 1024, 1024], P(None, 'dp', 'mp'), may hold values from -0.25 to 0.25
- attn_out_weight: bfloat16 [1024, 1024], P('mp', 'dp'), may hold values from -1.5 to 1.5
- ffn_norm: bfloat16 [1024], P('dp'), may hold values from 0.099609375 to 1.8984375
- ffn_in_weight: bfloat16 [2, 1024, 2624], P(None, 'dp', 'mp'), may hold values from -0.1875 to 0.1875
- ffn_out_weight: bfloat16 [2624, 1024], P('mp', 'dp'), may hold values from -0.125 to 0.125
- out_grad: bfloat16 [16, 1024, 1024], P('dp', 'mp'), may hold values from -6 to 6
Outputs:
- output: bfloat16 [16, 1024, 1024], P('dp', 'mp')
- grad_input: bfloat16 [16, 1024, 1024], P('dp', 'mp')
- grad_attn_norm: float32 [1024], P('dp')
- grad_qkv: float32 [3, 1024, 1024], P(None, 'dp', 'mp')
- grad_attn_out: float32 [1024, 1024], P('mp', 'dp')
- grad_ffn_norm: float32 [1024], P('dp')
- grad_ffn_in: float32 [2, 1024, 2624], P(None, 'dp', 'mp')
- grad_ffn_out: float32 [2624, 1024], P('mp', 'dp')
The draws below stay inside these ranges and needn't reach their ends.
Inputs may be any that keep to these rules, and one draw needn't show every extreme that they name: Sequence s holds valid tokens at positions 0 to lengths[s] - 1 and padding after; some sequence has exactly 1024 and some exactly 256.
All inputs are finite; a program needn't handle non-finite values.
Results may differ from the reference program's by a relative error of at most 0.02.
Values may be sent and summed in bfloat16 or wider, within the bound.
No kernel may reach another device: no remote copies, remote signals or barrier semaphores. Data moves between devices by JAX's collectives and lax.ppermute only.
A program may use at most 192 MiB of HBM per device.

```python
import jax
import jax.numpy as jnp
from jax import lax

D = 1024
H = 16
HD = 64
FF = 2624
LEN = 1024
MIN_LEN = 256
SEQS = 16


def draw_lengths(key, part):
    key_base, key_top, key_low = jax.random.split(key, 3)
    drawn_lengths = jax.random.randint(key_base, (SEQS,), MIN_LEN, LEN + 1)
    top_index = jax.random.randint(key_top, (), 0, SEQS)
    low_index = (top_index + 1 + jax.random.randint(key_low, (), 0, SEQS - 1)) % SEQS
    drawn_lengths = drawn_lengths.at[top_index].set(LEN)
    drawn_lengths = drawn_lengths.at[low_index].set(MIN_LEN)
    return drawn_lengths.astype(jnp.int32)


def raised(values, rng, source, target, shards_of, factor):
    def block_of(dim):
        return (jnp.arange(values.shape[dim]) // (values.shape[dim] // shards_of)).reshape((-1,) + (1,) * (values.ndim - 1 - dim))

    one_side = jax.random.permutation(rng, shards_of)[block_of(target)]
    far = (block_of(target) + shards_of // 2) % shards_of
    return jnp.where((block_of(source) == one_side) | (block_of(source) == far), factor * values, values)


def levels(stream_key, extent, pieces, least, top_value):
    gain, own = 1.0, jax.random.fold_in(stream_key, 6)
    for axis_at, shards_of in pieces:
        draws = jnp.exp(jax.random.uniform(jax.random.fold_in(own, axis_at), (shards_of,), jnp.float32, least / len(pieces), top_value / len(pieces)))
        gain = gain * jnp.repeat(draws, extent[axis_at] // shards_of).reshape([-1 if axis == axis_at else 1 for axis in range(len(extent))])
    return gain


def scatter_about(own_key, dims, width, most, pieces=(), kind=jnp.bfloat16):
    values = jax.random.normal(own_key, dims, jnp.float32) * width
    if len(pieces) > 0:
        values = levels(own_key, dims, pieces, -0.22, 0.18) * values
    return jnp.clip(values, min=-most, max=most).astype(kind)


def heavy_noise(own_key, dims, deviation, most, pieces, heavy, kind=jnp.bfloat16):
    values = deviation * jax.random.normal(own_key, dims, jnp.float32)
    if pieces:
        values = values * levels(own_key, dims, pieces, -0.22, 0.18)
    return jnp.clip(raised(values, jax.random.fold_in(own_key, 3), *heavy), -most, most).astype(kind)


def setup_inputs(seed: int = 0) -> dict:
    key_of = jax.random.split(jax.random.key(seed), 10)
    tokens = heavy_noise(key_of[0], (SEQS, LEN, D), 1.0, 6.0, ((0, 8), (1, 4)), (0, 2, 8, 2.0))
    lengths = draw_lengths(jax.random.fold_in(key_of[9], 71), 0)
    attn_norm = jnp.clip(1.0 + 0.18 * jax.random.normal(key_of[2], (D,), jnp.float32), 0.099609375, 1.8984375).astype(jnp.bfloat16)
    qkv_weight = scatter_about(key_of[3], (3, D, D), (D // 2) ** -0.5, 0.25, ((1, 8), (2, 4)))
    attn_out_weight = scatter_about(key_of[4], (D, D), (D // 64) ** -0.5, 1.5, ((0, 4), (1, 8)))
    ffn_norm = jnp.clip(1.0 + 0.18 * jax.random.normal(key_of[5], (D,), jnp.float32), 0.099609375, 1.8984375).astype(jnp.bfloat16)
    ffn_in_weight = scatter_about(key_of[6], (2, D, FF), D ** -0.5, 0.1875, ((1, 8), (2, 4)))
    ffn_out_weight = scatter_about(key_of[7], (FF, D), FF ** -0.5, 0.125, ((0, 4), (1, 8)))
    out_grad = heavy_noise(key_of[8], (SEQS, LEN, D), 1.0, 6.0, ((0, 8), (1, 4)), (0, 2, 8, 2.0))
    return {"tokens": tokens, "lengths": lengths, "attn_norm": attn_norm, "qkv_weight": qkv_weight, "attn_out_weight": attn_out_weight, "ffn_norm": ffn_norm, "ffn_in_weight": ffn_in_weight, "ffn_out_weight": ffn_out_weight, "out_grad": out_grad}


norm_eps = 1e-05
rope_base = 160000.0

@jax.custom_vjp
def low(v):
    return lax.optimization_barrier(v.astype(jnp.bfloat16)).astype(jnp.float32)

@jax.custom_vjp
def low_back(v):
    return v

def low_keep(v):
    return (low(v), None)

def low_pass(kept, grad):
    return (grad,)

def back_keep(v):
    return (v, None)

def back_low(kept, grad):
    return (low(grad),)
low.defvjp(low_keep, low_pass)
low_back.defvjp(back_keep, back_low)

def layer_norm(values, norm_gain):
    average = lax.optimization_barrier(jnp.mean(values, axis=-1, keepdims=True))
    centred = values - average
    spread = lax.optimization_barrier(jnp.mean(centred * centred, axis=-1, keepdims=True))
    return centred * lax.rsqrt(spread + norm_eps) * norm_gain

def rope_tables(length, head_size):
    places = jnp.arange(length, dtype=jnp.float32)
    frequency = rope_base ** (-jnp.arange(0, head_size, 2, dtype=jnp.float32) / head_size)
    angles = places[:, None] * frequency[None, :]
    angles = jnp.concatenate([angles, angles], axis=-1)
    return (jnp.cos(angles), jnp.sin(angles))

def rotate(values, cosine_table, sine_table):
    half_size = values.shape[-1] // 2
    turned = jnp.concatenate([-values[..., half_size:], values[..., :half_size]], axis=-1)
    return values * cosine_table + turned * sine_table

def sequence_forward(seq_rows, length, attn_gain, qkv_all, attn_out, ffn_gain, ffn_in, ffn_out):
    highest = lax.Precision.HIGHEST
    positions = jnp.arange(LEN, dtype=jnp.int32)
    row_valid = (positions < length).astype(jnp.float32)[:, None]
    key_valid = positions < length
    cosine_table, sine_table = rope_tables(LEN, HD)
    cosine_table = cosine_table[:, None, :]
    sine_table = sine_table[:, None, :]
    normed_one = low(layer_norm(seq_rows, attn_gain))
    query_pre = low_back(jnp.dot(normed_one, qkv_all[0], precision=highest))
    key_pre = low_back(jnp.dot(normed_one, qkv_all[1], precision=highest))
    value_pre = low_back(jnp.dot(normed_one, qkv_all[2], precision=highest))
    query_rows = low(rotate(query_pre.reshape(LEN, H, HD), cosine_table, sine_table))
    key_rows = low(rotate(key_pre.reshape(LEN, H, HD), cosine_table, sine_table))
    value_rows = low(value_pre.reshape(LEN, H, HD))
    scores = low_back(jnp.einsum('qhd,khd->hqk', query_rows, key_rows, precision=highest) * HD ** (-0.5))
    scores = jnp.where(key_valid[None, None, :], scores, -jnp.inf)
    probabilities = low(jax.nn.softmax(scores, axis=-1))
    context = jnp.einsum('hqk,khd->qhd', probabilities, value_rows, precision=highest).reshape(LEN, D)
    context = low_back(low(context))
    attention = low_back(jnp.dot(context, attn_out, precision=highest))
    hidden = seq_rows + attention
    normed_two = low(layer_norm(hidden, ffn_gain))
    up_rows = low_back(jnp.dot(normed_two, ffn_in[0], precision=highest))
    gate_rows = low_back(jnp.dot(normed_two, ffn_in[1], precision=highest))
    mixed_rows = low(jax.nn.gelu(up_rows, approximate=False) * gate_rows)
    feedforward = low_back(jnp.dot(mixed_rows, ffn_out, precision=highest))
    return row_valid * (hidden + feedforward)

def reference(tokens, lengths, attn_norm, qkv_weight, attn_out_weight, ffn_norm, ffn_in_weight, ffn_out_weight, out_grad):
    inputs = tuple((element.astype(jnp.float32) for element in (tokens, attn_norm, qkv_weight, attn_out_weight, ffn_norm, ffn_in_weight, ffn_out_weight)))
    step_fn = jax.checkpoint(sequence_forward)

    def whole_layer(seq_all, attn_gain, qkv_all, attn_out, ffn_gain, ffn_in, ffn_out):

        def one_sequence(seq_pair):
            return step_fn(seq_pair[0], seq_pair[1], attn_gain, qkv_all, attn_out, ffn_gain, ffn_in, ffn_out)
        return lax.map(one_sequence, (seq_all, lengths))
    result, pullback = jax.vjp(whole_layer, *inputs)
    gradients = pullback(out_grad.astype(jnp.float32))
    return (result.astype(jnp.bfloat16), gradients[0].astype(jnp.bfloat16), gradients[1], gradients[2], gradients[3], gradients[4], gradients[5], gradients[6])
```

```python
import functools

import jax
import jax.numpy as jnp
import numpy as np
from jax import lax
from jax.experimental import pallas as pl
from jax.experimental.pallas import tpu as pltpu
from jax.sharding import PartitionSpec as P

HD = 64
norm_eps = 1e-05
rope_base = 160000.0
SCALE = HD ** (-0.5)
LOG2E = 1.4426950408889634
BF = jnp.bfloat16
F32 = jnp.float32


def exchange(value, axis, bit):
    size = lax.axis_size(axis)
    return lax.ppermute(value, axis, [(i, i ^ bit) for i in range(size)])


def after(value, *done):
    return lax.optimization_barrier((value, done))[0]


def bits_of(size):
    assert size & (size - 1) == 0
    return [1 << i for i in reversed(range(size.bit_length() - 1))]


def rank_order(size):
    order = [0]
    for bit in bits_of(size):
        order = order + [o ^ bit for o in order]
    return order


def far_first():
    return bits_of(lax.axis_size("dp"))


def near_first():
    bits = bits_of(lax.axis_size("dp"))
    return bits[-1:] + bits[:-1]


def cut(array, parts):
    size = array.shape[-1] // parts
    return [array[..., i * size : (i + 1) * size] for i in range(parts)]


def join(pieces):
    return pieces[0] if len(pieces) == 1 else jnp.concatenate(pieces, axis=-1)


def gather_steps(shard, order):
    held = []
    for bit in order:
        got = exchange(shard, "dp", bit)
        outer = 2 ** sum(1 for other in held if other < bit)
        shard = join([piece for pair in zip(cut(shard, outer), cut(got, outer)) for piece in pair])
        held.append(bit)
    return shard


def halves(total, left, bit):
    outer = 2 ** sum(1 for other in left if other < bit)
    pieces = cut(total, 2 * outer)
    return join(pieces[0::2]), join(pieces[1::2])


def scatter_steps(keep, send, order):
    left = list(order)
    for bit in order:
        got = exchange(send.astype(BF), "dp", bit)
        total = keep.astype(F32) + got.astype(F32)
        left.remove(bit)
        if left:
            keep, send = halves(total, left, left[0])
    return total


def gather_rows(rows):
    across = exchange(rows, "mp", 2)
    beside = exchange(rows, "mp", 1)
    return rows, beside, across, exchange(across, "mp", 1)


def reduce_start(parts):
    far = exchange(parts[3], "mp", 1)
    away = (parts[2].astype(F32) + far.astype(F32)).astype(BF)
    return away


def reduce_end(parts, away):
    back = exchange(away, "mp", 2)
    near = exchange(parts[1], "mp", 1)
    return parts[0].astype(F32) + near.astype(F32) + back.astype(F32)


def nt(a, b):
    return lax.dot_general(a, b, (((1,), (1,)), ((), ())), preferred_element_type=F32)


def nn(a, b):
    return lax.dot_general(a, b, (((1,), (0,)), ((), ())), preferred_element_type=F32)


def tn(a, b):
    return lax.dot_general(a, b, (((0,), (0,)), ((), ())), preferred_element_type=F32)


def aligned(index, step):
    return pl.ds(pl.multiple_of(index * step, step), step)


def fetch(parts, place, sem, base=0):
    copies = [
        pltpu.make_async_copy(part, place(p), sem.at[base + p]) for p, part in enumerate(parts)
    ]
    for copy in copies:
        copy.start()
    return copies


def finish(copies):
    for copy in copies:
        copy.wait()


def send_block(spot, held_ref, outs, sem, base=0):
    for k, out in enumerate(outs):

        @pl.when(spot == k)
        def _(k=k, out=out):
            pltpu.make_async_copy(held_ref.at[k], out, sem.at[base + k]).start()


def sent_blocks(held_ref, outs, sem, base=0):
    finish([pltpu.make_async_copy(held_ref.at[k], out, sem.at[base + k]) for k, out in enumerate(outs)])


def spin(value, cos, sin):
    a, b = value[: HD // 2], value[HD // 2 :]
    return jnp.concatenate([a * cos - b * sin, b * cos + a * sin], axis=0)


def attn_fwd_kernel(
    where_ref, p0, p1, p2, p3, wa_ref, wb_ref, cos_ref, sin_ref,
    o0, o1, o2, o3, rows_ref, q_ref, k_ref, v_ref, ctx_ref, lse_ref,
    knat_ref, held_ref, sem, out_sem,
):
    me = where_ref[0]
    length = where_ref[1]
    outs = (o0, o1, o2, o3)
    block = rows_ref.shape[1]
    heads = lse_ref.shape[0]
    width = heads * HD
    count = lax.div(length + block - 1, block)
    finish(fetch((p0, p1, p2, p3), lambda p: rows_ref.at[me ^ p], sem))

    def project(i, carry):
        rows = rows_ref[i]
        spot = aligned(i, block)
        cos = cos_ref[:, spot]
        sin = sin_ref[:, spot]
        query = nt(wa_ref[:width], rows)
        key = nt(wa_ref[width:], rows)
        for h in range(heads):
            hs = slice(h * HD, (h + 1) * HD)
            q_ref[hs, spot] = spin(query[hs], cos, sin).astype(BF)
            turned = spin(key[hs], cos, sin)
            k_ref[hs, spot] = turned.astype(BF)
            knat_ref[h, spot, :] = turned.T.astype(BF)
        v_ref[:, spot] = nt(wb_ref[:width], rows).astype(BF)
        return carry

    lax.fori_loop(0, count, project, 0)

    for n in range(1, 5):

        @pl.when(count == n)
        def _(n=n):
            last = lax.broadcasted_iota(jnp.int32, (block, block), 0) + (n - 1) * block < length

            def rows_of(i, carry):
                spot = aligned(i, block)
                for h in range(heads):
                    hs = slice(h * HD, (h + 1) * HD)
                    query = q_ref[hs, spot]
                    tiles = []
                    for j in range(n):
                        tile = nn(knat_ref[h, j * block : (j + 1) * block, :], query) * (SCALE * LOG2E)
                        if j == n - 1:
                            tile = jnp.where(last, tile, -1e30)
                        tiles.append(tile)
                    top = jnp.max(functools.reduce(jnp.maximum, tiles), axis=0, keepdims=True)
                    total = jnp.zeros((1, block), F32)
                    found = jnp.zeros((HD, block), F32)
                    for j, tile in enumerate(tiles):
                        weight = jnp.exp2(tile - top)
                        total = total + jnp.sum(weight, axis=0, keepdims=True)
                        found = found + nn(v_ref[hs, j * block : (j + 1) * block], weight.astype(BF))
                    ctx_ref[hs, spot] = (found / total).astype(BF)
                    lse_ref[h, :, spot] = top + jnp.log2(total)
                out = me ^ i
                held_ref[out] = nn(ctx_ref[:, spot].T, wb_ref[width:]).astype(BF)
                send_block(out, held_ref, outs, out_sem)
                return carry

            lax.fori_loop(0, n, rows_of, 0)

    def blank(i, carry):
        out = me ^ i
        held_ref[out] = jnp.zeros(held_ref.shape[1:], BF)
        send_block(out, held_ref, outs, out_sem)
        return carry

    lax.fori_loop(count, 4, blank, 0)
    sent_blocks(held_ref, outs, out_sem)


def put_halves(keep_ref, send_ref, rows, value, outer):
    size = value.shape[-1] // (2 * outer)
    for i in range(outer):
        at = slice(i * size, (i + 1) * size)
        keep_ref[rows, at] = value[:, 2 * i * size : (2 * i + 1) * size].astype(BF)
        send_ref[rows, at] = value[:, (2 * i + 1) * size : (2 * i + 2) * size].astype(BF)


def attn_bwd_kernel(
    where_ref, p0, p1, p2, p3, rows_ref, q_ref, k_ref, v_ref, ctx_ref, lse_ref,
    wa_ref, wb_ref, cos_ref, sin_ref, *rest, old, outer,
):
    if old:
        old_ref, oldgain_ref, *rest = rest
    outs, rest = rest[:4], rest[4:]
    if old:
        keep_a, send_a, keep_b, send_b, grad_ref, gain_ref, *rest = rest
    else:
        grad_ref, gain_ref, *rest = rest
    back_ref, cb_ref, knat_ref, vnat_ref, d_ref, dk_ref, dv_ref, delta_ref, held_ref, sem, out_sem = rest
    me = where_ref[0]
    length = where_ref[1]
    block = rows_ref.shape[1]
    heads = lse_ref.shape[0]
    width = heads * HD
    count = lax.div(length + block - 1, block)
    copies = fetch((p0, p1, p2, p3), lambda p: back_ref.at[me ^ p], sem)
    if old:
        grad_ref[...] = old_ref[...]
        gain_ref[...] = oldgain_ref[...]
    else:
        grad_ref[...] = jnp.zeros(grad_ref.shape, F32)
        gain_ref[...] = jnp.zeros(gain_ref.shape, F32)
    finish(copies)

    def prepare(i, carry):
        spot = aligned(i, block)
        low = nt(wb_ref[width:], back_ref[i]).astype(BF)
        cb_ref[:, spot] = low
        ctx = ctx_ref[:, spot]
        inner = low.astype(F32) * ctx.astype(F32)
        for h in range(heads):
            hs = slice(h * HD, (h + 1) * HD)
            delta_ref[h, :, spot] = jnp.sum(inner[hs], axis=0, keepdims=True)
            knat_ref[h, spot, :] = k_ref[hs, spot].T
            vnat_ref[h, spot, :] = v_ref[hs, spot].T
        grad_ref[3 * width :, :] += nn(ctx, back_ref[i])
        return carry

    lax.fori_loop(0, count, prepare, 0)
    dk_ref[...] = jnp.zeros(dk_ref.shape, F32)
    dv_ref[...] = jnp.zeros(dv_ref.shape, F32)

    def unspin(value, spot):
        return spin(value * SCALE, cos_ref[:, spot], -sin_ref[:, spot]).astype(BF)

    for n in range(1, 5):

        @pl.when(count == n)
        def _(n=n):
            last = lax.broadcasted_iota(jnp.int32, (block, block), 0) + (n - 1) * block < length

            def rows_of(i, carry):
                spot = aligned(i, block)
                for h in range(heads):
                    hs = slice(h * HD, (h + 1) * HD)
                    query = q_ref[hs, spot]
                    cb = cb_ref[hs, spot]
                    lse = lse_ref[h, :, spot]
                    delta = delta_ref[h, :, spot]
                    dq = jnp.zeros((HD, block), F32)
                    for j in range(n):
                        js = slice(j * block, (j + 1) * block)
                        tile = nn(knat_ref[h, js, :], query) * (SCALE * LOG2E) - lse
                        if j == n - 1:
                            tile = jnp.where(last, tile, -1e30)
                        weight = jnp.exp2(tile)
                        back = nn(vnat_ref[h, js, :], cb)
                        ds = (weight * (back - delta)).astype(BF)
                        dv_ref[hs, js] += nt(cb, weight.astype(BF))
                        dk_ref[hs, js] += nt(query, ds)
                        dq = dq + nn(k_ref[hs, js], ds)
                    d_ref[hs, spot] = unspin(dq, spot)
                return carry

            lax.fori_loop(0, n, rows_of, 0)

    def close(i, carry):
        spot = aligned(i, block)
        rows = rows_ref[i]
        for h in range(heads):
            hs = slice(h * HD, (h + 1) * HD)
            d_ref[width + h * HD : width + (h + 1) * HD, spot] = unspin(dk_ref[hs, spot], spot)
        d_ref[2 * width :, spot] = dv_ref[:, spot].astype(BF)
        d = d_ref[:, spot]
        turned = d.T
        out = nn(turned[:, : 2 * width], wa_ref[...]) + nn(turned[:, 2 * width :], wb_ref[:width])
        held_ref[me ^ i] = out.astype(BF)
        send_block(me ^ i, held_ref, outs, out_sem)
        gain_ref[:1] += jnp.sum(out * rows.astype(F32), axis=0, keepdims=True)
        grad_ref[: 3 * width, :] += nn(d, rows)
        return carry

    lax.fori_loop(0, count, close, 0)

    def blank(i, carry):
        held_ref[me ^ i] = jnp.zeros(held_ref.shape[1:], BF)
        send_block(me ^ i, held_ref, outs, out_sem)
        return carry

    lax.fori_loop(count, 4, blank, 0)
    if old:
        put_halves(keep_a, send_a, slice(0, 2 * width), grad_ref[: 2 * width], outer[0])
        put_halves(keep_b, send_b, slice(0, 2 * width), grad_ref[2 * width :], outer[1])
        put_halves(keep_b, send_b, slice(2 * width, None), gain_ref[...], outer[1])
    sent_blocks(held_ref, outs, out_sem)


def ffn_kernel(
    where_ref, a0, a1, a2, a3, b0, b1, b2, b3, wu_ref, wg_ref, wo_ref,
    f0, f1, f2, f3, n0, n1, n2, n3, mixed_ref, ub_ref, gb_ref, gain_ref,
    rows_ref, back_ref, fheld_ref, nheld_ref, sem, out_sem,
):
    me = where_ref[0]
    length = where_ref[1]
    block = rows_ref.shape[1]
    copies = fetch((a0, a1, a2, a3), lambda p: rows_ref.at[p], sem)
    copies += fetch((b0, b1, b2, b3), lambda p: back_ref.at[p], sem, 4)
    gain_ref[...] = jnp.zeros(gain_ref.shape, F32)
    finish(copies)

    def step(p, carry):
        valid = (me ^ p) * block < length

        @pl.when(valid)
        def _():
            rows = rows_ref[p]
            up = nt(rows, wu_ref[...])
            gate = nt(rows, wg_ref[...])
            mb = nt(back_ref[p], wo_ref[...])
            phi = 0.5 + 0.5 * lax.erf(up * (0.5**0.5))
            act = up * phi
            mixed = (act * gate).astype(BF)
            mixed_ref[p] = mixed
            slope = phi + up * (jnp.exp(-0.5 * up * up) * (0.5 / np.pi) ** 0.5)
            ub = (mb * gate * slope).astype(BF)
            gb = (mb * act).astype(BF)
            ub_ref[p] = ub
            gb_ref[p] = gb
            out = nn(ub, wu_ref[...]) + nn(gb, wg_ref[...])
            nheld_ref[p] = out.astype(BF)
            gain_ref[:1] += jnp.sum(out * rows.astype(F32), axis=0, keepdims=True)
            fheld_ref[p] = nn(mixed, wo_ref[...]).astype(BF)

        @pl.when(jnp.logical_not(valid))
        def _():
            for ref in (mixed_ref, ub_ref, gb_ref, nheld_ref, fheld_ref):
                ref[p] = jnp.zeros(ref.shape[1:], BF)

        send_block(p, nheld_ref, (n0, n1, n2, n3), out_sem, 4)
        send_block(p, fheld_ref, (f0, f1, f2, f3), out_sem)
        return carry

    lax.fori_loop(0, 4, step, 0)
    sent_blocks(nheld_ref, (n0, n1, n2, n3), out_sem, 4)
    sent_blocks(fheld_ref, (f0, f1, f2, f3), out_sem)


def ffn_grad_kernel(*refs, outer):
    parts, refs = refs[:16], refs[16:]
    saved, gains, refs = (refs[:3], refs[3:6]), refs[6:8], refs[8:]
    keep_a, send_a, keep_b, send_b, rows_ref, back_ref, ga_ref, gb_ref, sem = refs
    units = ga_ref.shape[0] // 2
    copies = [
        fetch(parts[8 * s : 8 * s + 4], lambda p: rows_ref.at[s, p], sem, 8 * s)
        + fetch(parts[8 * s + 4 : 8 * s + 8], lambda p: back_ref.at[s, p], sem, 8 * s + 4)
        for s in range(2)
    ]
    for s, (mixed_ref, ub_ref, gate_ref) in enumerate(saved):
        finish(copies[s])
        rows = rows_ref[s].reshape(-1, rows_ref.shape[-1])
        back = back_ref[s].reshape(-1, rows_ref.shape[-1])
        flat = [ref[...].reshape(-1, units) for ref in (ub_ref, gate_ref, mixed_ref)]
        if s == 0:
            ga_ref[:units] = tn(flat[0], rows)
            ga_ref[units:] = tn(flat[1], rows)
            gb_ref[...] = tn(flat[2], back)
        else:
            put_halves(keep_a, send_a, slice(0, units), ga_ref[:units] + tn(flat[0], rows), outer[0])
            put_halves(keep_a, send_a, slice(units, None), ga_ref[units:] + tn(flat[1], rows), outer[0])
            put_halves(keep_b, send_b, slice(0, units), gb_ref[...] + tn(flat[2], back), outer[1])
    put_halves(keep_b, send_b, slice(units, None), gains[0][...] + gains[1][...], outer[1])


SMEM = pl.BlockSpec(memory_space=pltpu.SMEM)
VMEM = pl.BlockSpec(memory_space=pltpu.VMEM)
ANY = pl.BlockSpec(memory_space=pl.ANY)
LIMIT = 60 * 1024 * 1024
PARAMS = pltpu.CompilerParams(vmem_limit_bytes=LIMIT)
GAIN_ROWS = 16


def shape(*dims, kind=BF):
    return jax.ShapeDtypeStruct(dims, kind)


def first_outer(order):
    return 2 ** sum(1 for other in order if other < order[0])


def attn_fwd(where, parts, wa, wb, cos, sin):
    block, width = parts[0].shape
    cols = wa.shape[0] // 2
    heads = cols // HD
    full = 4 * block
    flops = 2 * full * width * cols * 4 + 4 * full * full * cols
    return pl.pallas_call(
        attn_fwd_kernel,
        out_shape=(shape(block, width),) * 4
        + (shape(4, block, width),)
        + (shape(cols, full),) * 4
        + (shape(heads, 1, full, kind=F32),),
        in_specs=[SMEM] + [ANY] * 4 + [VMEM] * 4,
        out_specs=(ANY,) * 4 + (VMEM,) * 6,
        scratch_shapes=[
            pltpu.VMEM((heads, full, HD), BF),
            pltpu.VMEM((4, block, width), BF),
            pltpu.SemaphoreType.DMA((4,)),
            pltpu.SemaphoreType.DMA((4,)),
        ],
        compiler_params=PARAMS,
        cost_estimate=pl.CostEstimate(flops=flops * 3, bytes_accessed=12 << 20, transcendentals=heads * full * full),
        name="attn_fwd",
    )(where, *parts, wa, wb, cos, sin)


def attn_bwd(where, parts, saved, wa, wb, cos, sin, old, orders):
    block, width = parts[0].shape
    cols = wa.shape[0] // 2
    heads = cols // HD
    full = 4 * block
    flops = 4 * full * width * cols * 4 + 10 * full * full * cols
    extra = [] if old is None else list(old)
    sums = (shape(4 * cols, width, kind=F32), shape(GAIN_ROWS, width, kind=F32))
    scratch = []
    if old is None:
        outs = (shape(block, width),) * 4 + sums
    else:
        outs = (shape(block, width),) * 4 + (shape(2 * cols, width // 2),) * 2
        outs += (shape(2 * cols + GAIN_ROWS, width // 2),) * 2
        scratch = [pltpu.VMEM(s.shape, F32) for s in sums]
    return pl.pallas_call(
        functools.partial(attn_bwd_kernel, old=old is not None, outer=[first_outer(o) for o in orders]),
        out_shape=outs,
        in_specs=[SMEM] + [ANY] * 4 + [VMEM] * (10 + len(extra)),
        out_specs=(ANY,) * 4 + (VMEM,) * (len(outs) - 4),
        scratch_shapes=scratch + [
            pltpu.VMEM((4, block, width), BF),
            pltpu.VMEM((cols, full), BF),
            pltpu.VMEM((heads, full, HD), BF),
            pltpu.VMEM((heads, full, HD), BF),
            pltpu.VMEM((3 * cols, full), BF),
            pltpu.VMEM((cols, full), F32),
            pltpu.VMEM((cols, full), F32),
            pltpu.VMEM((heads, 1, full), F32),
            pltpu.VMEM((4, block, width), BF),
            pltpu.SemaphoreType.DMA((4,)),
            pltpu.SemaphoreType.DMA((4,)),
        ],
        compiler_params=PARAMS,
        cost_estimate=pl.CostEstimate(flops=flops * 3, bytes_accessed=16 << 20, transcendentals=heads * full * full),
        name="attn_bwd",
    )(where, *parts, *saved, wa, wb, cos, sin, *extra)


def ffn(where, parts, backs, wu, wg, wo):
    block, width = parts[0].shape
    units = wo.shape[0]
    flops = 2 * 4 * block * width * units * 6
    return pl.pallas_call(
        ffn_kernel,
        out_shape=(shape(block, width),) * 8
        + (shape(4, block, units),) * 3
        + (shape(GAIN_ROWS, width, kind=F32),),
        in_specs=[SMEM] + [ANY] * 8 + [VMEM] * 3,
        out_specs=(ANY,) * 8 + (VMEM,) * 4,
        scratch_shapes=[pltpu.VMEM((4, block, width), BF)] * 4 + [pltpu.SemaphoreType.DMA((8,))] * 2,
        compiler_params=PARAMS,
        cost_estimate=pl.CostEstimate(flops=flops, bytes_accessed=20 << 20, transcendentals=2 * 4 * block * units),
        name="ffn",
    )(where, *parts, *backs, wu, wg, wo)


def ffn_grad(parts, saved, gains, orders):
    block, width = parts[0].shape
    units = saved[0].shape[2]
    return pl.pallas_call(
        functools.partial(ffn_grad_kernel, outer=[first_outer(o) for o in orders]),
        out_shape=(shape(2 * units, width // 2),) * 2 + (shape(units + GAIN_ROWS, width // 2),) * 2,
        in_specs=[ANY] * 16 + [VMEM] * 8,
        out_specs=(VMEM,) * 4,
        scratch_shapes=[pltpu.VMEM((2, 4, block, width), BF)] * 2
        + [pltpu.VMEM((2 * units, width), F32), pltpu.VMEM((units, width), F32), pltpu.SemaphoreType.DMA((16,))],
        compiler_params=PARAMS,
        cost_estimate=pl.CostEstimate(flops=2 * 8 * block * width * units * 3, bytes_accessed=24 << 20, transcendentals=0),
        name="ffn_grad",
    )(*parts, *saved, *gains)


def norm_parts(values):
    average = jnp.mean(values, axis=-1, keepdims=True)
    centred = values - average
    spread = jnp.mean(centred * centred, axis=-1, keepdims=True)
    scale = lax.rsqrt(spread + norm_eps)
    return centred * scale, scale


def norm_back(grad, gain, normed, scale):
    y = grad * gain
    return scale * (
        y - jnp.mean(y, axis=-1, keepdims=True) - normed * jnp.mean(y * normed, axis=-1, keepdims=True)
    )


def rope_tables(length):
    places = np.arange(length, dtype=np.float32)
    frequency = (rope_base ** (-np.arange(0, HD, 2, dtype=np.float32) / HD)).astype(np.float32)
    angles = (frequency[:, None] * places[None, :]).astype(np.float32)
    return jnp.asarray(np.cos(angles)), jnp.asarray(np.sin(angles))


def per_device(
    tokens, lengths, attn_norm, qkv_weight, attn_out_weight, ffn_norm, ffn_in_weight, ffn_out_weight, out_grad
):
    seqs, local_len, width = tokens.shape
    assert lax.axis_size("mp") == 4 and seqs == 2
    groups = lax.axis_size("dp")
    me = lax.axis_index("mp")
    full_len = 4 * local_len
    cols = qkv_weight.shape[2]
    units = ffn_in_weight.shape[2]
    span = width // groups
    cos, sin = rope_tables(full_len)

    order = jnp.asarray(np.array(rank_order(groups), np.int32)) ^ lax.axis_index("dp")
    source = (order[:, None] * span + jnp.arange(span, dtype=jnp.int32)[None, :]).reshape(width)
    reorder = (source[None, :] == jnp.arange(width, dtype=jnp.int32)[:, None]).astype(BF)

    def to_own(rows):
        return jnp.dot(rows, reorder, preferred_element_type=F32).astype(BF)

    def from_own(rows):
        return lax.dot_general(
            rows, reorder, (((1,), (1,)), ((), ())), preferred_element_type=F32
        ).astype(BF)

    far, near = far_first(), near_first()
    gains = gather_steps(jnp.stack([attn_norm, ffn_norm]), far).astype(F32)
    attn_gain = gains[0]
    ffn_gain = gains[1]
    qkv = jnp.swapaxes(qkv_weight, 1, 2)
    wa = gather_steps(qkv[:2].reshape(2 * cols, span), far)
    wb = gather_steps(jnp.concatenate([qkv[2], attn_out_weight], axis=0), near)
    ffn_in = jnp.swapaxes(ffn_in_weight, 1, 2)
    wu = gather_steps(ffn_in[0], far)
    wg = gather_steps(ffn_in[1], far)
    wo = gather_steps(ffn_out_weight, near)
    orders = (far[::-1], near[::-1])

    local = me * local_len + jnp.arange(local_len, dtype=jnp.int32)
    where = [jnp.stack([me, lengths[s]]).astype(jnp.int32) for s in range(seqs)]
    valid = [(local < lengths[s]).astype(F32)[:, None] for s in range(seqs)]

    own_tokens = to_own(tokens.reshape(seqs * local_len, width)).reshape(seqs, local_len, width)
    own_grad = to_own(out_grad.reshape(seqs * local_len, width)).reshape(seqs, local_len, width)
    token_rows = [own_tokens[s].astype(F32) for s in range(seqs)]
    first = [norm_parts(token_rows[s]) for s in range(seqs)]
    ones = [gather_rows((first[s][0] * attn_gain).astype(BF)) for s in range(seqs)]
    out_back = [valid[s] * own_grad[s].astype(F32) for s in range(seqs)]
    backs = [gather_rows(out_back[s].astype(BF)) for s in range(seqs)]

    saved, attention, away = [], [], []
    for s in range(seqs):
        at = where[s] if s == 0 else after(where[s], away[0])
        out = attn_fwd(at, ones[s], wa, wb, cos, sin)
        attention.append(out[:4])
        saved.append(out[4:])
        away.append(reduce_start(out[:4]))

    hidden, second, twos = [], [], []
    for s in range(seqs):
        hidden.append(token_rows[s] + reduce_end(attention[s], away[s]))
        second.append(norm_parts(hidden[s]))
        twos.append(gather_rows((second[s][0] * ffn_gain).astype(BF)))

    forward, backward, ffn_saved, ffn_gains, away = [], [], [], [], []
    for s in range(seqs):
        at = after(where[s], saved[1][-1]) if s == 0 else after(where[s], away[0])
        out = ffn(at, twos[s], backs[s], wu, wg, wo)
        forward.append(out[:4])
        backward.append(out[4:8])
        ffn_saved += out[8:11]
        ffn_gains.append(out[11])
        away.append(reduce_start(out[4:8]))

    hidden_back, low_back = [], []
    for s in range(seqs):
        two_back = reduce_end(backward[s], away[s])
        hidden_back.append(out_back[s] + norm_back(two_back, ffn_gain, *second[s]))
        low_back.append(hidden_back[s].astype(BF))
    full_back = [gather_rows(low_back[s]) for s in range(seqs)]
    ffn_gains[0] = after(ffn_gains[0], low_back[0], away[1])
    ffn_sums = ffn_grad(
        [part for s in range(seqs) for part in twos[s] + backs[s]], ffn_saved, ffn_gains, orders
    )

    outputs = []
    for s in range(seqs):
        parts = after(forward[s], low_back[1])
        feedforward = reduce_end(parts, reduce_start(parts))
        outputs.append((valid[s] * (hidden[s] + feedforward)).astype(BF))

    out = attn_bwd(
        after(where[0], ffn_sums[0]), full_back[0], saved[0], wa, wb, cos, sin, None, orders
    )
    parts, sums = [out[:4]], out[4:]
    away = [reduce_start(out[:4])]
    out = attn_bwd(
        after(where[1], away[0]), full_back[1], saved[1], wa, wb, cos, sin, sums, orders
    )
    parts.append(out[:4])
    sums = out[4:]
    away.append(reduce_start(out[:4]))
    input_grads = []
    for s in range(seqs):
        one_back = reduce_end(parts[s], away[s])
        input_grads.append((hidden_back[s] + norm_back(one_back, attn_gain, *first[s])).astype(BF))

    grad_in = scatter_steps(*ffn_sums[:2], orders[0])
    grad_out = scatter_steps(*ffn_sums[2:], orders[1])
    grad_qk = scatter_steps(*sums[:2], orders[0])
    grad_vo = scatter_steps(*sums[2:], orders[1])
    gain_back = jnp.stack([grad_vo[2 * cols], grad_out[units]])
    gain_back = gain_back + exchange(gain_back, "mp", 1)
    gain_back = gain_back + exchange(gain_back, "mp", 2)

    output = from_own(jnp.concatenate(outputs, axis=0)).reshape(seqs, local_len, width)
    input_grad = from_own(jnp.concatenate(input_grads, axis=0)).reshape(seqs, local_len, width)
    grad_qkv = jnp.concatenate([grad_qk, grad_vo[:cols]], axis=0).reshape(3, cols, span)
    return (
        output,
        input_grad,
        gain_back[0] / attn_norm.astype(F32),
        jnp.swapaxes(grad_qkv, 1, 2),
        grad_vo[cols : 2 * cols],
        gain_back[1] / ffn_norm.astype(F32),
        jnp.swapaxes(grad_in.reshape(2, units, span), 1, 2),
        grad_out[:units],
    )


def solution(mesh):
    in_specs = (
        P("dp", "mp", None),
        P("dp"),
        P("dp"),
        P(None, "dp", "mp"),
        P("mp", "dp"),
        P("dp"),
        P(None, "dp", "mp"),
        P("mp", "dp"),
        P("dp", "mp", None),
    )
    out_specs = (
        P("dp", "mp", None),
        P("dp", "mp", None),
        P("dp"),
        P(None, "dp", "mp"),
        P("mp", "dp"),
        P("dp"),
        P(None, "dp", "mp"),
        P("mp", "dp"),
    )
    return jax.shard_map(
        per_device, mesh=mesh, in_specs=in_specs, out_specs=out_specs, check_vma=False
    )
```

```python
import functools

import jax
import jax.numpy as jnp
import numpy as np
from jax import lax
from jax.experimental import pallas as pl
from jax.experimental.pallas import tpu as pltpu
from jax.sharding import PartitionSpec as P

HD = 64
norm_eps = 1e-05
rope_base = 160000.0
SCALE = HD ** (-0.5)
LOG2E = 1.4426950408889634
BF = jnp.bfloat16
F32 = jnp.float32


def exchange(value, axis, bit, name):
    size = lax.axis_size(axis)
    with jax.named_scope(f"{name}_{axis}{bit}"):
        return lax.ppermute(value, axis, [(i, i ^ bit) for i in range(size)])


def bits_of(size):
    assert size & (size - 1) == 0 and size >= 8
    return [1 << i for i in reversed(range(size.bit_length() - 1))]


def rank_order(size):
    order = [0]
    for bit in bits_of(size):
        order = order + [o ^ bit for o in order]
    return order


def gather_order(*low):
    return bits_of(lax.axis_size("dp"))[:-3] + list(low)


def scatter_order(*low):
    return list(low) + bits_of(lax.axis_size("dp"))[:-3][::-1]


def cut(array, parts):
    size = array.shape[-1] // parts
    return [array[..., i * size : (i + 1) * size] for i in range(parts)]


def join(pieces):
    return pieces[0] if len(pieces) == 1 else jnp.concatenate(pieces, axis=-1)


class Move:
    def __init__(self, value, axis, bit, name):
        self.value, self.axis, self.bit, self.name = value, axis, bit, name

    def take(self, got):
        self.got = got


class Gather:
    def __init__(self, shard, order, name):
        self.value, self.order, self.name, self.axis = shard, list(order), name, "dp"
        self.held = []
        while len(self.order) > 3:
            self.take(exchange(self.value, "dp", self.bit, self.name))

    @property
    def bit(self):
        return self.order[0]

    def take(self, got):
        bit = self.order.pop(0)
        outer = 2 ** sum(1 for other in self.held if other < bit)
        self.held.append(bit)
        if self.order:
            pairs = zip(cut(self.value, outer), cut(got, outer))
            self.value = join([piece for pair in pairs for piece in pair])
        else:
            self.outer = outer
            self.halves = (self.value, got)


def halves(total, left):
    outer = 2 ** sum(1 for other in left if other < left[0])
    pieces = cut(total, 2 * outer)
    return join(pieces[0::2]), join(pieces[1::2])


class Scatter:
    def __init__(self, keep, send, order, name):
        self.keep, self.value, self.left, self.name, self.axis = keep, send, list(order), name, "dp"

    @property
    def bit(self):
        return self.left[0]

    def take(self, got):
        self.left.pop(0)
        if self.left:
            pairs = zip(halves(self.keep, self.left), halves(got, self.left))
            self.keep, self.value = ((a.astype(F32) + b.astype(F32)).astype(BF) for a, b in pairs)
        else:
            self.total = self.keep.astype(F32) + got.astype(F32)

    def end(self):
        while self.left:
            self.take(exchange(self.value, "dp", self.bit, self.name))
        return self.total


def stage(moves, work=None, *carry):
    got = [exchange(m.value, m.axis, m.bit, m.name) for m in moves]
    if work is None:
        carry = (idle(carry[0]), *carry[1:])
        done = ()
    else:
        done = work()
    got, done, carry = lax.optimization_barrier((got, tuple(done), carry))
    for m, g in zip(moves, got):
        m.take(g)
    return done, carry


class Rows:
    def __init__(self, both, name):
        self.both, self.name = both, name
        self.beside = Move(both, "mp", 1, name)
        self.across = [Move(both[s], "mp", 2, f"{name}{s}") for s in range(2)]
        self.last = [None, None]

    def diag(self, s):
        self.last[s] = Move(self.across[s].got, "mp", 1, f"{self.name}{s}_diag")
        return self.last[s]

    def parts(self, s):
        return (self.both, s), (self.beside.got, s), (self.across[s].got, None), (self.last[s].got, None)


class SeqRows:
    def __init__(self, own, name):
        self.own, self.name = own, name
        self.beside = Move(own, "mp", 1, name)
        self.across = Move(own, "mp", 2, name)

    def diag(self):
        self.last = Move(self.across.got, "mp", 1, self.name + "_diag")
        return self.last

    def parts(self):
        return tuple((a, None) for a in (self.own, self.beside.got, self.across.got, self.last.got))


class Sums:
    def __init__(self, keep, far, turn, name):
        self.keep, self.far, self.name = keep, far, name
        self.turn = Move(turn, "mp", 1, name + "_turn")

    def away(self):
        total = self.far.astype(F32) + self.turn.got[1].astype(F32)
        self.last = Move(total.astype(BF), "mp", 2, self.name)
        return self.last

    def total(self):
        return self.keep.astype(F32) + self.turn.got[0].astype(F32) + self.last.got.astype(F32)


def nt(a, b):
    return lax.dot_general(a, b, (((1,), (1,)), ((), ())), preferred_element_type=F32)


def nn(a, b):
    return lax.dot_general(a, b, (((1,), (0,)), ((), ())), preferred_element_type=F32)


def tn(a, b):
    return lax.dot_general(a, b, (((0,), (0,)), ((), ())), preferred_element_type=F32)


def aligned(index, step):
    return pl.ds(pl.multiple_of(index * step, step), step)


def picked(refs, picks):
    return [ref if pick is None else ref.at[pick] for ref, pick in zip(refs, picks)]


def start(source, into, sem):
    copy = pltpu.make_async_copy(source, into, sem)
    copy.start()
    return copy


def fetch(parts, place, sem, base=0):
    return [start(part, place(p), sem.at[base + p]) for p, part in enumerate(parts)]


def finish(copies):
    for copy in copies:
        copy.wait()


def await_slot(ref, sem):
    pltpu.make_async_copy(ref, ref, sem).wait()


def fetch_halves(own, got, into, outer, sem, base):
    size = own.shape[-1] // outer
    return [
        start(
            (own, got)[i % 2].at[:, i // 2 * size : (i // 2 + 1) * size],
            into.at[:, i * size : (i + 1) * size],
            sem.at[base + i],
        )
        for i in range(2 * outer)
    ]


def send_block(spot, held_ref, outs, sem, base=0):
    for k, out in enumerate(outs):

        @pl.when(spot == k)
        def _(k=k, out=out):
            start(held_ref.at[k], out, sem.at[base + k])


def sent_blocks(held_ref, outs, sem, base=0):
    finish([pltpu.make_async_copy(held_ref.at[k], out, sem.at[base + k]) for k, out in enumerate(outs)])


def spin(value, cos, sin):
    a, b = value[: HD // 2], value[HD // 2 :]
    return jnp.concatenate([a * cos - b * sin, b * cos + a * sin], axis=0)


def attn_fwd_kernel(
    where_ref, p0, p1, p2, p3, wa0, wa1, wb0, wb1, cos_in, sin_in,
    o0, o2, o13, rows_out, q_out, k_out, v_out, ctx_out, lse_out,
    raw_ref, wa_ref, wb_ref, cos_ref, sin_ref, rows_ref, q_ref, k_ref, v_ref, ctx_ref, lse_ref,
    knat_ref, held_ref, sem, out_sem, *, seq, outer, picks,
):
    me = where_ref[0]
    length = where_ref[1 + seq]
    outs = (o0, o13.at[0], o2, o13.at[1])
    block = rows_ref.shape[1]
    heads = lse_ref.shape[0]
    width = heads * HD
    count = lax.div(length + block - 1, block)
    copies = fetch_halves(wa0, wa1, wa_ref, outer[0], sem, 4)
    copies += fetch((cos_in, sin_in), lambda p: (cos_ref, sin_ref)[p], sem, 12)
    fetch(picked((p0, p1, p2, p3), picks), lambda p: raw_ref.at[me ^ p], sem)
    copies += fetch_halves(wb0, wb1, wb_ref, outer[1], sem, 8)
    finish(copies)

    def project(i, carry):
        await_slot(raw_ref.at[i], sem.at[me ^ i])
        raw = raw_ref[i].astype(F32)
        raw = raw - jnp.mean(raw, axis=-1, keepdims=True)
        scale = lax.rsqrt(jnp.mean(raw * raw, axis=-1, keepdims=True) + norm_eps)
        rows = (raw * scale * wa_ref[2 * width : 2 * width + 1].astype(F32)).astype(BF)
        rows_ref[i] = rows
        start(rows_ref.at[i], rows_out.at[i], out_sem.at[4 + i])
        spot = aligned(i, block)
        cos = cos_ref[:, spot]
        sin = sin_ref[:, spot]
        query = nt(wa_ref[:width], rows)
        key = nt(wa_ref[width : 2 * width], rows)
        for h in range(heads):
            hs = slice(h * HD, (h + 1) * HD)
            q_ref[hs, spot] = spin(query[hs], cos, sin).astype(BF)
            turned = spin(key[hs], cos, sin)
            k_ref[hs, spot] = turned.astype(BF)
            knat_ref[h, spot, :] = turned.T.astype(BF)
        v_ref[:, spot] = nt(wb_ref[:width], rows).astype(BF)
        return carry

    lax.fori_loop(0, count, project, 0)
    saves = [(q_ref, q_out), (k_ref, k_out), (v_ref, v_out)]
    saves = [start(ref, out, out_sem.at[8 + i]) for i, (ref, out) in enumerate(saves)]

    for n in range(1, 5):

        @pl.when(count == n)
        def _(n=n):
            last = lax.broadcasted_iota(jnp.int32, (block, block), 0) + (n - 1) * block < length

            def rows_of(i, carry):
                spot = aligned(i, block)
                for h in range(heads):
                    hs = slice(h * HD, (h + 1) * HD)
                    query = q_ref[hs, spot]
                    tiles = []
                    for j in range(n):
                        tile = nn(knat_ref[h, j * block : (j + 1) * block, :], query) * (SCALE * LOG2E)
                        if j == n - 1:
                            tile = jnp.where(last, tile, -1e30)
                        tiles.append(tile)
                    top = jnp.max(functools.reduce(jnp.maximum, tiles), axis=0, keepdims=True)
                    total = jnp.zeros((1, block), F32)
                    found = jnp.zeros((HD, block), F32)
                    for j, tile in enumerate(tiles):
                        weight = jnp.exp2(tile - top)
                        total = total + jnp.sum(weight, axis=0, keepdims=True)
                        found = found + nn(v_ref[hs, j * block : (j + 1) * block], weight.astype(BF))
                    ctx_ref[hs, spot] = (found / total).astype(BF)
                    lse_ref[h, :, spot] = top + jnp.log2(total)
                out = me ^ i
                held_ref[out] = nn(ctx_ref[:, spot].T, wb_ref[width:]).astype(BF)
                send_block(out, held_ref, outs, out_sem)
                return carry

            lax.fori_loop(0, n, rows_of, 0)

    saves += [start(ref, out, out_sem.at[11 + i]) for i, (ref, out) in enumerate([(ctx_ref, ctx_out), (lse_ref, lse_out)])]

    def blank(i, carry):
        await_slot(raw_ref.at[i], sem.at[me ^ i])
        out = me ^ i
        held_ref[out] = jnp.zeros(held_ref.shape[1:], BF)
        send_block(out, held_ref, outs, out_sem)
        rows_ref[i] = held_ref[out]
        start(rows_ref.at[i], rows_out.at[i], out_sem.at[4 + i])
        return carry

    lax.fori_loop(count, 4, blank, 0)
    finish(saves)
    sent_blocks(rows_ref, [rows_out.at[i] for i in range(4)], out_sem, 4)
    sent_blocks(held_ref, outs, out_sem)


def put_halves(keep_ref, send_ref, rows, value, outer):
    size = value.shape[-1] // (2 * outer)
    for i in range(outer):
        at = slice(i * size, (i + 1) * size)
        keep_ref[rows, at] = value[:, 2 * i * size : (2 * i + 1) * size].astype(BF)
        send_ref[rows, at] = value[:, (2 * i + 1) * size : (2 * i + 2) * size].astype(BF)


def attn_bwd_kernel(
    where_ref, p0, p1, p2, p3, wa0, wa1, wb0, wb1, rows_in, q_in, k_in, v_in, ctx_in, lse_in,
    cos_in, sin_in, *rest, seq, old, outer, outer_w,
):
    if old:
        old_in, oldgain_ref, *rest = rest
    (o0, o2, o13), rest = rest[:3], rest[3:]
    outs = (o0, o13.at[0], o2, o13.at[1])
    if old:
        g_outs, gain_ref, g_refs, rest = rest[:4], rest[4], rest[5:9], rest[9:]
    else:
        grad_out, gain_ref, *rest = rest
    (
        grad_ref, wa_ref, wb_ref, rows_ref, q_ref, k_ref, v_ref, ctx_ref, lse_ref, cos_ref, sin_ref,
        back_ref, cb_ref, knat_ref, vnat_ref, d_ref, dk_ref, dv_ref, delta_ref, held_ref, sem, out_sem,
    ) = rest
    me = where_ref[0]
    length = where_ref[1 + seq]
    block = rows_ref.shape[1]
    heads = lse_ref.shape[0]
    width = heads * HD
    count = lax.div(length + block - 1, block)
    early = fetch_halves(wb0, wb1, wb_ref, outer_w[1], sem, 8)
    fetch((p0, p1, p2, p3), lambda p: back_ref.at[me ^ p], sem)
    saved = (ctx_in, k_in, v_in, q_in, lse_in, cos_in, sin_in)
    places = (ctx_ref, k_ref, v_ref, q_ref, lse_ref, cos_ref, sin_ref)
    early += fetch(saved, lambda p: places[p], sem, 12)
    late = fetch((rows_in,), lambda p: rows_ref, sem, 19)
    late += fetch_halves(wa0, wa1, wa_ref, outer_w[0], sem, 4)
    if old:
        late += fetch((old_in,), lambda p: grad_ref, sem, 20)
        gain_ref[...] = oldgain_ref[...]
    else:
        gain_ref[...] = jnp.zeros(gain_ref.shape, F32)
    dk_ref[...] = jnp.zeros(dk_ref.shape, F32)
    dv_ref[...] = jnp.zeros(dv_ref.shape, F32)
    finish(early)

    def prepare(i, carry):
        await_slot(back_ref.at[i], sem.at[me ^ i])
        spot = aligned(i, block)
        low = nt(wb_ref[width:], back_ref[i]).astype(BF)
        cb_ref[:, spot] = low
        inner = low.astype(F32) * ctx_ref[:, spot].astype(F32)
        for h in range(heads):
            hs = slice(h * HD, (h + 1) * HD)
            delta_ref[h, :, spot] = jnp.sum(inner[hs], axis=0, keepdims=True)
            knat_ref[h, spot, :] = k_ref[hs, spot].T
            vnat_ref[h, spot, :] = v_ref[hs, spot].T
        return carry

    lax.fori_loop(0, count, prepare, 0)

    def unspin(value, spot):
        return spin(value * SCALE, cos_ref[:, spot], -sin_ref[:, spot]).astype(BF)

    for n in range(1, 5):

        @pl.when(count == n)
        def _(n=n):
            last = lax.broadcasted_iota(jnp.int32, (block, block), 0) + (n - 1) * block < length

            def rows_of(i, carry):
                spot = aligned(i, block)
                for h in range(heads):
                    hs = slice(h * HD, (h + 1) * HD)
                    query = q_ref[hs, spot]
                    cb = cb_ref[hs, spot]
                    lse = lse_ref[h, :, spot]
                    delta = delta_ref[h, :, spot]
                    dq = jnp.zeros((HD, block), F32)
                    for j in range(n):
                        js = slice(j * block, (j + 1) * block)
                        tile = nn(knat_ref[h, js, :], query) * (SCALE * LOG2E) - lse
                        if j == n - 1:
                            tile = jnp.where(last, tile, -1e30)
                        weight = jnp.exp2(tile)
                        back = nn(vnat_ref[h, js, :], cb)
                        ds = (weight * (back - delta)).astype(BF)
                        dv_ref[hs, js] += nt(cb, weight.astype(BF))
                        dk_ref[hs, js] += nt(query, ds)
                        dq = dq + nn(k_ref[hs, js], ds)
                    d_ref[hs, spot] = unspin(dq, spot)
                return carry

            lax.fori_loop(0, n, rows_of, 0)
            for i in range(n):
                spot = slice(i * block, (i + 1) * block)
                for h in range(heads):
                    hs = slice(h * HD, (h + 1) * HD)
                    d_ref[width + h * HD : width + (h + 1) * HD, spot] = unspin(dk_ref[hs, spot], spot)
                d_ref[2 * width :, spot] = dv_ref[:, spot].astype(BF)
            finish(late)
            full = slice(0, n * block)
            rows = rows_ref[:n].reshape(n * block, -1)
            back = back_ref[:n].reshape(n * block, -1)
            pieces = [(k, d_ref[k * width : (k + 1) * width, full], rows) for k in range(3)]
            pieces.append((3, ctx_ref[:, full], back))
            for k, left, right in pieces:
                at = slice(k * width, (k + 1) * width)
                value = nn(left, right)
                if old:
                    pair = g_refs[k // 2 * 2 : k // 2 * 2 + 2]
                    put_halves(*pair, slice(k % 2 * width, (k % 2 + 1) * width), grad_ref[at] + value, outer[k // 2])
                else:
                    grad_ref[at] = value

    if old:
        saves = [start(ref, out, out_sem.at[4 + i]) for i, (ref, out) in enumerate(zip(g_refs, g_outs))]
    else:
        saves = [start(grad_ref, grad_out, out_sem.at[4])]

    def close(i, carry):
        turned = d_ref[:, aligned(i, block)].T
        out = nn(turned[:, : 2 * width], wa_ref[: 2 * width]) + nn(turned[:, 2 * width :], wb_ref[:width])
        held_ref[me ^ i] = out.astype(BF)
        send_block(me ^ i, held_ref, outs, out_sem)
        gain_ref[:1] += jnp.sum(out * rows_ref[i].astype(F32), axis=0, keepdims=True)
        return carry

    lax.fori_loop(0, count, close, 0)

    def blank(i, carry):
        await_slot(back_ref.at[i], sem.at[me ^ i])
        held_ref[me ^ i] = jnp.zeros(held_ref.shape[1:], BF)
        send_block(me ^ i, held_ref, outs, out_sem)
        return carry

    lax.fori_loop(count, 4, blank, 0)
    finish(saves)
    sent_blocks(held_ref, outs, out_sem)


def ffn_kernel(
    where_ref, a0, a1, a2, a3, b0, b1, b2, b3, wu0, wu1, wg0, wg1, wo0, wo1,
    f0, f2, f13, n0, n2, n13, ub_out, gb_out, mixed_out, gain_ref,
    rows_ref, back_ref, fheld_ref, nheld_ref, ub_ref, gb_ref, mixed_ref, wu_ref, wg_ref, wo_ref, sem, out_sem,
    *, seq, outer, picks,
):
    me = where_ref[0]
    length = where_ref[1 + seq]
    block = rows_ref.shape[1]
    fouts = (f0, f13.at[0], f2, f13.at[1])
    nouts = (n0, n13.at[0], n2, n13.at[1])
    copies = fetch_halves(wu0, wu1, wu_ref, outer[0], sem, 8)
    aparts, bparts = picked((a0, a1, a2, a3), picks[:4]), picked((b0, b1, b2, b3), picks[4:])
    start(aparts[0], rows_ref.at[0], sem.at[0])
    copies += fetch_halves(wg0, wg1, wg_ref, outer[1], sem, 12)
    start(bparts[0], back_ref.at[0], sem.at[4])
    copies += fetch_halves(wo0, wo1, wo_ref, outer[2], sem, 16)
    for p in range(1, 4):
        start(aparts[p], rows_ref.at[p], sem.at[p])
        start(bparts[p], back_ref.at[p], sem.at[4 + p])
    gain_ref[...] = jnp.zeros(gain_ref.shape, F32)
    finish(copies)
    kept = ((ub_ref, ub_out), (gb_ref, gb_out), (mixed_ref, mixed_out))

    def step(p, carry):
        valid = (me ^ p) * block < length
        await_slot(rows_ref.at[p], sem.at[p])
        await_slot(back_ref.at[p], sem.at[4 + p])

        @pl.when(valid)
        def _():
            rows = rows_ref[p]
            up = nt(rows, wu_ref[...])
            gate = nt(rows, wg_ref[...])
            mb = nt(back_ref[p], wo_ref[...])
            phi = 0.5 + 0.5 * lax.erf(up * (0.5**0.5))
            act = up * phi
            mixed = (act * gate).astype(BF)
            mixed_ref[p] = mixed
            slope = phi + up * (jnp.exp(-0.5 * up * up) * (0.5 / np.pi) ** 0.5)
            ub = (mb * gate * slope).astype(BF)
            gb = (mb * act).astype(BF)
            ub_ref[p] = ub
            gb_ref[p] = gb
            out = nn(ub, wu_ref[...]) + nn(gb, wg_ref[...])
            nheld_ref[p] = out.astype(BF)
            gain_ref[:1] += jnp.sum(out * rows.astype(F32), axis=0, keepdims=True)
            fheld_ref[p] = nn(mixed, wo_ref[...]).astype(BF)

        @pl.when(jnp.logical_not(valid))
        def _():
            for ref in (mixed_ref, ub_ref, gb_ref, nheld_ref, fheld_ref):
                ref[p] = jnp.zeros(ref.shape[1:], BF)

        send_block(p, nheld_ref, nouts, out_sem, 4)
        send_block(p, fheld_ref, fouts, out_sem)
        for k, (ref, out) in enumerate(kept):
            start(ref.at[p], out.at[p], out_sem.at[8 + 4 * k + p])
        return carry

    lax.fori_loop(0, 4, step, 0)
    sent_blocks(nheld_ref, nouts, out_sem, 4)
    sent_blocks(fheld_ref, fouts, out_sem)
    for k, (ref, out) in enumerate(kept):
        sent_blocks(ref, [out.at[p] for p in range(4)], out_sem, 8 + 4 * k)


def ffn_grad_kernel(_, *refs, outer, picks):
    parts, saved, refs = picked(refs[:16], picks), refs[16:22], refs[22:]
    outs, (rows_ref, back_ref, saved_ref, *held), refs = refs[:4], refs[4:11], refs[11:]
    g_ref, sem, out_sem = refs
    units = g_ref.shape[1]
    copies = []
    for s in range(2):
        rows = fetch(parts[8 * s : 8 * s + 4], lambda p: rows_ref.at[s, p], sem, 8 * s)
        backs = lambda: fetch(parts[8 * s + 4 : 8 * s + 8], lambda p: back_ref.at[s, p], sem, 8 * s + 4)
        kept = lambda k: fetch((saved[3 * s + k],), lambda p: saved_ref.at[s, k], sem, 16 + 3 * s + k)
        copies += [rows + kept(0), kept(1), kept(2) + backs()]
    sent = []
    for s in range(2):
        rows = rows_ref.at[s]
        for k in range(3):
            finish(copies[3 * s + k])
            other = (back_ref if k == 2 else rows_ref)[s].reshape(-1, rows_ref.shape[-1])
            part = tn(saved_ref[s, k].reshape(-1, units), other)
            if s == 0:
                g_ref[k] = part
                continue
            pair = held[k // 2 * 2 : k // 2 * 2 + 2]
            at = slice(None) if k == 2 else slice(k * units, (k + 1) * units)
            put_halves(*pair, at, g_ref[k] + part, outer[k // 2])
            if k > 0:
                sent += [start(ref, out, out_sem.at[k // 2 * 2 + i]) for i, (ref, out) in enumerate(zip(pair, outs[k // 2 * 2 :][:2]))]
    finish(sent)


SMEM = pl.BlockSpec(memory_space=pltpu.SMEM)
VMEM = pl.BlockSpec(memory_space=pltpu.VMEM)
HBM = pl.BlockSpec(memory_space=pltpu.HBM)
LIMIT = 60 * 1024 * 1024
PARAMS = pltpu.CompilerParams(vmem_limit_bytes=LIMIT)
GAIN_ROWS = 8


def shape(*dims, kind=BF):
    return jax.ShapeDtypeStruct(dims, kind)


def first_outer(order):
    return 2 ** sum(1 for other in order if other < order[0])


def idle_kernel(in_ref, out_ref):
    for i in range(in_ref.shape[0]):
        out_ref[i] = in_ref[i]


def idle(where):
    return pl.pallas_call(
        idle_kernel,
        out_shape=jax.ShapeDtypeStruct(where.shape, where.dtype),
        in_specs=[SMEM],
        out_specs=SMEM,
        cost_estimate=pl.CostEstimate(flops=1 << 34, bytes_accessed=1 << 20, transcendentals=0),
        name="idle",
    )(where)


def partials(block, width):
    return (shape(block, width), shape(block, width), shape(2, block, width))


def vmem(array):
    return pltpu.VMEM(array.shape, array.dtype)


def attn_fwd(where, seq, parts, wa, wb, cos, sin):
    arrays, picks = zip(*parts)
    block, width = arrays[0].shape[-2:]
    rows = wb.halves[0].shape[0]
    cols = rows // 2
    heads = cols // HD
    full = 4 * block
    flops = 2 * full * width * cols * 4 + 4 * full * full * cols
    saved = (shape(4, block, width),) + (shape(cols, full),) * 4 + (shape(heads, 1, full, kind=F32),)
    return pl.pallas_call(
        functools.partial(attn_fwd_kernel, seq=seq, outer=(wa.outer, wb.outer), picks=picks),
        out_shape=partials(block, width) + saved,
        in_specs=[SMEM] + [HBM] * 10,
        out_specs=(HBM,) * 9,
        scratch_shapes=[
            pltpu.VMEM((4, block, width), BF),
            pltpu.VMEM(wa.halves[0].shape[:1] + (width,), BF),
            pltpu.VMEM((rows, width), BF),
            vmem(cos),
            vmem(sin),
            *[vmem(array) for array in saved],
            pltpu.VMEM((heads, full, HD), BF),
            pltpu.VMEM((4, block, width), BF),
            pltpu.SemaphoreType.DMA((14,)),
            pltpu.SemaphoreType.DMA((13,)),
        ],
        compiler_params=PARAMS,
        cost_estimate=pl.CostEstimate(flops=flops * 3, bytes_accessed=12 << 20, transcendentals=heads * full * full),
        name="attn_fwd",
    )(where, *arrays, *wa.halves, *wb.halves, cos, sin)


def attn_bwd(where, seq, parts, saved, wa, wb, cos, sin, old, orders):
    arrays = [array for array, _ in parts]
    block, width = arrays[0].shape
    rows = wb.halves[0].shape[0]
    cols = rows // 2
    heads = cols // HD
    full = 4 * block
    flops = 4 * full * width * cols * 4 + 10 * full * full * cols
    extra = [] if old is None else list(old)
    grads = shape(4 * cols, width, kind=F32)
    gain = shape(GAIN_ROWS, width, kind=F32)
    halved = (shape(rows, width // 2),) * 4
    outs = (grads,) if old is None else halved
    return pl.pallas_call(
        functools.partial(
            attn_bwd_kernel,
            seq=seq,
            old=old is not None,
            outer=[first_outer(o) for o in orders],
            outer_w=(wa.outer, wb.outer),
        ),
        out_shape=partials(block, width) + outs + (gain,),
        in_specs=[SMEM] + [HBM] * 16 + ([] if old is None else [HBM, VMEM]),
        out_specs=(HBM,) * (3 + len(outs)) + (VMEM,),
        scratch_shapes=[vmem(array) for array in (() if old is None else halved) + (grads,)] + [
            pltpu.VMEM(wa.halves[0].shape[:1] + (width,), BF),
            pltpu.VMEM((rows, width), BF),
            *[vmem(array) for array in saved],
            vmem(cos),
            vmem(sin),
            pltpu.VMEM((4, block, width), BF),
            pltpu.VMEM((cols, full), BF),
            pltpu.VMEM((heads, full, HD), BF),
            pltpu.VMEM((heads, full, HD), BF),
            pltpu.VMEM((3 * cols, full), BF),
            pltpu.VMEM((cols, full), F32),
            pltpu.VMEM((cols, full), F32),
            pltpu.VMEM((heads, 1, full), F32),
            pltpu.VMEM((4, block, width), BF),
            pltpu.SemaphoreType.DMA((21,)),
            pltpu.SemaphoreType.DMA((8,)),
        ],
        compiler_params=PARAMS,
        cost_estimate=pl.CostEstimate(flops=flops * 3, bytes_accessed=16 << 20, transcendentals=heads * full * full),
        name="attn_bwd",
    )(where, *arrays, *wa.halves, *wb.halves, *saved, cos, sin, *extra)


def ffn(where, seq, parts, backs, weights):
    arrays, picks = zip(*parts, *backs)
    block, width = arrays[0].shape[-2:]
    units = weights[0].halves[0].shape[0]
    flops = 2 * 4 * block * width * units * 6
    saved = (shape(4, block, units),) * 3
    return pl.pallas_call(
        functools.partial(ffn_kernel, seq=seq, outer=[w.outer for w in weights], picks=picks),
        out_shape=partials(block, width) * 2 + saved + (shape(GAIN_ROWS, width, kind=F32),),
        in_specs=[SMEM] + [HBM] * 14,
        out_specs=(HBM,) * 9 + (VMEM,),
        scratch_shapes=[pltpu.VMEM((4, block, width), BF)] * 4
        + [vmem(array) for array in saved]
        + [pltpu.VMEM((units, width), BF)] * 3
        + [pltpu.SemaphoreType.DMA((20,)), pltpu.SemaphoreType.DMA((20,))],
        compiler_params=PARAMS,
        cost_estimate=pl.CostEstimate(flops=flops, bytes_accessed=20 << 20, transcendentals=2 * 4 * block * units),
        name="ffn",
    )(where, *arrays, *[half for w in weights for half in w.halves])


def ffn_grad(where, parts, saved, orders):
    arrays, picks = zip(*parts)
    block, width = arrays[0].shape[-2:]
    units = saved[0].shape[2]
    outs = (shape(2 * units, width // 2),) * 2 + (shape(units, width // 2),) * 2
    return pl.pallas_call(
        functools.partial(ffn_grad_kernel, outer=[first_outer(o) for o in orders], picks=picks),
        out_shape=outs,
        in_specs=[SMEM] + [HBM] * 22,
        out_specs=(HBM,) * 4,
        scratch_shapes=[pltpu.VMEM((2, 4, block, width), BF)] * 2
        + [pltpu.VMEM((2, 3) + saved[0].shape, BF)]
        + [vmem(array) for array in outs]
        + [pltpu.VMEM((3, units, width), F32), pltpu.SemaphoreType.DMA((22,)), pltpu.SemaphoreType.DMA((4,))],
        compiler_params=PARAMS,
        cost_estimate=pl.CostEstimate(flops=2 * 8 * block * width * units * 3, bytes_accessed=24 << 20, transcendentals=0),
        name="ffn_grad",
    )(where, *arrays, *saved)


def norm_parts(values):
    average = jnp.mean(values, axis=-1, keepdims=True)
    centred = values - average
    spread = jnp.mean(centred * centred, axis=-1, keepdims=True)
    scale = lax.rsqrt(spread + norm_eps)
    return centred * scale, scale


def norm_back(grad, gain, normed, scale):
    y = grad * gain
    return scale * (
        y - jnp.mean(y, axis=-1, keepdims=True) - normed * jnp.mean(y * normed, axis=-1, keepdims=True)
    )


def rope_tables(length):
    places = np.arange(length, dtype=np.float32)
    frequency = (rope_base ** (-np.arange(0, HD, 2, dtype=np.float32) / HD)).astype(np.float32)
    angles = (frequency[:, None] * places[None, :]).astype(np.float32)
    return jnp.asarray(np.cos(angles)), jnp.asarray(np.sin(angles))


def per_device(
    tokens, lengths, attn_norm, qkv_weight, attn_out_weight, ffn_norm, ffn_in_weight, ffn_out_weight, out_grad
):
    seqs, local_len, width = tokens.shape
    assert lax.axis_size("mp") == 4 and seqs == 2
    groups = lax.axis_size("dp")
    me = lax.axis_index("mp")
    full_len = 4 * local_len
    cols = qkv_weight.shape[2]
    units = ffn_in_weight.shape[2]
    span = width // groups
    cos, sin = rope_tables(full_len)

    ranks = rank_order(groups)
    order = jnp.asarray(np.array(ranks, np.int32)) ^ lax.axis_index("dp")
    source = (order[:, None] * span + jnp.arange(span, dtype=jnp.int32)[None, :]).reshape(width)
    reorder = (source[None, :] == jnp.arange(width, dtype=jnp.int32)[:, None]).astype(BF)

    def to_own(rows):
        return jnp.dot(rows.reshape(-1, width), reorder, preferred_element_type=F32).astype(BF).reshape(rows.shape)

    def from_own(rows):
        return lax.dot_general(
            rows, reorder, (((1,), (1,)), ((), ())), preferred_element_type=F32
        ).astype(BF)

    far, near = gather_order(4, 2, 1), gather_order(1, 4, 2)
    qkv = jnp.swapaxes(qkv_weight, 1, 2)
    ffn_in = jnp.swapaxes(ffn_in_weight, 1, 2)
    own_gains = jnp.stack([attn_norm, ffn_norm])
    own_gains = jnp.pad(own_gains, ((0, 14), (0, 0)))
    wa = Gather(jnp.concatenate([qkv[:2].reshape(2 * cols, span), own_gains], axis=0), far, "w_qk")
    wb = Gather(jnp.concatenate([qkv[2], attn_out_weight], axis=0), near, "w_vo")
    w_up = Gather(ffn_in[0], far, "w_up")
    w_gate = Gather(ffn_in[1], far, "w_gate")
    w_out = Gather(ffn_out_weight, near, "w_out")

    local = me * local_len + jnp.arange(local_len, dtype=jnp.int32)
    where = jnp.concatenate([me[None], lengths]).astype(jnp.int32)
    valid = [(local < lengths[s]).astype(F32)[:, None] for s in range(seqs)]
    token_low = to_own(tokens)
    token = Rows(token_low, "token")

    _, (where, token.across[1].value, out_grad) = stage(
        [token.across[0], token.beside, wa, wb, w_out], None, where, token.across[1].value, out_grad
    )

    def prepare():
        rows = to_own(out_grad)
        low = [(valid[s] * rows[s].astype(F32)).astype(BF) for s in range(seqs)]
        return (jnp.stack(low),)

    (back_low, where), (w_up.value, token_low) = stage(
        [token.across[1], wb, wa, token.diag(0)], lambda: prepare() + (idle(where),), w_up.value, token_low
    )
    outback = Rows(back_low, "outback")
    _, (where, w_gate.value, w_out.value) = stage(
        [outback.across[0], wa, wb, token.diag(1), w_up], None, where, w_gate.value, w_out.value
    )
    ffn_gain = join([half[2 * cols + 1 : 2 * cols + 2] for half in wa.halves]).astype(F32)
    attn_gain = join([half[2 * cols : 2 * cols + 1] for half in wa.halves]).astype(F32)

    done, (where,) = stage(
        [outback.across[1], outback.beside, w_up, w_gate],
        lambda: attn_fwd(where, 0, token.parts(0), wa, wb, cos, sin),
        where,
    )
    attn = [Sums(*done[:3], "attn0")]
    saved = [done[3:]]
    stage_turn = lambda sums, *others: stage([sums.turn, *others], lambda: (), where)
    _, (where,) = stage_turn(attn[0], outback.diag(0))
    done, (where,) = stage(
        [attn[0].away(), w_up, w_gate, w_out, outback.diag(1)],
        lambda: attn_fwd(where, 1, token.parts(1), wa, wb, cos, sin),
        where,
    )
    attn.append(Sums(*done[:3], "attn1"))
    saved.append(done[3:])

    def second_norm(s):
        rows = token_low[s].astype(F32) + attn[s].total()
        normed, scale = norm_parts(rows)
        return rows, normed, scale, (normed * ffn_gain).astype(BF)

    hidden, second, two = [None, None], [None, None], [None, None]

    (done,), (where,) = stage([attn[1].turn], lambda: (second_norm(0),), where)
    hidden[0], second[0] = done[0], done[1:3]
    two[0] = SeqRows(done[3], "two0")
    _, (where,) = stage([two[0].across, attn[1].away(), w_out, w_gate, two[0].beside], None, where)
    (done,), (where,) = stage([two[0].diag()], lambda: (second_norm(1),), where)
    hidden[1], second[1] = done[0], done[1:3]
    two[1] = SeqRows(done[3], "two1")
    weights = (w_up, w_gate, w_out)
    done, (where,) = stage(
        [two[1].across, two[1].beside],
        lambda: ffn(where, 0, two[0].parts(), outback.parts(0), weights),
        where,
    )
    ff, twoback = [Sums(*done[:3], "ff0")], [Sums(*done[3:6], "twoback0")]
    ffn_saved, ffn_gains = list(done[6:9]), done[9]
    _, (where,) = stage_turn(twoback[0], two[1].diag())
    done, (where,) = stage(
        [twoback[0].away(), ff[0].turn],
        lambda: ffn(where, 1, two[1].parts(), outback.parts(1), weights),
        where,
    )
    ff.append(Sums(*done[:3], "ff1"))
    twoback.append(Sums(*done[3:6], "twoback1"))
    ffn_saved += done[6:9]
    ffn_gains = ffn_gains + done[9]

    def second_back(s):
        rows = back_low[s].astype(F32) + norm_back(twoback[s].total(), ffn_gain, *second[s])
        return rows, rows.astype(BF)

    hidden_back, hidback = [None, None], [None, None]
    (done,), (where,) = stage([twoback[1].turn], lambda: (second_back(0),), where)
    hidden_back[0] = done[0]
    hidback[0] = SeqRows(done[1], "hidback0")
    orders = (scatter_order(1, 4, 2), scatter_order(2, 1, 4))
    done, (where,) = stage(
        [twoback[1].away(), hidback[0].across, hidback[0].beside, ff[1].turn],
        lambda: ffn_grad(
            where, [p for s in range(seqs) for p in two[s].parts() + outback.parts(s)], ffn_saved, orders
        ),
        where,
    )
    g_in = Scatter(*done[:2], orders[0], "g_in")
    g_out = Scatter(*done[2:], orders[1], "g_out")
    (done,), (where,) = stage([hidback[0].diag()], lambda: (second_back(1),), where)
    hidden_back[1] = done[0]
    hidback[1] = SeqRows(done[1], "hidback1")

    orders = (scatter_order(1, 2, 4), scatter_order(2, 4, 1))
    done, (where,) = stage(
        [hidback[1].across, ff[0].away(), g_in, g_out, hidback[1].beside],
        lambda: attn_bwd(where, 0, hidback[0].parts(), saved[0], wa, wb, cos, sin, None, orders),
        where,
    )
    oneback = [Sums(*done[:3], "oneback0")]
    sums = done[3:]
    _, (where,) = stage_turn(oneback[0], hidback[1].diag())
    done, (where, token_low) = stage(
        [oneback[0].away(), ff[1].away(), g_in, g_out],
        lambda: attn_bwd(where, 1, hidback[1].parts(), saved[1], wa, wb, cos, sin, sums, orders),
        where, token_low,
    )
    oneback.append(Sums(*done[:3], "oneback1"))
    g_qk = Scatter(*done[3:5], orders[0], "g_qk")
    g_vo = Scatter(*done[5:7], orders[1], "g_vo")
    gain_sums = jnp.stack([done[7][0], ffn_gains[0]])
    gain_moves = [Move(gain_sums, "mp", k, "gain_sum") for k in (1, 2, 3)]

    def close(s):
        parts = norm_parts(token_low[s].astype(F32))
        return (hidden_back[s] + norm_back(oneback[s].total(), attn_gain, *parts)).astype(BF)

    def ready():
        rows = [(valid[s] * (hidden[s] + ff[s].total())).astype(BF) for s in range(seqs)]
        return from_own(jnp.concatenate(rows, axis=0)), close(0)

    (output, input_grad), (where,) = stage([g_qk, g_vo, oneback[1].turn, *gain_moves], ready, where)
    ones, twos, threes = (m.got for m in gain_moves)
    gain_sums = (gain_sums + ones) + (twos + threes)
    gain = Scatter(*halves(gain_sums, scatter_order(1, 2, 4)), scatter_order(1, 2, 4), "gain")
    _, (where,) = stage([oneback[1].away(), g_qk, g_vo, g_out, gain], None, where)
    stage([g_qk, g_vo, g_in, gain], None, where)
    gain_back = gain.end()
    input_grad = from_own(jnp.concatenate([input_grad, close(1)], axis=0))
    grad_qk, grad_vo = g_qk.end(), g_vo.end()
    grad_qkv = jnp.concatenate([grad_qk, grad_vo[:cols]], axis=0).reshape(3, cols, span)
    return (
        output.reshape(seqs, local_len, width),
        input_grad.reshape(seqs, local_len, width),
        gain_back[0] / attn_norm.astype(F32),
        jnp.swapaxes(grad_qkv, 1, 2),
        grad_vo[cols:],
        gain_back[1] / ffn_norm.astype(F32),
        jnp.swapaxes(g_in.end().reshape(2, units, span), 1, 2),
        g_out.end(),
    )


def solution(mesh):
    in_specs = (
        P("dp", "mp", None),
        P("dp"),
        P("dp"),
        P(None, "dp", "mp"),
        P("mp", "dp"),
        P("dp"),
        P(None, "dp", "mp"),
        P("mp", "dp"),
        P("dp", "mp", None),
    )
    out_specs = (
        P("dp", "mp", None),
        P("dp", "mp", None),
        P("dp"),
        P(None, "dp", "mp"),
        P("mp", "dp"),
        P("dp"),
        P(None, "dp", "mp"),
        P("mp", "dp"),
    )
    return jax.shard_map(
        per_device, mesh=mesh, in_specs=in_specs, out_specs=out_specs, check_vma=False
    )
```

```python
import functools

import jax
import jax.numpy as jnp
import numpy as np
from jax import lax
from jax.experimental import pallas as pl
from jax.experimental.pallas import tpu as pltpu
from jax.sharding import PartitionSpec as P

HD = 64
norm_eps = 1e-05
rope_base = 160000.0
SCALE = HD ** (-0.5)
LOG2E = 1.4426950408889634
BF = jnp.bfloat16
F32 = jnp.float32


def exchange(value, axis, bit, name):
    size = lax.axis_size(axis)
    with jax.named_scope(f"{name}_{axis}{bit}"):
        return lax.ppermute(value, axis, [(i, i ^ bit) for i in range(size)])


def bits_of(size):
    assert size & (size - 1) == 0 and size >= 8
    return [1 << i for i in reversed(range(size.bit_length() - 1))]


def rank_order(size):
    order = [0]
    for bit in bits_of(size):
        order = order + [o ^ bit for o in order]
    return order


def gather_order(*low):
    return bits_of(lax.axis_size("dp"))[:-3] + list(low)


def scatter_order(*low):
    return list(low) + bits_of(lax.axis_size("dp"))[:-3][::-1]


def cut(array, parts):
    size = array.shape[-1] // parts
    return [array[..., i * size : (i + 1) * size] for i in range(parts)]


def join(pieces):
    return pieces[0] if len(pieces) == 1 else jnp.concatenate(pieces, axis=-1)


class Move:
    def __init__(self, value, axis, bit, name):
        self.value, self.axis, self.bit, self.name = value, axis, bit, name

    def take(self, got):
        self.got = got


class Gather:
    def __init__(self, shard, order, name):
        self.value, self.order, self.name, self.axis = shard, list(order), name, "dp"
        self.held = []
        while len(self.order) > 3:
            self.take(exchange(self.value, "dp", self.bit, self.name))

    @property
    def bit(self):
        return self.order[0]

    def take(self, got):
        bit = self.order.pop(0)
        outer = 2 ** sum(1 for other in self.held if other < bit)
        self.held.append(bit)
        if self.order:
            pairs = zip(cut(self.value, outer), cut(got, outer))
            self.value = join([piece for pair in pairs for piece in pair])
        else:
            self.outer = outer
            self.halves = (self.value, got)


def halves(total, left):
    outer = 2 ** sum(1 for other in left if other < left[0])
    pieces = cut(total, 2 * outer)
    return join(pieces[0::2]), join(pieces[1::2])


class Scatter:
    def __init__(self, keep, send, order, name):
        self.keep, self.value, self.left, self.name, self.axis = keep, send, list(order), name, "dp"

    @property
    def bit(self):
        return self.left[0]

    def take(self, got):
        self.left.pop(0)
        if self.left:
            pairs = zip(halves(self.keep, self.left), halves(got, self.left))
            self.keep, self.value = ((a.astype(F32) + b.astype(F32)).astype(BF) for a, b in pairs)
        else:
            self.total = self.keep.astype(F32) + got.astype(F32)

    def end(self):
        while self.left:
            self.take(exchange(self.value, "dp", self.bit, self.name))
        return self.total


def stage(moves, work=None, *carry):
    got = [exchange(m.value, m.axis, m.bit, m.name) for m in moves]
    if work is None:
        carry = (idle(carry[0]), *carry[1:])
        done = ()
    else:
        done = work()
    got, done, carry = lax.optimization_barrier((got, tuple(done), carry))
    for m, g in zip(moves, got):
        m.take(g)
    return done, carry


class SeqRows:
    def __init__(self, own, name):
        self.own, self.name = own, name
        self.beside = Move(own, "mp", 1, name)
        self.across = Move(own, "mp", 2, name)

    def diag(self):
        self.last = Move(self.across.got, "mp", 1, self.name + "_diag")
        return self.last

    def parts(self):
        return tuple((a, None) for a in (self.own, self.beside.got, self.across.got, self.last.got))


class Sums:
    def __init__(self, keep, far, turn, name):
        self.keep, self.far, self.name = keep, far, name
        self.turn = Move(turn, "mp", 1, name + "_turn")

    def away(self):
        total = self.far.astype(F32) + self.turn.got[1].astype(F32)
        self.last = Move(total.astype(BF), "mp", 2, self.name)
        return self.last

    def total(self):
        return self.keep.astype(F32) + self.turn.got[0].astype(F32) + self.last.got.astype(F32)


def nt(a, b):
    return lax.dot_general(a, b, (((1,), (1,)), ((), ())), preferred_element_type=F32)


def nn(a, b):
    return lax.dot_general(a, b, (((1,), (0,)), ((), ())), preferred_element_type=F32)


def tn(a, b):
    return lax.dot_general(a, b, (((0,), (0,)), ((), ())), preferred_element_type=F32)


def aligned(index, step):
    return pl.ds(pl.multiple_of(index * step, step), step)


def picked(refs, picks):
    return [ref if pick is None else ref.at[pick] for ref, pick in zip(refs, picks)]


def start(source, into, sem):
    copy = pltpu.make_async_copy(source, into, sem)
    copy.start()
    return copy


def fetch(parts, place, sem, base=0):
    return [start(part, place(p), sem.at[base + p]) for p, part in enumerate(parts)]


def finish(copies):
    for copy in copies:
        copy.wait()


def await_slot(ref, sem):
    pltpu.make_async_copy(ref, ref, sem).wait()


def fetch_halves(own, got, into, outer, sem, base):
    size = own.shape[-1] // outer
    return [
        start(
            (own, got)[i % 2].at[:, i // 2 * size : (i // 2 + 1) * size],
            into.at[:, i * size : (i + 1) * size],
            sem.at[base + i],
        )
        for i in range(2 * outer)
    ]


def send_block(spot, held_ref, outs, sem, base=0):
    for k, out in enumerate(outs):

        @pl.when(spot == k)
        def _(k=k, out=out):
            start(held_ref.at[k], out, sem.at[base + k])


def sent_blocks(held_ref, outs, sem, base=0):
    finish([pltpu.make_async_copy(held_ref.at[k], out, sem.at[base + k]) for k, out in enumerate(outs)])


def spin(value, cos, sin):
    a, b = value[: HD // 2], value[HD // 2 :]
    return jnp.concatenate([a * cos - b * sin, b * cos + a * sin], axis=0)


def attn_fwd_kernel(
    where_ref, p0, p1, p2, p3, wa0, wa1, wb0, wb1, cos_in, sin_in,
    o0, o2, o13, rows_out, q_out, k_out, v_out, ctx_out, lse_out,
    raw_ref, wa_ref, wb_ref, cos_ref, sin_ref, rows_ref, q_ref, k_ref, v_ref, ctx_ref, lse_ref,
    knat_ref, held_ref, sem, out_sem, *, seq, outer, picks,
):
    me = where_ref[0]
    length = where_ref[1 + seq]
    outs = (o0, o13.at[0], o2, o13.at[1])
    block = rows_ref.shape[1]
    heads = lse_ref.shape[0]
    width = heads * HD
    count = lax.div(length + block - 1, block)
    copies = fetch_halves(wa0, wa1, wa_ref, outer[0], sem, 4)
    copies += fetch((cos_in, sin_in), lambda p: (cos_ref, sin_ref)[p], sem, 12)
    fetch(picked((p0, p1, p2, p3), picks), lambda p: raw_ref.at[me ^ p], sem)
    copies += fetch_halves(wb0, wb1, wb_ref, outer[1], sem, 8)
    finish(copies)

    def project(i, carry):
        await_slot(raw_ref.at[i], sem.at[me ^ i])
        raw = raw_ref[i].astype(F32)
        raw = raw - jnp.mean(raw, axis=-1, keepdims=True)
        scale = lax.rsqrt(jnp.mean(raw * raw, axis=-1, keepdims=True) + norm_eps)
        rows = (raw * scale * wa_ref[2 * width : 2 * width + 1].astype(F32)).astype(BF)
        rows_ref[i] = rows
        start(rows_ref.at[i], rows_out.at[i], out_sem.at[4 + i])
        spot = aligned(i, block)
        cos = cos_ref[:, spot]
        sin = sin_ref[:, spot]
        query = nt(wa_ref[:width], rows)
        key = nt(wa_ref[width : 2 * width], rows)
        for h in range(heads):
            hs = slice(h * HD, (h + 1) * HD)
            q_ref[hs, spot] = spin(query[hs], cos, sin).astype(BF)
            turned = spin(key[hs], cos, sin)
            k_ref[hs, spot] = turned.astype(BF)
            knat_ref[h, spot, :] = turned.T.astype(BF)
        v_ref[:, spot] = nt(wb_ref[:width], rows).astype(BF)
        return carry

    lax.fori_loop(0, count, project, 0)
    saves = [(q_ref, q_out), (k_ref, k_out), (v_ref, v_out)]
    saves = [start(ref, out, out_sem.at[8 + i]) for i, (ref, out) in enumerate(saves)]

    for n in range(1, 5):

        @pl.when(count == n)
        def _(n=n):
            last = lax.broadcasted_iota(jnp.int32, (block, block), 0) + (n - 1) * block < length

            def rows_of(i, carry):
                spot = aligned(i, block)
                for h in range(heads):
                    hs = slice(h * HD, (h + 1) * HD)
                    query = q_ref[hs, spot]
                    tiles = []
                    for j in range(n):
                        tile = nn(knat_ref[h, j * block : (j + 1) * block, :], query) * (SCALE * LOG2E)
                        if j == n - 1:
                            tile = jnp.where(last, tile, -1e30)
                        tiles.append(tile)
                    top = jnp.max(functools.reduce(jnp.maximum, tiles), axis=0, keepdims=True)
                    total = jnp.zeros((1, block), F32)
                    found = jnp.zeros((HD, block), F32)
                    for j, tile in enumerate(tiles):
                        weight = jnp.exp2(tile - top)
                        total = total + jnp.sum(weight, axis=0, keepdims=True)
                        found = found + nn(v_ref[hs, j * block : (j + 1) * block], weight.astype(BF))
                    ctx_ref[hs, spot] = (found / total).astype(BF)
                    lse_ref[h, :, spot] = top + jnp.log2(total)
                out = me ^ i
                held_ref[out] = nn(ctx_ref[:, spot].T, wb_ref[width:]).astype(BF)
                send_block(out, held_ref, outs, out_sem)
                return carry

            lax.fori_loop(0, n, rows_of, 0)

    saves += [start(ref, out, out_sem.at[11 + i]) for i, (ref, out) in enumerate([(ctx_ref, ctx_out), (lse_ref, lse_out)])]

    def blank(i, carry):
        await_slot(raw_ref.at[i], sem.at[me ^ i])
        out = me ^ i
        held_ref[out] = jnp.zeros(held_ref.shape[1:], BF)
        send_block(out, held_ref, outs, out_sem)
        rows_ref[i] = held_ref[out]
        start(rows_ref.at[i], rows_out.at[i], out_sem.at[4 + i])
        return carry

    lax.fori_loop(count, 4, blank, 0)
    finish(saves)
    sent_blocks(rows_ref, [rows_out.at[i] for i in range(4)], out_sem, 4)
    sent_blocks(held_ref, outs, out_sem)


def put_halves(keep_ref, send_ref, rows, value, outer):
    size = value.shape[-1] // (2 * outer)
    for i in range(outer):
        at = slice(i * size, (i + 1) * size)
        keep_ref[rows, at] = value[:, 2 * i * size : (2 * i + 1) * size].astype(BF)
        send_ref[rows, at] = value[:, (2 * i + 1) * size : (2 * i + 2) * size].astype(BF)


def attn_bwd_kernel(
    where_ref, p0, p1, p2, p3, wa0, wa1, wb0, wb1, rows_in, q_in, k_in, v_in, ctx_in, lse_in,
    cos_in, sin_in, *rest, seq, old, outer, outer_w,
):
    if old:
        old_in, oldgain_ref, *rest = rest
    (o0, o2, o13), rest = rest[:3], rest[3:]
    outs = (o0, o13.at[0], o2, o13.at[1])
    if old:
        g_outs, gain_ref, g_refs, rest = rest[:4], rest[4], rest[5:9], rest[9:]
    else:
        grad_out, gain_ref, *rest = rest
    (
        grad_ref, wa_ref, wb_ref, rows_ref, q_ref, k_ref, v_ref, ctx_ref, lse_ref, cos_ref, sin_ref,
        back_ref, cb_ref, knat_ref, vnat_ref, d_ref, dk_ref, dv_ref, delta_ref, held_ref, sem, out_sem,
    ) = rest
    me = where_ref[0]
    length = where_ref[1 + seq]
    block = rows_ref.shape[1]
    heads = lse_ref.shape[0]
    width = heads * HD
    count = lax.div(length + block - 1, block)
    early = fetch_halves(wb0, wb1, wb_ref, outer_w[1], sem, 8)
    fetch((p0, p1, p2, p3), lambda p: back_ref.at[me ^ p], sem)
    saved = (ctx_in, k_in, v_in, q_in, lse_in, cos_in, sin_in)
    places = (ctx_ref, k_ref, v_ref, q_ref, lse_ref, cos_ref, sin_ref)
    early += fetch(saved, lambda p: places[p], sem, 12)
    late = fetch((rows_in,), lambda p: rows_ref, sem, 19)
    late += fetch_halves(wa0, wa1, wa_ref, outer_w[0], sem, 4)
    if old:
        late += fetch((old_in,), lambda p: grad_ref, sem, 20)
        gain_ref[...] = oldgain_ref[...]
    else:
        gain_ref[...] = jnp.zeros(gain_ref.shape, F32)
    dk_ref[...] = jnp.zeros(dk_ref.shape, F32)
    dv_ref[...] = jnp.zeros(dv_ref.shape, F32)
    finish(early)

    def prepare(i, carry):
        await_slot(back_ref.at[i], sem.at[me ^ i])
        spot = aligned(i, block)
        low = nt(wb_ref[width:], back_ref[i]).astype(BF)
        cb_ref[:, spot] = low
        inner = low.astype(F32) * ctx_ref[:, spot].astype(F32)
        for h in range(heads):
            hs = slice(h * HD, (h + 1) * HD)
            delta_ref[h, :, spot] = jnp.sum(inner[hs], axis=0, keepdims=True)
            knat_ref[h, spot, :] = k_ref[hs, spot].T
            vnat_ref[h, spot, :] = v_ref[hs, spot].T
        return carry

    lax.fori_loop(0, count, prepare, 0)

    def unspin(value, spot):
        return spin(value * SCALE, cos_ref[:, spot], -sin_ref[:, spot]).astype(BF)

    for n in range(1, 5):

        @pl.when(count == n)
        def _(n=n):
            last = lax.broadcasted_iota(jnp.int32, (block, block), 0) + (n - 1) * block < length

            def rows_of(i, carry):
                spot = aligned(i, block)
                for h in range(heads):
                    hs = slice(h * HD, (h + 1) * HD)
                    query = q_ref[hs, spot]
                    cb = cb_ref[hs, spot]
                    lse = lse_ref[h, :, spot]
                    delta = delta_ref[h, :, spot]
                    dq = jnp.zeros((HD, block), F32)
                    for j in range(n):
                        js = slice(j * block, (j + 1) * block)
                        tile = nn(knat_ref[h, js, :], query) * (SCALE * LOG2E) - lse
                        if j == n - 1:
                            tile = jnp.where(last, tile, -1e30)
                        weight = jnp.exp2(tile)
                        back = nn(vnat_ref[h, js, :], cb)
                        ds = (weight * (back - delta)).astype(BF)
                        dv_ref[hs, js] += nt(cb, weight.astype(BF))
                        dk_ref[hs, js] += nt(query, ds)
                        dq = dq + nn(k_ref[hs, js], ds)
                    d_ref[hs, spot] = unspin(dq, spot)
                return carry

            lax.fori_loop(0, n, rows_of, 0)
            for i in range(n):
                spot = slice(i * block, (i + 1) * block)
                for h in range(heads):
                    hs = slice(h * HD, (h + 1) * HD)
                    d_ref[width + h * HD : width + (h + 1) * HD, spot] = unspin(dk_ref[hs, spot], spot)
                d_ref[2 * width :, spot] = dv_ref[:, spot].astype(BF)
            finish(late)
            full = slice(0, n * block)
            rows = rows_ref[:n].reshape(n * block, -1)
            back = back_ref[:n].reshape(n * block, -1)
            pieces = [(k, d_ref[k * width : (k + 1) * width, full], rows) for k in range(3)]
            pieces.append((3, ctx_ref[:, full], back))
            for k, left, right in pieces:
                at = slice(k * width, (k + 1) * width)
                value = nn(left, right)
                if old:
                    pair = g_refs[k // 2 * 2 : k // 2 * 2 + 2]
                    put_halves(*pair, slice(k % 2 * width, (k % 2 + 1) * width), grad_ref[at] + value, outer[k // 2])
                else:
                    grad_ref[at] = value

    if old:
        saves = [start(ref, out, out_sem.at[4 + i]) for i, (ref, out) in enumerate(zip(g_refs, g_outs))]
    else:
        saves = [start(grad_ref, grad_out, out_sem.at[4])]

    def close(i, carry):
        turned = d_ref[:, aligned(i, block)].T
        out = nn(turned[:, : 2 * width], wa_ref[: 2 * width]) + nn(turned[:, 2 * width :], wb_ref[:width])
        held_ref[me ^ i] = out.astype(BF)
        send_block(me ^ i, held_ref, outs, out_sem)
        gain_ref[:1] += jnp.sum(out * rows_ref[i].astype(F32), axis=0, keepdims=True)
        return carry

    lax.fori_loop(0, count, close, 0)

    def blank(i, carry):
        await_slot(back_ref.at[i], sem.at[me ^ i])
        held_ref[me ^ i] = jnp.zeros(held_ref.shape[1:], BF)
        send_block(me ^ i, held_ref, outs, out_sem)
        return carry

    lax.fori_loop(count, 4, blank, 0)
    finish(saves)
    sent_blocks(held_ref, outs, out_sem)


def ffn_kernel(
    where_ref, a0, a1, a2, a3, b0, b1, b2, b3, wu0, wu1, wg0, wg1, wo0, wo1,
    f0, f2, f13, n0, n2, n13, ub_out, gb_out, mixed_out, gain_ref,
    rows_ref, back_ref, fheld_ref, nheld_ref, ub_ref, gb_ref, mixed_ref, wu_ref, wg_ref, wo_ref, sem, out_sem,
    *, seq, outer, picks,
):
    me = where_ref[0]
    length = where_ref[1 + seq]
    block = rows_ref.shape[1]
    fouts = (f0, f13.at[0], f2, f13.at[1])
    nouts = (n0, n13.at[0], n2, n13.at[1])
    copies = fetch_halves(wu0, wu1, wu_ref, outer[0], sem, 8)
    aparts, bparts = picked((a0, a1, a2, a3), picks[:4]), picked((b0, b1, b2, b3), picks[4:])
    start(aparts[0], rows_ref.at[0], sem.at[0])
    copies += fetch_halves(wg0, wg1, wg_ref, outer[1], sem, 12)
    start(bparts[0], back_ref.at[0], sem.at[4])
    copies += fetch_halves(wo0, wo1, wo_ref, outer[2], sem, 16)
    for p in range(1, 4):
        start(aparts[p], rows_ref.at[p], sem.at[p])
        start(bparts[p], back_ref.at[p], sem.at[4 + p])
    gain_ref[...] = jnp.zeros(gain_ref.shape, F32)
    finish(copies)
    kept = ((ub_ref, ub_out), (gb_ref, gb_out), (mixed_ref, mixed_out))

    def step(p, carry):
        valid = (me ^ p) * block < length
        await_slot(rows_ref.at[p], sem.at[p])
        await_slot(back_ref.at[p], sem.at[4 + p])

        @pl.when(valid)
        def _():
            rows = rows_ref[p]
            up = nt(rows, wu_ref[...])
            gate = nt(rows, wg_ref[...])
            mb = nt(back_ref[p], wo_ref[...])
            phi = 0.5 + 0.5 * lax.erf(up * (0.5**0.5))
            act = up * phi
            mixed = (act * gate).astype(BF)
            mixed_ref[p] = mixed
            slope = phi + up * (jnp.exp(-0.5 * up * up) * (0.5 / np.pi) ** 0.5)
            ub = (mb * gate * slope).astype(BF)
            gb = (mb * act).astype(BF)
            ub_ref[p] = ub
            gb_ref[p] = gb
            out = nn(ub, wu_ref[...]) + nn(gb, wg_ref[...])
            nheld_ref[p] = out.astype(BF)
            gain_ref[:1] += jnp.sum(out * rows.astype(F32), axis=0, keepdims=True)
            fheld_ref[p] = nn(mixed, wo_ref[...]).astype(BF)

        @pl.when(jnp.logical_not(valid))
        def _():
            for ref in (mixed_ref, ub_ref, gb_ref, nheld_ref, fheld_ref):
                ref[p] = jnp.zeros(ref.shape[1:], BF)

        send_block(p, nheld_ref, nouts, out_sem, 4)
        send_block(p, fheld_ref, fouts, out_sem)
        for k, (ref, out) in enumerate(kept):
            start(ref.at[p], out.at[p], out_sem.at[8 + 4 * k + p])
        return carry

    lax.fori_loop(0, 4, step, 0)
    sent_blocks(nheld_ref, nouts, out_sem, 4)
    sent_blocks(fheld_ref, fouts, out_sem)
    for k, (ref, out) in enumerate(kept):
        sent_blocks(ref, [out.at[p] for p in range(4)], out_sem, 8 + 4 * k)


def ffn_grad_kernel(_, *refs, outer, picks):
    parts, saved, refs = picked(refs[:16], picks), refs[16:22], refs[22:]
    outs, (rows_ref, back_ref, saved_ref, *held), refs = refs[:4], refs[4:11], refs[11:]
    g_ref, sem, out_sem = refs
    units = g_ref.shape[1]
    copies = []
    for s in range(2):
        rows = fetch(parts[8 * s : 8 * s + 4], lambda p: rows_ref.at[s, p], sem, 8 * s)
        backs = lambda: fetch(parts[8 * s + 4 : 8 * s + 8], lambda p: back_ref.at[s, p], sem, 8 * s + 4)
        kept = lambda k: fetch((saved[3 * s + k],), lambda p: saved_ref.at[s, k], sem, 16 + 3 * s + k)
        copies += [rows + kept(0), kept(1), kept(2) + backs()]
    sent = []
    for s in range(2):
        rows = rows_ref.at[s]
        for k in range(3):
            finish(copies[3 * s + k])
            other = (back_ref if k == 2 else rows_ref)[s].reshape(-1, rows_ref.shape[-1])
            part = tn(saved_ref[s, k].reshape(-1, units), other)
            if s == 0:
                g_ref[k] = part
                continue
            pair = held[k // 2 * 2 : k // 2 * 2 + 2]
            at = slice(None) if k == 2 else slice(k * units, (k + 1) * units)
            put_halves(*pair, at, g_ref[k] + part, outer[k // 2])
            if k > 0:
                sent += [start(ref, out, out_sem.at[k // 2 * 2 + i]) for i, (ref, out) in enumerate(zip(pair, outs[k // 2 * 2 :][:2]))]
    finish(sent)


SMEM = pl.BlockSpec(memory_space=pltpu.SMEM)
VMEM = pl.BlockSpec(memory_space=pltpu.VMEM)
HBM = pl.BlockSpec(memory_space=pl.ANY)
LIMIT = 60 * 1024 * 1024
PARAMS = pltpu.CompilerParams(vmem_limit_bytes=LIMIT)
GAIN_ROWS = 8


def shape(*dims, kind=BF):
    return jax.ShapeDtypeStruct(dims, kind)


def first_outer(order):
    return 2 ** sum(1 for other in order if other < order[0])


def idle(where):
    return pl.pallas_call(
        lambda in_ref, out_ref: None,
        out_shape=jax.ShapeDtypeStruct(where.shape, where.dtype),
        in_specs=[pl.BlockSpec(memory_space=pl.ANY)],
        out_specs=pl.BlockSpec(memory_space=pl.ANY),
        input_output_aliases={0: 0},
        cost_estimate=pl.CostEstimate(flops=1 << 34, bytes_accessed=1 << 20, transcendentals=0),
        name="idle",
    )(where)


def partials(block, width):
    return (shape(block, width), shape(block, width), shape(2, block, width))


def vmem(array):
    return pltpu.VMEM(array.shape, array.dtype)


def attn_fwd(where, seq, parts, wa, wb, cos, sin):
    arrays, picks = zip(*parts)
    block, width = arrays[0].shape[-2:]
    rows = wb.halves[0].shape[0]
    cols = rows // 2
    heads = cols // HD
    full = 4 * block
    flops = 2 * full * width * cols * 4 + 4 * full * full * cols
    saved = (shape(4, block, width),) + (shape(cols, full),) * 4 + (shape(heads, 1, full, kind=F32),)
    return pl.pallas_call(
        functools.partial(attn_fwd_kernel, seq=seq, outer=(wa.outer, wb.outer), picks=picks),
        out_shape=partials(block, width) + saved,
        in_specs=[SMEM] + [HBM] * 10,
        out_specs=(HBM,) * 9,
        scratch_shapes=[
            pltpu.VMEM((4, block, width), BF),
            pltpu.VMEM(wa.halves[0].shape[:1] + (width,), BF),
            pltpu.VMEM((rows, width), BF),
            vmem(cos),
            vmem(sin),
            *[vmem(array) for array in saved],
            pltpu.VMEM((heads, full, HD), BF),
            pltpu.VMEM((4, block, width), BF),
            pltpu.SemaphoreType.DMA((14,)),
            pltpu.SemaphoreType.DMA((13,)),
        ],
        compiler_params=pltpu.CompilerParams(vmem_limit_bytes=58 << 20),
        cost_estimate=pl.CostEstimate(flops=flops * 3, bytes_accessed=12 << 20, transcendentals=heads * full * full),
        name="attn_fwd",
    )(where, *arrays, *wa.halves, *wb.halves, cos, sin)


def attn_bwd(where, seq, parts, saved, wa, wb, cos, sin, old, orders):
    arrays = [array for array, _ in parts]
    block, width = arrays[0].shape
    rows = wb.halves[0].shape[0]
    cols = rows // 2
    heads = cols // HD
    full = 4 * block
    flops = 4 * full * width * cols * 4 + 10 * full * full * cols
    extra = [] if old is None else list(old)
    grads = shape(4 * cols, width, kind=F32)
    gain = shape(GAIN_ROWS, width, kind=F32)
    halved = (shape(rows, width // 2),) * 4
    outs = (grads,) if old is None else halved
    return pl.pallas_call(
        functools.partial(
            attn_bwd_kernel,
            seq=seq,
            old=old is not None,
            outer=[first_outer(o) for o in orders],
            outer_w=(wa.outer, wb.outer),
        ),
        out_shape=partials(block, width) + outs + (gain,),
        in_specs=[SMEM] + [HBM] * 16 + ([] if old is None else [HBM, VMEM]),
        out_specs=(HBM,) * (3 + len(outs)) + (VMEM,),
        scratch_shapes=[vmem(array) for array in (() if old is None else halved) + (grads,)] + [
            pltpu.VMEM(wa.halves[0].shape[:1] + (width,), BF),
            pltpu.VMEM((rows, width), BF),
            *[vmem(array) for array in saved],
            vmem(cos),
            vmem(sin),
            pltpu.VMEM((4, block, width), BF),
            pltpu.VMEM((cols, full), BF),
            pltpu.VMEM((heads, full, HD), BF),
            pltpu.VMEM((heads, full, HD), BF),
            pltpu.VMEM((3 * cols, full), BF),
            pltpu.VMEM((cols, full), F32),
            pltpu.VMEM((cols, full), F32),
            pltpu.VMEM((heads, 1, full), F32),
            pltpu.VMEM((4, block, width), BF),
            pltpu.SemaphoreType.DMA((21,)),
            pltpu.SemaphoreType.DMA((8,)),
        ],
        compiler_params=pltpu.CompilerParams(vmem_limit_bytes=32 << 20),
        cost_estimate=pl.CostEstimate(flops=flops * 3, bytes_accessed=16 << 20, transcendentals=heads * full * full),
        name="attn_bwd",
    )(where, *arrays, *wa.halves, *wb.halves, *saved, cos, sin, *extra)


def ffn(where, seq, parts, backs, weights):
    arrays, picks = zip(*parts, *backs)
    block, width = arrays[0].shape[-2:]
    units = weights[0].halves[0].shape[0]
    flops = 2 * 4 * block * width * units * 6
    saved = (shape(4, block, units),) * 3
    return pl.pallas_call(
        functools.partial(ffn_kernel, seq=seq, outer=[w.outer for w in weights], picks=picks),
        out_shape=partials(block, width) * 2 + saved + (shape(GAIN_ROWS, width, kind=F32),),
        in_specs=[SMEM] + [HBM] * 14,
        out_specs=(HBM,) * 9 + (VMEM,),
        scratch_shapes=[pltpu.VMEM((4, block, width), BF)] * 4
        + [vmem(array) for array in saved]
        + [pltpu.VMEM((units, width), BF)] * 3
        + [pltpu.SemaphoreType.DMA((20,)), pltpu.SemaphoreType.DMA((20,))],
        compiler_params=pltpu.CompilerParams(vmem_limit_bytes=58 << 20),
        cost_estimate=pl.CostEstimate(flops=flops, bytes_accessed=20 << 20, transcendentals=2 * 4 * block * units),
        name="ffn",
    )(where, *arrays, *[half for w in weights for half in w.halves])


def ffn_grad(where, parts, saved, orders):
    arrays, picks = zip(*parts)
    block, width = arrays[0].shape[-2:]
    units = saved[0].shape[2]
    outs = (shape(2 * units, width // 2),) * 2 + (shape(units, width // 2),) * 2
    return pl.pallas_call(
        functools.partial(ffn_grad_kernel, outer=[first_outer(o) for o in orders], picks=picks),
        out_shape=outs,
        in_specs=[SMEM] + [HBM] * 22,
        out_specs=(HBM,) * 4,
        scratch_shapes=[pltpu.VMEM((2, 4, block, width), BF)] * 2
        + [pltpu.VMEM((2, 3) + saved[0].shape, BF)]
        + [vmem(array) for array in outs]
        + [pltpu.VMEM((3, units, width), F32), pltpu.SemaphoreType.DMA((22,)), pltpu.SemaphoreType.DMA((4,))],
        compiler_params=pltpu.CompilerParams(vmem_limit_bytes=40 << 20),
        cost_estimate=pl.CostEstimate(flops=2 * 8 * block * width * units * 3, bytes_accessed=24 << 20, transcendentals=0),
        name="ffn_grad",
    )(where, *arrays, *saved)


def norm_parts(values):
    average = jnp.mean(values, axis=-1, keepdims=True)
    centred = values - average
    spread = jnp.mean(centred * centred, axis=-1, keepdims=True)
    scale = lax.rsqrt(spread + norm_eps)
    return centred * scale, scale


def norm_back(grad, gain, normed, scale):
    y = grad * gain
    return scale * (
        y - jnp.mean(y, axis=-1, keepdims=True) - normed * jnp.mean(y * normed, axis=-1, keepdims=True)
    )


def rope_tables(length):
    places = np.arange(length, dtype=np.float32)
    frequency = (rope_base ** (-np.arange(0, HD, 2, dtype=np.float32) / HD)).astype(np.float32)
    angles = (frequency[:, None] * places[None, :]).astype(np.float32)
    return jnp.asarray(np.cos(angles)), jnp.asarray(np.sin(angles))


def per_device(
    tokens, lengths, attn_norm, qkv_weight, attn_out_weight, ffn_norm, ffn_in_weight, ffn_out_weight, out_grad
):
    seqs, local_len, width = tokens.shape
    assert lax.axis_size("mp") == 4 and seqs == 2
    groups = lax.axis_size("dp")
    me = lax.axis_index("mp")
    full_len = 4 * local_len
    cols = qkv_weight.shape[2]
    units = ffn_in_weight.shape[2]
    span = width // groups
    cos, sin = rope_tables(full_len)

    ranks = rank_order(groups)
    order = jnp.asarray(np.array(ranks, np.int32)) ^ lax.axis_index("dp")
    source = (order[:, None] * span + jnp.arange(span, dtype=jnp.int32)[None, :]).reshape(width)
    reorder = (source[None, :] == jnp.arange(width, dtype=jnp.int32)[:, None]).astype(BF)

    def to_own(rows):
        return jnp.dot(rows.reshape(-1, width), reorder, preferred_element_type=F32).astype(BF).reshape(rows.shape)

    def from_own(rows):
        return lax.dot_general(
            rows, reorder, (((1,), (1,)), ((), ())), preferred_element_type=F32
        ).astype(BF)

    far, near = gather_order(4, 2, 1), gather_order(1, 4, 2)
    qkv = jnp.swapaxes(qkv_weight, 1, 2)
    ffn_in = jnp.swapaxes(ffn_in_weight, 1, 2)
    own_gains = jnp.stack([attn_norm, ffn_norm])
    own_gains = jnp.pad(own_gains, ((0, 14), (0, 0)))
    wa = Gather(jnp.concatenate([qkv[:2].reshape(2 * cols, span), own_gains], axis=0), far, "w_qk")
    wb = Gather(jnp.concatenate([qkv[2], attn_out_weight], axis=0), near, "w_vo")
    w_up = Gather(ffn_in[0], far, "w_up")
    w_gate = Gather(ffn_in[1], far, "w_gate")
    w_out = Gather(ffn_out_weight, near, "w_out")

    local = me * local_len + jnp.arange(local_len, dtype=jnp.int32)
    where = jnp.concatenate([me[None], lengths]).astype(jnp.int32)
    valid = [(local < lengths[s]).astype(F32)[:, None] for s in range(seqs)]
    token_low = [to_own(tokens[s]) for s in range(seqs)]
    token = [SeqRows(token_low[s], f"token{s}") for s in range(seqs)]

    _, (where, token[1].across.value, out_grad, w_out.value) = stage(
        [token[0].across, token[0].beside, wa, wb, w_up],
        None,
        where, token[1].across.value, out_grad, w_out.value,
    )

    def prepare():
        return *[(valid[s] * to_own(out_grad[s]).astype(F32)).astype(BF) for s in range(seqs)], idle(where)

    (*back_low, where), (token_low,) = stage(
        [token[1].across, wb, wa, w_out, token[0].diag()], prepare, token_low
    )
    outback = [SeqRows(back_low[s], f"outback{s}") for s in range(seqs)]
    _, (where, w_gate.value) = stage(
        [outback[0].across, wa, wb, token[1].beside, token[1].diag()], None, where, w_gate.value
    )
    ffn_gain = join([half[2 * cols + 1 : 2 * cols + 2] for half in wa.halves]).astype(F32)
    attn_gain = join([half[2 * cols : 2 * cols + 1] for half in wa.halves]).astype(F32)

    done, (where,) = stage(
        [outback[1].across, w_up, w_gate, outback[0].beside, outback[1].beside],
        lambda: attn_fwd(where, 0, token[0].parts(), wa, wb, cos, sin),
        where,
    )
    attn = [Sums(*done[:3], "attn0")]
    saved = [done[3:]]
    stage_turn = lambda sums, *others: stage([sums.turn, *others], lambda: (), where)
    _, (where,) = stage_turn(attn[0], outback[0].diag())
    done, (where,) = stage(
        [attn[0].away(), w_up, w_gate, w_out, outback[1].diag()],
        lambda: attn_fwd(where, 1, token[1].parts(), wa, wb, cos, sin),
        where,
    )
    attn.append(Sums(*done[:3], "attn1"))
    saved.append(done[3:])

    def second_norm(s):
        rows = token_low[s].astype(F32) + attn[s].total()
        normed, scale = norm_parts(rows)
        return rows, normed, scale, (normed * ffn_gain).astype(BF)

    hidden, second, two = [None, None], [None, None], [None, None]

    (done,), (where,) = stage([attn[1].turn], lambda: (second_norm(0),), where)
    hidden[0], second[0] = done[0], done[1:3]
    two[0] = SeqRows(done[3], "two0")
    _, (where,) = stage([two[0].across, attn[1].away(), w_out, w_gate, two[0].beside], None, where)
    (done,), (where,) = stage([two[0].diag()], lambda: (second_norm(1),), where)
    hidden[1], second[1] = done[0], done[1:3]
    two[1] = SeqRows(done[3], "two1")
    weights = (w_up, w_gate, w_out)
    done, (where,) = stage(
        [two[1].across, two[1].beside],
        lambda: ffn(where, 0, two[0].parts(), outback[0].parts(), weights),
        where,
    )
    ff, twoback = [Sums(*done[:3], "ff0")], [Sums(*done[3:6], "twoback0")]
    ffn_saved, ffn_gains = list(done[6:9]), done[9]
    _, (where,) = stage_turn(twoback[0], two[1].diag())
    done, (where,) = stage(
        [twoback[0].away(), ff[0].turn],
        lambda: ffn(where, 1, two[1].parts(), outback[1].parts(), weights),
        where,
    )
    ff.append(Sums(*done[:3], "ff1"))
    twoback.append(Sums(*done[3:6], "twoback1"))
    ffn_saved += done[6:9]
    ffn_gains = ffn_gains + done[9]

    def second_back(s):
        rows = back_low[s].astype(F32) + norm_back(twoback[s].total(), ffn_gain, *second[s])
        return rows, rows.astype(BF)

    hidden_back, hidback = [None, None], [None, None]
    (done,), (where,) = stage([twoback[1].turn], lambda: (second_back(0),), where)
    hidden_back[0] = done[0]
    hidback[0] = SeqRows(done[1], "hidback0")
    orders = (scatter_order(1, 4, 2), scatter_order(2, 1, 4))

    def weight_grads():
        grads = ffn_grad(
            where, [p for s in range(seqs) for p in two[s].parts() + outback[s].parts()], ffn_saved, orders
        )
        return grads

    done, (where,) = stage(
        [twoback[1].away(), hidback[0].across, hidback[0].beside, ff[1].turn], weight_grads, where
    )
    g_in = Scatter(*done[:2], orders[0], "g_in")
    g_out = Scatter(*done[2:], orders[1], "g_out")
    (done,), (where,) = stage([hidback[0].diag()], lambda: (second_back(1),), where)
    hidden_back[1] = done[0]
    hidback[1] = SeqRows(done[1], "hidback1")

    orders = (scatter_order(1, 2, 4), scatter_order(2, 4, 1))
    done, (where,) = stage(
        [hidback[1].across, ff[0].away(), g_in, g_out, hidback[1].beside],
        lambda: attn_bwd(where, 0, hidback[0].parts(), saved[0], wa, wb, cos, sin, None, orders),
        where,
    )
    oneback = [Sums(*done[:3], "oneback0")]
    sums = done[3:]
    _, (where,) = stage_turn(oneback[0], hidback[1].diag())
    done, (where, token_low) = stage(
        [oneback[0].away(), ff[1].away(), g_in, g_out],
        lambda: attn_bwd(where, 1, hidback[1].parts(), saved[1], wa, wb, cos, sin, sums, orders),
        where, token_low,
    )
    oneback.append(Sums(*done[:3], "oneback1"))
    g_qk = Scatter(*done[3:5], orders[0], "g_qk")
    g_vo = Scatter(*done[5:7], orders[1], "g_vo")
    gain_sums = jnp.stack([done[7][0], ffn_gains[0]])
    gain_moves = [Move(gain_sums, "mp", k, "gain_sum") for k in (1, 2, 3)]

    def close(s):
        return (hidden_back[s] + norm_back(oneback[s].total(), attn_gain, *norm_parts(token_low[s].astype(F32)))).astype(BF)

    def ready():
        rows = [(valid[s] * (hidden[s] + ff[s].total())).astype(BF) for s in range(seqs)]
        return from_own(jnp.concatenate(rows, axis=0)), close(0)

    (output, input_grad), (where,) = stage([g_qk, g_vo, oneback[1].turn, *gain_moves], ready, where)
    ones, twos, threes = (m.got for m in gain_moves)
    gain_sums = (gain_sums + ones) + (twos + threes)
    gain = Scatter(*halves(gain_sums, scatter_order(1, 2, 4)), scatter_order(1, 2, 4), "gain")
    _, (where,) = stage([oneback[1].away(), g_qk, g_vo, g_out, gain], None, where)
    stage([g_qk, g_vo, g_in, gain], None, where)
    gain_back = gain.end()
    input_grad = from_own(jnp.concatenate([input_grad, close(1)], axis=0))
    grad_qk, grad_vo = g_qk.end(), g_vo.end()
    grad_qkv = jnp.concatenate([grad_qk, grad_vo[:cols]], axis=0).reshape(3, cols, span)
    return (
        output.reshape(seqs, local_len, width),
        input_grad.reshape(seqs, local_len, width),
        gain_back[0] / attn_norm.astype(F32),
        jnp.swapaxes(grad_qkv, 1, 2),
        grad_vo[cols:],
        gain_back[1] / ffn_norm.astype(F32),
        jnp.swapaxes(g_in.end().reshape(2, units, span), 1, 2),
        g_out.end(),
    )


def solution(mesh):
    in_specs = (
        P("dp", "mp", None),
        P("dp"),
        P("dp"),
        P(None, "dp", "mp"),
        P("mp", "dp"),
        P("dp"),
        P(None, "dp", "mp"),
        P("mp", "dp"),
        P("dp", "mp", None),
    )
    out_specs = (
        P("dp", "mp", None),
        P("dp", "mp", None),
        P("dp"),
        P(None, "dp", "mp"),
        P("mp", "dp"),
        P("dp"),
        P(None, "dp", "mp"),
        P("mp", "dp"),
    )
    return jax.shard_map(
        per_device, mesh=mesh, in_specs=in_specs, out_specs=out_specs, check_vma=False
    )
```

```python
import functools

import jax
import jax.numpy as jnp
import numpy as np
from jax import lax
from jax.experimental import pallas as pl
from jax.experimental.pallas import tpu as pltpu
from jax.sharding import PartitionSpec as P

HD = 64
norm_eps = 1e-05
rope_base = 160000.0
SCALE = HD ** (-0.5)
LOG2E = 1.4426950408889634
BF = jnp.bfloat16
F32 = jnp.float32


EIGHTHS = [0, 4, 2, 6, 1, 5, 3, 7]


def exchange(value, axis, bit, name):
    size = lax.axis_size(axis)
    with jax.named_scope(f"{name}_{axis}{bit}"):
        return lax.ppermute(value, axis, [(i, i ^ bit) for i in range(size)])


def bits_of(size):
    assert size & (size - 1) == 0 and size >= 8
    return [1 << i for i in reversed(range(size.bit_length() - 1))]


def rank_order(size):
    order = [0]
    for bit in bits_of(size):
        order = order + [o ^ bit for o in order]
    return order


def gather_order(*low):
    return bits_of(lax.axis_size("dp"))[:-3] + list(low)


def scatter_order(*low):
    return list(low) + bits_of(lax.axis_size("dp"))[:-3][::-1]


def cut(array, parts):
    size = array.shape[-1] // parts
    return [array[..., i * size : (i + 1) * size] for i in range(parts)]


def join(pieces):
    return pieces[0] if len(pieces) == 1 else jnp.concatenate(pieces, axis=-1)


class Move:
    def __init__(self, value, axis, bit, name):
        self.value, self.axis, self.bit, self.name = value, axis, bit, name

    def take(self, got):
        self.got = got


class Gather:
    def __init__(self, shard, order, name):
        self.value, self.order, self.name, self.axis = shard, list(order), name, "dp"
        self.held = []
        while len(self.order) > 3:
            self.take(exchange(self.value, "dp", self.bit, self.name))

    @property
    def bit(self):
        return self.order[0]

    def take(self, got):
        bit = self.order.pop(0)
        outer = 2 ** sum(1 for other in self.held if other < bit)
        self.held.append(bit)
        if self.order:
            pairs = zip(cut(self.value, outer), cut(got, outer))
            self.value = join([piece for pair in pairs for piece in pair])
        else:
            self.outer = outer
            self.halves = (self.value, got)


class Scatter:
    def __init__(self, keep, send, order, name):
        self.keep, self.value, self.left, self.name, self.axis = keep, send, list(order), name, "dp"

    @property
    def bit(self):
        return self.left[0]

    def take(self, got):
        self.left.pop(0)
        if self.left:
            half = got.shape[-1] // 2
            sides = [(a[..., :half], a[..., half:]) for a in (self.keep, got)]
            self.keep, self.value = ((a.astype(F32) + b.astype(F32)).astype(BF) for a, b in zip(*sides))
        else:
            self.total = self.keep.astype(F32) + got.astype(F32)

    def end(self):
        while self.left:
            self.take(exchange(self.value, "dp", self.bit, self.name))
        return self.total


def stage(moves, work=None, *carry):
    got = [exchange(m.value, m.axis, m.bit, m.name) for m in moves]
    if work is None:
        carry = (idle(carry[0]), *carry[1:])
        done = ()
    else:
        done = work()
    got, done, carry = lax.optimization_barrier((got, tuple(done), carry))
    for m, g in zip(moves, got):
        m.take(g)
    return done, carry


class SeqRows:
    def __init__(self, own, name):
        self.own, self.name = own, name
        self.beside = Move(own, "mp", 1, name)
        self.across = Move(own, "mp", 2, name)

    def diag(self):
        self.last = Move(self.across.got, "mp", 1, self.name + "_diag")
        return self.last

    def parts(self):
        return tuple((a, None) for a in (self.own, self.beside.got, self.across.got, self.last.got))


class Sums:
    def __init__(self, keep, far, turn, name):
        self.keep, self.far, self.name = keep, far, name
        self.turn = Move(turn, "mp", 1, name + "_turn")

    def away(self):
        total = self.far.astype(F32) + self.turn.got[1].astype(F32)
        self.last = Move(total.astype(BF), "mp", 2, self.name)
        return self.last

    def total(self):
        return self.keep.astype(F32) + self.turn.got[0].astype(F32) + self.last.got.astype(F32)


def nt(a, b):
    return lax.dot_general(a, b, (((1,), (1,)), ((), ())), preferred_element_type=F32)


def nn(a, b):
    return lax.dot_general(a, b, (((1,), (0,)), ((), ())), preferred_element_type=F32)


def tn(a, b):
    return lax.dot_general(a, b, (((0,), (0,)), ((), ())), preferred_element_type=F32)


def aligned(index, step):
    return pl.ds(pl.multiple_of(index * step, step), step)


def picked(refs, picks):
    return [ref if pick is None else ref.at[pick] for ref, pick in zip(refs, picks)]


def start(source, into, sem):
    copy = pltpu.make_async_copy(source, into, sem)
    copy.start()
    return copy


def fetch(parts, place, sem, base=0):
    return [start(part, place(p), sem.at[base + p]) for p, part in enumerate(parts)]


def finish(copies):
    for copy in copies:
        copy.wait()


def await_slot(ref, sem):
    pltpu.make_async_copy(ref, ref, sem).wait()


def fetch_halves(own, got, into, outer, sem, base):
    size = own.shape[-1] // outer
    return [
        start(
            (own, got)[i % 2].at[:, i // 2 * size : (i // 2 + 1) * size],
            into.at[:, i * size : (i + 1) * size],
            sem.at[base + i],
        )
        for i in range(2 * outer)
    ]


def send_block(spot, held_ref, outs, sem, base=0):
    for k, out in enumerate(outs):

        @pl.when(spot == k)
        def _(k=k, out=out):
            start(held_ref.at[k], out, sem.at[base + k])


def sent_blocks(held_ref, outs, sem, base=0):
    finish([pltpu.make_async_copy(held_ref.at[k], out, sem.at[base + k]) for k, out in enumerate(outs)])


def spin(value, cos, sin):
    a, b = value[: HD // 2], value[HD // 2 :]
    return jnp.concatenate([a * cos - b * sin, b * cos + a * sin], axis=0)


def attn_fwd_kernel(
    where_ref, p0, p1, p2, p3, wa0, wa1, wb0, wb1, cos_in, sin_in,
    o0, o2, o13, rows_out, q_out, k_out, v_out, ctx_out, lse_out,
    raw_ref, wa_ref, wb_ref, cos_ref, sin_ref, rows_ref, q_ref, k_ref, v_ref, ctx_ref, lse_ref,
    knat_ref, held_ref, sem, out_sem, *, seq, outer, picks,
):
    me = where_ref[0]
    length = where_ref[1 + seq]
    outs = (o0, o13.at[0], o2, o13.at[1])
    block = rows_ref.shape[1]
    heads = lse_ref.shape[0]
    width = heads * HD
    count = lax.div(length + block - 1, block)
    copies = fetch_halves(wa0, wa1, wa_ref, outer[0], sem, 4)
    copies += fetch((cos_in, sin_in), lambda p: (cos_ref, sin_ref)[p], sem, 12)
    fetch(picked((p0, p1, p2, p3), picks), lambda p: raw_ref.at[me ^ p], sem)
    copies += fetch_halves(wb0, wb1, wb_ref, outer[1], sem, 8)
    finish(copies)

    def project(i, carry):
        await_slot(raw_ref.at[i], sem.at[me ^ i])
        raw = raw_ref[i].astype(F32)
        raw = raw - jnp.mean(raw, axis=-1, keepdims=True)
        scale = lax.rsqrt(jnp.mean(raw * raw, axis=-1, keepdims=True) + norm_eps)
        rows = (raw * scale * wa_ref[2 * width : 2 * width + 1].astype(F32)).astype(BF)
        rows_ref[i] = rows
        start(rows_ref.at[i], rows_out.at[i], out_sem.at[4 + i])
        spot = aligned(i, block)
        cos = cos_ref[:, spot]
        sin = sin_ref[:, spot]
        query = nt(wa_ref[:width], rows)
        key = nt(wa_ref[width : 2 * width], rows)
        for h in range(heads):
            hs = slice(h * HD, (h + 1) * HD)
            q_ref[hs, spot] = spin(query[hs], cos, sin).astype(BF)
            turned = spin(key[hs], cos, sin)
            k_ref[hs, spot] = turned.astype(BF)
            knat_ref[h, spot, :] = turned.T.astype(BF)
        v_ref[:, spot] = nt(wb_ref[:width], rows).astype(BF)
        return carry

    lax.fori_loop(0, count, project, 0)
    saves = [(q_ref, q_out), (k_ref, k_out), (v_ref, v_out)]
    saves = [start(ref, out, out_sem.at[8 + i]) for i, (ref, out) in enumerate(saves)]

    for n in range(1, 5):

        @pl.when(count == n)
        def _(n=n):
            last = lax.broadcasted_iota(jnp.int32, (block, block), 0) + (n - 1) * block < length

            def rows_of(i, carry):
                spot = aligned(i, block)
                for h in range(heads):
                    hs = slice(h * HD, (h + 1) * HD)
                    query = q_ref[hs, spot]
                    tiles = []
                    for j in range(n):
                        tile = nn(knat_ref[h, j * block : (j + 1) * block, :], query) * (SCALE * LOG2E)
                        if j == n - 1:
                            tile = jnp.where(last, tile, -1e30)
                        tiles.append(tile)
                    top = jnp.max(functools.reduce(jnp.maximum, tiles), axis=0, keepdims=True)
                    total = jnp.zeros((1, block), F32)
                    found = jnp.zeros((HD, block), F32)
                    for j, tile in enumerate(tiles):
                        weight = jnp.exp2(tile - top)
                        total = total + jnp.sum(weight, axis=0, keepdims=True)
                        found = found + nn(v_ref[hs, j * block : (j + 1) * block], weight.astype(BF))
                    ctx_ref[hs, spot] = (found / total).astype(BF)
                    lse_ref[h, :, spot] = top + jnp.log2(total)
                out = me ^ i
                held_ref[out] = nn(ctx_ref[:, spot].T, wb_ref[width:]).astype(BF)
                send_block(out, held_ref, outs, out_sem)
                return carry

            lax.fori_loop(0, n, rows_of, 0)

    saves += [start(ref, out, out_sem.at[11 + i]) for i, (ref, out) in enumerate([(ctx_ref, ctx_out), (lse_ref, lse_out)])]

    def blank(i, carry):
        await_slot(raw_ref.at[i], sem.at[me ^ i])
        out = me ^ i
        held_ref[out] = jnp.zeros(held_ref.shape[1:], BF)
        send_block(out, held_ref, outs, out_sem)
        rows_ref[i] = held_ref[out]
        start(rows_ref.at[i], rows_out.at[i], out_sem.at[4 + i])
        return carry

    lax.fori_loop(count, 4, blank, 0)
    finish(saves)
    sent_blocks(rows_ref, [rows_out.at[i] for i in range(4)], out_sem, 4)
    sent_blocks(held_ref, outs, out_sem)


def put_halves(keep_ref, send_ref, rows, value, order):
    size = value.shape[-1] // 8
    for side, ref in enumerate((keep_ref, send_ref)):
        for i in range(4):
            offset = side * order[0] + i // 2 * order[1] + i % 2 * order[2]
            place = EIGHTHS.index(offset)
            ref[rows, i * size : (i + 1) * size] = value[:, place * size : (place + 1) * size].astype(BF)


def attn_bwd_kernel(
    where_ref, p0, p1, p2, p3, wa0, wa1, wb0, wb1, rows_in, q_in, k_in, v_in, ctx_in, lse_in,
    cos_in, sin_in, *rest, seq, old, orders, outer_w,
):
    if old:
        old_in, oldgain_ref, *rest = rest
    (o0, o2, o13), rest = rest[:3], rest[3:]
    outs = (o0, o13.at[0], o2, o13.at[1])
    if old:
        g_outs, g_refs, gain_ref, rest = rest[:4], rest[4:8], rest[8], rest[9:]
    else:
        grad_out, gain_ref, *rest = rest
    (
        grad_ref, wa_ref, wb_ref, rows_ref, q_ref, k_ref, v_ref, ctx_ref, lse_ref, cos_ref, sin_ref,
        back_ref, cb_ref, knat_ref, vnat_ref, d_ref, dk_ref, dv_ref, delta_ref, held_ref, sem, out_sem,
    ) = rest
    me = where_ref[0]
    length = where_ref[1 + seq]
    block = rows_ref.shape[1]
    heads = lse_ref.shape[0]
    width = heads * HD
    count = lax.div(length + block - 1, block)
    early = fetch_halves(wb0, wb1, wb_ref, outer_w[1], sem, 8)
    fetch((p0, p1, p2, p3), lambda p: back_ref.at[me ^ p], sem)
    saved = (ctx_in, k_in, v_in, q_in, lse_in, cos_in, sin_in)
    places = (ctx_ref, k_ref, v_ref, q_ref, lse_ref, cos_ref, sin_ref)
    early += fetch(saved, lambda p: places[p], sem, 12)
    late = fetch((rows_in,), lambda p: rows_ref, sem, 19)
    late += fetch_halves(wa0, wa1, wa_ref, outer_w[0], sem, 4)
    if old:
        late += fetch((old_in,), lambda p: grad_ref, sem, 20)
        gain_ref[...] = oldgain_ref[...]
    else:
        gain_ref[...] = jnp.zeros(gain_ref.shape, F32)
    dk_ref[...] = jnp.zeros(dk_ref.shape, F32)
    dv_ref[...] = jnp.zeros(dv_ref.shape, F32)
    finish(early)

    def prepare(i, carry):
        await_slot(back_ref.at[i], sem.at[me ^ i])
        spot = aligned(i, block)
        low = nt(wb_ref[width:], back_ref[i]).astype(BF)
        cb_ref[:, spot] = low
        inner = low.astype(F32) * ctx_ref[:, spot].astype(F32)
        for h in range(heads):
            hs = slice(h * HD, (h + 1) * HD)
            delta_ref[h, :, spot] = jnp.sum(inner[hs], axis=0, keepdims=True)
            knat_ref[h, spot, :] = k_ref[hs, spot].T
            vnat_ref[h, spot, :] = v_ref[hs, spot].T
        return carry

    lax.fori_loop(0, count, prepare, 0)

    def unspin(value, spot):
        return spin(value * SCALE, cos_ref[:, spot], -sin_ref[:, spot]).astype(BF)

    for n in range(1, 5):

        @pl.when(count == n)
        def _(n=n):
            last = lax.broadcasted_iota(jnp.int32, (block, block), 0) + (n - 1) * block < length

            def rows_of(i, carry):
                spot = aligned(i, block)
                for h in range(heads):
                    hs = slice(h * HD, (h + 1) * HD)
                    query = q_ref[hs, spot]
                    cb = cb_ref[hs, spot]
                    lse = lse_ref[h, :, spot]
                    delta = delta_ref[h, :, spot]
                    dq = jnp.zeros((HD, block), F32)
                    for j in range(n):
                        js = slice(j * block, (j + 1) * block)
                        tile = nn(knat_ref[h, js, :], query) * (SCALE * LOG2E) - lse
                        if j == n - 1:
                            tile = jnp.where(last, tile, -1e30)
                        weight = jnp.exp2(tile)
                        back = nn(vnat_ref[h, js, :], cb)
                        ds = (weight * (back - delta)).astype(BF)
                        dv_ref[hs, js] += nt(cb, weight.astype(BF))
                        dk_ref[hs, js] += nt(query, ds)
                        dq = dq + nn(k_ref[hs, js], ds)
                    d_ref[hs, spot] = unspin(dq, spot)
                return carry

            lax.fori_loop(0, n, rows_of, 0)
            for i in range(n):
                spot = slice(i * block, (i + 1) * block)
                for h in range(heads):
                    hs = slice(h * HD, (h + 1) * HD)
                    d_ref[width + h * HD : width + (h + 1) * HD, spot] = unspin(dk_ref[hs, spot], spot)
                d_ref[2 * width :, spot] = dv_ref[:, spot].astype(BF)
            finish(late)
            full = slice(0, n * block)
            rows = rows_ref[:n].reshape(n * block, -1)
            back = back_ref[:n].reshape(n * block, -1)
            pieces = [(k, d_ref[k * width : (k + 1) * width, full], rows) for k in range(3)]
            pieces.append((3, ctx_ref[:, full], back))
            for k, left, right in pieces:
                at = slice(k * width, (k + 1) * width)
                value = nn(left, right)
                if old:
                    pair = g_refs[k // 2 * 2 : k // 2 * 2 + 2]
                    put_halves(*pair, slice(k % 2 * width, (k % 2 + 1) * width), grad_ref[at] + value, orders[k // 2])
                else:
                    grad_ref[at] = value

    saves = []
    if not old:
        saves = [start(grad_ref, grad_out, out_sem.at[4])]
    else:
        saves = [start(ref, out, out_sem.at[4 + i]) for i, (ref, out) in enumerate(zip(g_refs[:2], g_outs[:2]))]

    def close(i, carry):
        turned = d_ref[:, aligned(i, block)].T
        out = nn(turned[:, : 2 * width], wa_ref[: 2 * width]) + nn(turned[:, 2 * width :], wb_ref[:width])
        held_ref[me ^ i] = out.astype(BF)
        send_block(me ^ i, held_ref, outs, out_sem)
        gain_ref[:1] += jnp.sum(out * rows_ref[i].astype(F32), axis=0, keepdims=True)
        return carry

    lax.fori_loop(0, count, close, 0)

    def blank(i, carry):
        await_slot(back_ref.at[i], sem.at[me ^ i])
        held_ref[me ^ i] = jnp.zeros(held_ref.shape[1:], BF)
        send_block(me ^ i, held_ref, outs, out_sem)
        return carry

    lax.fori_loop(count, 4, blank, 0)
    if old:
        put_halves(g_refs[2], g_refs[3], slice(2 * width, None), gain_ref[...], orders[1])
        saves += [start(ref, out, out_sem.at[6 + i]) for i, (ref, out) in enumerate(zip(g_refs[2:], g_outs[2:]))]
    finish(saves)
    sent_blocks(held_ref, outs, out_sem)


def ffn_kernel(
    where_ref, a0, a1, a2, a3, b0, b1, b2, b3, wu0, wu1, wg0, wg1, wo0, wo1,
    f0, f2, f13, n0, n2, n13, ub_out, gb_out, mixed_out, gain_ref,
    rows_ref, back_ref, fheld_ref, nheld_ref, ub_ref, gb_ref, mixed_ref, wu_ref, wg_ref, wo_ref, sem, out_sem,
    *, seq, outer, picks,
):
    me = where_ref[0]
    length = where_ref[1 + seq]
    block = rows_ref.shape[1]
    fouts = (f0, f13.at[0], f2, f13.at[1])
    nouts = (n0, n13.at[0], n2, n13.at[1])
    copies = fetch_halves(wu0, wu1, wu_ref, outer[0], sem, 8)
    aparts, bparts = picked((a0, a1, a2, a3), picks[:4]), picked((b0, b1, b2, b3), picks[4:])
    start(aparts[0], rows_ref.at[0], sem.at[0])
    copies += fetch_halves(wg0, wg1, wg_ref, outer[1], sem, 12)
    start(bparts[0], back_ref.at[0], sem.at[4])
    copies += fetch_halves(wo0, wo1, wo_ref, outer[2], sem, 16)
    for p in range(1, 4):
        start(aparts[p], rows_ref.at[p], sem.at[p])
        start(bparts[p], back_ref.at[p], sem.at[4 + p])
    gain_ref[...] = jnp.zeros(gain_ref.shape, F32)
    finish(copies)
    kept = ((ub_ref, ub_out), (gb_ref, gb_out), (mixed_ref, mixed_out))

    def step(p, carry):
        valid = (me ^ p) * block < length
        await_slot(rows_ref.at[p], sem.at[p])
        await_slot(back_ref.at[p], sem.at[4 + p])

        @pl.when(valid)
        def _():
            rows = rows_ref[p]
            up = nt(rows, wu_ref[...])
            gate = nt(rows, wg_ref[...])
            mb = nt(back_ref[p], wo_ref[...])
            phi = 0.5 + 0.5 * lax.erf(up * (0.5**0.5))
            act = up * phi
            mixed = (act * gate).astype(BF)
            mixed_ref[p] = mixed
            slope = phi + up * (jnp.exp(-0.5 * up * up) * (0.5 / np.pi) ** 0.5)
            ub = (mb * gate * slope).astype(BF)
            gb = (mb * act).astype(BF)
            ub_ref[p] = ub
            gb_ref[p] = gb
            out = nn(ub, wu_ref[...]) + nn(gb, wg_ref[...])
            nheld_ref[p] = out.astype(BF)
            gain_ref[1:2] += jnp.sum(out * rows.astype(F32), axis=0, keepdims=True)
            fheld_ref[p] = nn(mixed, wo_ref[...]).astype(BF)

        @pl.when(jnp.logical_not(valid))
        def _():
            for ref in (mixed_ref, ub_ref, gb_ref, nheld_ref, fheld_ref):
                ref[p] = jnp.zeros(ref.shape[1:], BF)

        send_block(p, nheld_ref, nouts, out_sem, 4)
        send_block(p, fheld_ref, fouts, out_sem)
        for k, (ref, out) in enumerate(kept):
            start(ref.at[p], out.at[p], out_sem.at[8 + 4 * k + p])
        return carry

    lax.fori_loop(0, 4, step, 0)
    sent_blocks(nheld_ref, nouts, out_sem, 4)
    sent_blocks(fheld_ref, fouts, out_sem)
    for k, (ref, out) in enumerate(kept):
        sent_blocks(ref, [out.at[p] for p in range(4)], out_sem, 8 + 4 * k)


def ffn_grad_kernel(_, *refs, orders, picks):
    parts, saved, refs = picked(refs[:16], picks), refs[16:22], refs[22:]
    outs, (rows_ref, back_ref, saved_ref, *held), refs = refs[:4], refs[4:11], refs[11:]
    g_ref, sem, out_sem = refs
    units = g_ref.shape[1]
    copies = []
    for s in range(2):
        rows = fetch(parts[8 * s : 8 * s + 4], lambda p: rows_ref.at[s, p], sem, 8 * s)
        backs = lambda: fetch(parts[8 * s + 4 : 8 * s + 8], lambda p: back_ref.at[s, p], sem, 8 * s + 4)
        kept = lambda k: fetch((saved[3 * s + k],), lambda p: saved_ref.at[s, k], sem, 16 + 3 * s + k)
        copies += [rows + kept(0), kept(1), kept(2) + backs()]
    sent = []
    for s in range(2):
        rows = rows_ref.at[s]
        for k in range(3):
            finish(copies[3 * s + k])
            other = (back_ref if k == 2 else rows_ref)[s].reshape(-1, rows_ref.shape[-1])
            part = tn(saved_ref[s, k].reshape(-1, units), other)
            if s == 0:
                g_ref[k] = part
                continue
            pair = held[k // 2 * 2 : k // 2 * 2 + 2]
            at = slice(None) if k == 2 else slice(k * units, (k + 1) * units)
            put_halves(*pair, at, g_ref[k] + part, orders[k // 2])
            if k > 0:
                sent += [start(ref, out, out_sem.at[k // 2 * 2 + i]) for i, (ref, out) in enumerate(zip(pair, outs[k // 2 * 2 :][:2]))]
    finish(sent)


SMEM = pl.BlockSpec(memory_space=pltpu.SMEM)
VMEM = pl.BlockSpec(memory_space=pltpu.VMEM)
HBM = pl.BlockSpec(memory_space=pl.ANY)
LIMIT = 60 * 1024 * 1024
PARAMS = pltpu.CompilerParams(vmem_limit_bytes=LIMIT)
GAIN_ROWS = 16


def shape(*dims, kind=BF):
    return jax.ShapeDtypeStruct(dims, kind)


def idle(where):
    return pl.pallas_call(
        lambda in_ref, out_ref: None,
        out_shape=jax.ShapeDtypeStruct(where.shape, where.dtype),
        in_specs=[pl.BlockSpec(memory_space=pl.ANY)],
        out_specs=pl.BlockSpec(memory_space=pl.ANY),
        input_output_aliases={0: 0},
        cost_estimate=pl.CostEstimate(flops=1 << 34, bytes_accessed=1 << 20, transcendentals=0),
        name="idle",
    )(where)


def partials(block, width):
    return (shape(block, width), shape(block, width), shape(2, block, width))


def vmem(array):
    return pltpu.VMEM(array.shape, array.dtype)


def attn_fwd(where, seq, parts, wa, wb, cos, sin):
    arrays, picks = zip(*parts)
    block, width = arrays[0].shape[-2:]
    rows = wb.halves[0].shape[0]
    cols = rows // 2
    heads = cols // HD
    full = 4 * block
    flops = 2 * full * width * cols * 4 + 4 * full * full * cols
    saved = (shape(4, block, width),) + (shape(cols, full),) * 4 + (shape(heads, 1, full, kind=F32),)
    return pl.pallas_call(
        functools.partial(attn_fwd_kernel, seq=seq, outer=(wa.outer, wb.outer), picks=picks),
        out_shape=partials(block, width) + saved,
        in_specs=[SMEM] + [HBM] * 10,
        out_specs=(HBM,) * 9,
        scratch_shapes=[
            pltpu.VMEM((4, block, width), BF),
            pltpu.VMEM(wa.halves[0].shape[:1] + (width,), BF),
            pltpu.VMEM((rows, width), BF),
            vmem(cos),
            vmem(sin),
            *[vmem(array) for array in saved],
            pltpu.VMEM((heads, full, HD), BF),
            pltpu.VMEM((4, block, width), BF),
            pltpu.SemaphoreType.DMA((14,)),
            pltpu.SemaphoreType.DMA((13,)),
        ],
        compiler_params=pltpu.CompilerParams(vmem_limit_bytes=58 << 20),
        cost_estimate=pl.CostEstimate(flops=flops * 3, bytes_accessed=12 << 20, transcendentals=heads * full * full),
        name="attn_fwd",
    )(where, *arrays, *wa.halves, *wb.halves, cos, sin)


def attn_bwd(where, seq, parts, saved, wa, wb, cos, sin, old, orders):
    arrays = [array for array, _ in parts]
    block, width = arrays[0].shape
    rows = wb.halves[0].shape[0]
    cols = rows // 2
    heads = cols // HD
    full = 4 * block
    flops = 4 * full * width * cols * 4 + 10 * full * full * cols
    extra = [] if old is None else list(old)
    grads = shape(4 * cols, width, kind=F32)
    gain = shape(GAIN_ROWS, width, kind=F32)
    halved = (shape(rows, width // 2),) * 2 + (shape(rows + GAIN_ROWS, width // 2),) * 2
    outs = (grads,) if old is None else halved
    return pl.pallas_call(
        functools.partial(
            attn_bwd_kernel,
            seq=seq,
            old=old is not None,
            orders=orders,
            outer_w=(wa.outer, wb.outer),
        ),
        out_shape=partials(block, width) + outs + (() if extra else (gain,)),
        in_specs=[SMEM] + [HBM] * 16 + ([] if old is None else [HBM, VMEM]),
        out_specs=(HBM,) * (3 + len(outs)) + (() if extra else (VMEM,)),
        scratch_shapes=[vmem(array) for array in ((grads,) if old is None else halved + (gain, grads))] + [
            pltpu.VMEM(wa.halves[0].shape[:1] + (width,), BF),
            pltpu.VMEM((rows, width), BF),
            *[vmem(array) for array in saved],
            vmem(cos),
            vmem(sin),
            pltpu.VMEM((4, block, width), BF),
            pltpu.VMEM((cols, full), BF),
            pltpu.VMEM((heads, full, HD), BF),
            pltpu.VMEM((heads, full, HD), BF),
            pltpu.VMEM((3 * cols, full), BF),
            pltpu.VMEM((cols, full), F32),
            pltpu.VMEM((cols, full), F32),
            pltpu.VMEM((heads, 1, full), F32),
            pltpu.VMEM((4, block, width), BF),
            pltpu.SemaphoreType.DMA((21,)),
            pltpu.SemaphoreType.DMA((8,)),
        ],
        compiler_params=pltpu.CompilerParams(vmem_limit_bytes=32 << 20),
        cost_estimate=pl.CostEstimate(flops=flops * 3, bytes_accessed=16 << 20, transcendentals=heads * full * full),
        name="attn_bwd",
    )(where, *arrays, *wa.halves, *wb.halves, *saved, cos, sin, *extra)


def ffn(where, seq, parts, backs, weights):
    arrays, picks = zip(*parts, *backs)
    block, width = arrays[0].shape[-2:]
    units = weights[0].halves[0].shape[0]
    flops = 2 * 4 * block * width * units * 6
    saved = (shape(4, block, units),) * 3
    return pl.pallas_call(
        functools.partial(ffn_kernel, seq=seq, outer=[w.outer for w in weights], picks=picks),
        out_shape=partials(block, width) * 2 + saved + (shape(GAIN_ROWS, width, kind=F32),),
        in_specs=[SMEM] + [HBM] * 14,
        out_specs=(HBM,) * 9 + (VMEM,),
        scratch_shapes=[pltpu.VMEM((4, block, width), BF)] * 4
        + [vmem(array) for array in saved]
        + [pltpu.VMEM((units, width), BF)] * 3
        + [pltpu.SemaphoreType.DMA((20,)), pltpu.SemaphoreType.DMA((20,))],
        compiler_params=pltpu.CompilerParams(vmem_limit_bytes=58 << 20),
        cost_estimate=pl.CostEstimate(flops=flops, bytes_accessed=20 << 20, transcendentals=2 * 4 * block * units),
        name="ffn",
    )(where, *arrays, *[half for w in weights for half in w.halves])


def ffn_grad(where, parts, saved, orders):
    arrays, picks = zip(*parts)
    block, width = arrays[0].shape[-2:]
    units = saved[0].shape[2]
    outs = (shape(2 * units, width // 2),) * 2 + (shape(units, width // 2),) * 2
    return pl.pallas_call(
        functools.partial(ffn_grad_kernel, orders=orders, picks=picks),
        out_shape=outs,
        in_specs=[SMEM] + [HBM] * 22,
        out_specs=(HBM,) * 4,
        scratch_shapes=[pltpu.VMEM((2, 4, block, width), BF)] * 2
        + [pltpu.VMEM((2, 3) + saved[0].shape, BF)]
        + [vmem(array) for array in outs]
        + [pltpu.VMEM((3, units, width), F32), pltpu.SemaphoreType.DMA((22,)), pltpu.SemaphoreType.DMA((4,))],
        compiler_params=pltpu.CompilerParams(vmem_limit_bytes=40 << 20),
        cost_estimate=pl.CostEstimate(flops=2 * 8 * block * width * units * 3, bytes_accessed=24 << 20, transcendentals=0),
        name="ffn_grad",
    )(where, *arrays, *saved)


def norm_parts(values):
    average = jnp.mean(values, axis=-1, keepdims=True)
    centred = values - average
    spread = jnp.mean(centred * centred, axis=-1, keepdims=True)
    scale = lax.rsqrt(spread + norm_eps)
    return centred * scale, scale


def norm_back(grad, gain, normed, scale):
    y = grad * gain
    return scale * (
        y - jnp.mean(y, axis=-1, keepdims=True) - normed * jnp.mean(y * normed, axis=-1, keepdims=True)
    )


def rope_tables(length):
    places = np.arange(length, dtype=np.float32)
    frequency = (rope_base ** (-np.arange(0, HD, 2, dtype=np.float32) / HD)).astype(np.float32)
    angles = (frequency[:, None] * places[None, :]).astype(np.float32)
    return jnp.asarray(np.cos(angles)), jnp.asarray(np.sin(angles))


def per_device(
    tokens, lengths, attn_norm, qkv_weight, attn_out_weight, ffn_norm, ffn_in_weight, ffn_out_weight, out_grad
):
    seqs, local_len, width = tokens.shape
    assert lax.axis_size("mp") == 4 and seqs == 2
    groups = lax.axis_size("dp")
    me = lax.axis_index("mp")
    full_len = 4 * local_len
    cols = qkv_weight.shape[2]
    units = ffn_in_weight.shape[2]
    span = width // groups
    cos, sin = rope_tables(full_len)

    ranks = rank_order(groups)
    order = jnp.asarray(np.array(ranks, np.int32)) ^ lax.axis_index("dp")
    source = (order[:, None] * span + jnp.arange(span, dtype=jnp.int32)[None, :]).reshape(width)
    reorder = (source[None, :] == jnp.arange(width, dtype=jnp.int32)[:, None]).astype(BF)

    def to_own(rows):
        return jnp.dot(rows.reshape(-1, width), reorder, preferred_element_type=F32).astype(BF).reshape(rows.shape)

    def from_own(rows):
        return lax.dot_general(
            rows, reorder, (((1,), (1,)), ((), ())), preferred_element_type=F32
        ).astype(BF)

    far, near = gather_order(4, 2, 1), gather_order(1, 4, 2)
    qkv = jnp.swapaxes(qkv_weight, 1, 2)
    ffn_in = jnp.swapaxes(ffn_in_weight, 1, 2)
    own_gains = jnp.stack([attn_norm, ffn_norm])
    own_gains = jnp.pad(own_gains, ((0, 14), (0, 0)))
    wa = Gather(jnp.concatenate([qkv[:2].reshape(2 * cols, span), own_gains], axis=0), far, "w_qk")
    wb = Gather(jnp.concatenate([qkv[2], attn_out_weight], axis=0), near, "w_vo")
    w_up = Gather(ffn_in[0], far, "w_up")
    w_gate = Gather(ffn_in[1], far, "w_gate")
    w_out = Gather(ffn_out_weight, near, "w_out")

    local = me * local_len + jnp.arange(local_len, dtype=jnp.int32)
    where = jnp.concatenate([me[None], lengths]).astype(jnp.int32)
    valid = [(local < lengths[s]).astype(F32)[:, None] for s in range(seqs)]
    token_low = [to_own(tokens[s]) for s in range(seqs)]
    token = [SeqRows(token_low[s], f"token{s}") for s in range(seqs)]

    _, (where, token[1].across.value, out_grad, w_out.value) = stage(
        [wa, w_up, token[0].across, wb, token[0].beside],
        None,
        where, token[1].across.value, out_grad, w_out.value,
    )

    def prepare():
        return *[(valid[s] * to_own(out_grad[s]).astype(F32)).astype(BF) for s in range(seqs)], idle(where)

    (*back_low, where), (token_low,) = stage(
        [wb, token[1].across, wa, w_out, token[0].diag()], prepare, token_low
    )
    outback = [SeqRows(back_low[s], f"outback{s}") for s in range(seqs)]
    _, (where, w_gate.value) = stage(
        [wb, wa, outback[0].across, token[1].beside, token[1].diag()], None, where, w_gate.value
    )
    ffn_gain = join([half[2 * cols + 1 : 2 * cols + 2] for half in wa.halves]).astype(F32)
    attn_gain = join([half[2 * cols : 2 * cols + 1] for half in wa.halves]).astype(F32)

    done, (where,) = stage(
        [outback[1].across, w_up, w_gate, outback[0].beside, outback[1].beside],
        lambda: attn_fwd(where, 0, token[0].parts(), wa, wb, cos, sin),
        where,
    )
    attn = [Sums(*done[:3], "attn0")]
    saved = [done[3:]]
    stage_turn = lambda sums, *others: stage([sums.turn, *others], lambda: (), where)
    _, (where,) = stage_turn(attn[0], outback[0].diag())
    done, (where,) = stage(
        [attn[0].away(), w_up, w_gate, w_out, outback[1].diag()],
        lambda: attn_fwd(where, 1, token[1].parts(), wa, wb, cos, sin),
        where,
    )
    attn.append(Sums(*done[:3], "attn1"))
    saved.append(done[3:])

    def second_norm(s):
        rows = token_low[s].astype(F32) + attn[s].total()
        normed, scale = norm_parts(rows)
        return rows, normed, scale, (normed * ffn_gain).astype(BF)

    hidden, second, two = [None, None], [None, None], [None, None]

    (done,), (where,) = stage([attn[1].turn], lambda: (second_norm(0),), where)
    hidden[0], second[0] = done[0], done[1:3]
    two[0] = SeqRows(done[3], "two0")
    _, (where,) = stage([two[0].across, attn[1].away(), w_out, w_gate, two[0].beside], None, where)
    (done,), (where,) = stage([two[0].diag()], lambda: (second_norm(1),), where)
    hidden[1], second[1] = done[0], done[1:3]
    two[1] = SeqRows(done[3], "two1")
    weights = (w_up, w_gate, w_out)
    done, (where,) = stage(
        [two[1].across, two[1].beside],
        lambda: ffn(where, 0, two[0].parts(), outback[0].parts(), weights),
        where,
    )
    ff, twoback = [Sums(*done[:3], "ff0")], [Sums(*done[3:6], "twoback0")]
    ffn_saved, ffn_gains = list(done[6:9]), done[9]
    _, (where,) = stage_turn(twoback[0], two[1].diag())
    done, (where,) = stage(
        [twoback[0].away(), ff[0].turn],
        lambda: ffn(where, 1, two[1].parts(), outback[1].parts(), weights),
        where,
    )
    ff.append(Sums(*done[:3], "ff1"))
    twoback.append(Sums(*done[3:6], "twoback1"))
    ffn_saved += done[6:9]
    ffn_gains = ffn_gains + done[9]

    def second_back(s):
        rows = back_low[s].astype(F32) + norm_back(twoback[s].total(), ffn_gain, *second[s])
        return rows, rows.astype(BF)

    hidden_back, hidback = [None, None], [None, None]
    (done,), (where,) = stage([twoback[1].turn], lambda: (second_back(0),), where)
    hidden_back[0] = done[0]
    hidback[0] = SeqRows(done[1], "hidback0")
    orders = (scatter_order(2, 4, 1), scatter_order(1, 2, 4))

    def weight_grads():
        grads = ffn_grad(
            where, [p for s in range(seqs) for p in two[s].parts() + outback[s].parts()], ffn_saved, orders
        )
        return grads

    done, (where,) = stage(
        [twoback[1].away(), hidback[0].across, hidback[0].beside, ff[1].turn], weight_grads, where
    )
    g_in = Scatter(*done[:2], orders[0], "g_in")
    g_out = Scatter(*done[2:], orders[1], "g_out")
    (done,), (where,) = stage([hidback[0].diag()], lambda: (second_back(1),), where)
    hidden_back[1] = done[0]
    hidback[1] = SeqRows(done[1], "hidback1")

    orders = (scatter_order(1, 2, 4), scatter_order(2, 4, 1))
    done, (where,) = stage(
        [g_in, g_out, hidback[1].across, ff[0].away(), hidback[1].beside],
        lambda: attn_bwd(where, 0, hidback[0].parts(), saved[0], wa, wb, cos, sin, None, orders),
        where,
    )
    oneback = [Sums(*done[:3], "oneback0")]
    sums = [done[3], done[4] + ffn_gains]
    _, (where,) = stage_turn(oneback[0], hidback[1].diag())
    done, (where, token_low) = stage(
        [g_in, oneback[0].away(), ff[1].away(), g_out],
        lambda: attn_bwd(where, 1, hidback[1].parts(), saved[1], wa, wb, cos, sin, sums, orders),
        where, token_low,
    )
    oneback.append(Sums(*done[:3], "oneback1"))
    g_qk = Scatter(*done[3:5], orders[0], "g_qk")
    g_vo = Scatter(*done[5:7], orders[1], "g_vo")
    def close(s):
        return (hidden_back[s] + norm_back(oneback[s].total(), attn_gain, *norm_parts(token_low[s].astype(F32)))).astype(BF)

    def ready():
        rows = [(valid[s] * (hidden[s] + ff[s].total())).astype(BF) for s in range(seqs)]
        return from_own(jnp.concatenate(rows, axis=0)), close(0)

    (output, input_grad), (where,) = stage([g_vo, g_qk, g_out, oneback[1].turn], ready, where)
    _, (where,) = stage([g_vo, oneback[1].away(), g_qk, g_in], None, where)
    stage([g_vo, g_qk], None, where)
    grad_qk, grad_vo = g_qk.end(), g_vo.end()
    gain_back = grad_vo[2 * cols : 2 * cols + 2]
    ones, twos, threes = (exchange(gain_back, "mp", k, "gain") for k in (1, 2, 3))
    gain_back = (gain_back + ones) + (twos + threes)
    input_grad = from_own(jnp.concatenate([input_grad, close(1)], axis=0))
    grad_qkv = jnp.concatenate([grad_qk, grad_vo[:cols]], axis=0).reshape(3, cols, span)
    return (
        output.reshape(seqs, local_len, width),
        input_grad.reshape(seqs, local_len, width),
        gain_back[0] / attn_norm.astype(F32),
        jnp.swapaxes(grad_qkv, 1, 2),
        grad_vo[cols : 2 * cols],
        gain_back[1] / ffn_norm.astype(F32),
        jnp.swapaxes(g_in.end().reshape(2, units, span), 1, 2),
        g_out.end(),
    )


def solution(mesh):
    in_specs = (
        P("dp", "mp", None),
        P("dp"),
        P("dp"),
        P(None, "dp", "mp"),
        P("mp", "dp"),
        P("dp"),
        P(None, "dp", "mp"),
        P("mp", "dp"),
        P("dp", "mp", None),
    )
    out_specs = (
        P("dp", "mp", None),
        P("dp", "mp", None),
        P("dp"),
        P(None, "dp", "mp"),
        P("mp", "dp"),
        P("dp"),
        P(None, "dp", "mp"),
        P("mp", "dp"),
    )
    return jax.shard_map(
        per_device, mesh=mesh, in_specs=in_specs, out_specs=out_specs, check_vma=False
    )
```

```python
import functools

import jax
import jax.numpy as jnp
import numpy as np
from jax import lax
from jax.experimental import pallas as pl
from jax.experimental.pallas import tpu as pltpu
from jax.sharding import PartitionSpec as P

HD = 64
norm_eps = 1e-05
rope_base = 160000.0
SCALE = HD ** (-0.5)
LOG2E = 1.4426950408889634
BF = jnp.bfloat16
F32 = jnp.float32


EIGHTHS = [0, 4, 2, 6, 1, 5, 3, 7]


def exchange(value, axis, bit, name):
    size = lax.axis_size(axis)
    with jax.named_scope(f"{name}_{axis}{bit}"):
        return lax.ppermute(value, axis, [(i, i ^ bit) for i in range(size)])


def bits_of(size):
    assert size & (size - 1) == 0 and size >= 8
    return [1 << i for i in reversed(range(size.bit_length() - 1))]


def rank_order(size):
    order = [0]
    for bit in bits_of(size):
        order = order + [o ^ bit for o in order]
    return order


def gather_order(*low):
    return bits_of(lax.axis_size("dp"))[:-3] + list(low)


def scatter_order(*low):
    return list(low) + bits_of(lax.axis_size("dp"))[:-3][::-1]


def cut(array, parts):
    size = array.shape[-1] // parts
    return [array[..., i * size : (i + 1) * size] for i in range(parts)]


def join(pieces):
    return pieces[0] if len(pieces) == 1 else jnp.concatenate(pieces, axis=-1)


class Move:
    def __init__(self, value, axis, bit, name):
        self.value, self.axis, self.bit, self.name = value, axis, bit, name

    def take(self, got):
        self.got = got


class Gather:
    def __init__(self, shard, order, name):
        self.value, self.order, self.name, self.axis = shard, list(order), name, "dp"
        self.held = []
        while len(self.order) > 3:
            self.take(exchange(self.value, "dp", self.bit, self.name))

    @property
    def bit(self):
        return self.order[0]

    def take(self, got):
        bit = self.order.pop(0)
        outer = 2 ** sum(1 for other in self.held if other < bit)
        self.held.append(bit)
        if self.order:
            pairs = zip(cut(self.value, outer), cut(got, outer))
            self.value = join([piece for pair in pairs for piece in pair])
        else:
            self.outer = outer
            self.halves = (self.value, got)


class Scatter:
    def __init__(self, keep, send, order, name):
        self.keep, self.value, self.left, self.name, self.axis = keep, send, list(order), name, "dp"

    @property
    def bit(self):
        return self.left[0]

    def take(self, got):
        self.left.pop(0)
        if self.left:
            half = got.shape[-1] // 2
            sides = [(a[..., :half], a[..., half:]) for a in (self.keep, got)]
            self.keep, self.value = ((a.astype(F32) + b.astype(F32)).astype(BF) for a, b in zip(*sides))
        else:
            self.total = self.keep.astype(F32) + got.astype(F32)

    def end(self):
        while self.left:
            self.take(exchange(self.value, "dp", self.bit, self.name))
        return self.total


def stage(moves, work=None, *carry):
    got = [exchange(m.value, m.axis, m.bit, m.name) for m in moves]
    if work is None:
        carry = (idle(carry[0]), *carry[1:])
        done = ()
    else:
        done = work()
    got, done, carry = lax.optimization_barrier((got, tuple(done), carry))
    for m, g in zip(moves, got):
        m.take(g)
    return done, carry


class SeqRows:
    def __init__(self, own, name):
        self.own, self.name = own, name
        self.beside = Move(own, "mp", 1, name)
        self.across = Move(own, "mp", 2, name)

    def diag(self):
        self.last = Move(self.across.got, "mp", 1, self.name + "_diag")
        return self.last

    def parts(self):
        return tuple((a, None) for a in (self.own, self.beside.got, self.across.got, self.last.got))


class Sums:
    def __init__(self, keep, far, turn, name):
        self.keep, self.far, self.name = keep, far, name
        self.turn = Move(turn, "mp", 1, name + "_turn")

    def away(self):
        total = self.far.astype(F32) + self.turn.got[1].astype(F32)
        self.last = Move(total.astype(BF), "mp", 2, self.name)
        return self.last

    def total(self):
        return self.keep.astype(F32) + self.turn.got[0].astype(F32) + self.last.got.astype(F32)


def nt(a, b):
    return lax.dot_general(a, b, (((1,), (1,)), ((), ())), preferred_element_type=F32)


def nn(a, b):
    return lax.dot_general(a, b, (((1,), (0,)), ((), ())), preferred_element_type=F32)


def tn(a, b):
    return lax.dot_general(a, b, (((0,), (0,)), ((), ())), preferred_element_type=F32)


def aligned(index, step):
    return pl.ds(pl.multiple_of(index * step, step), step)


def picked(refs, picks):
    return [ref if pick is None else ref.at[pick] for ref, pick in zip(refs, picks)]


def start(source, into, sem):
    copy = pltpu.make_async_copy(source, into, sem)
    copy.start()
    return copy


def fetch(parts, place, sem, base=0):
    return [start(part, place(p), sem.at[base + p]) for p, part in enumerate(parts)]


def finish(copies):
    for copy in copies:
        copy.wait()


def await_slot(ref, sem):
    pltpu.make_async_copy(ref, ref, sem).wait()


def fetch_halves(own, got, into, outer, sem, base):
    size = own.shape[-1] // outer
    return [
        start(
            (own, got)[i % 2].at[:, i // 2 * size : (i // 2 + 1) * size],
            into.at[:, i * size : (i + 1) * size],
            sem.at[base + i],
        )
        for i in range(2 * outer)
    ]


def send_block(spot, held_ref, outs, sem, base=0):
    for k, out in enumerate(outs):

        @pl.when(spot == k)
        def _(k=k, out=out):
            start(held_ref.at[k], out, sem.at[base + k])


def sent_blocks(held_ref, outs, sem, base=0):
    finish([pltpu.make_async_copy(held_ref.at[k], out, sem.at[base + k]) for k, out in enumerate(outs)])


def spin(value, cos, sin):
    a, b = value[: HD // 2], value[HD // 2 :]
    return jnp.concatenate([a * cos - b * sin, b * cos + a * sin], axis=0)


def attn_fwd_kernel(
    where_ref, p0, p1, p2, p3, wa0, wa1, wb0, wb1, cos_in, sin_in,
    o0, o2, o13, rows_out, q_out, k_out, v_out, ctx_out, lse_out,
    raw_ref, wa_ref, wb_ref, cos_ref, sin_ref, rows_ref, q_ref, k_ref, v_ref, ctx_ref, lse_ref,
    knat_ref, held_ref, sem, out_sem, *, seq, outer, picks,
):
    me = where_ref[0]
    length = where_ref[1 + seq]
    outs = (o0, o13.at[0], o2, o13.at[1])
    block = rows_ref.shape[1]
    heads = lse_ref.shape[0]
    width = heads * HD
    count = lax.div(length + block - 1, block)
    copies = fetch_halves(wa0, wa1, wa_ref, outer[0], sem, 4)
    copies += fetch((cos_in, sin_in), lambda p: (cos_ref, sin_ref)[p], sem, 12)
    fetch(picked((p0, p1, p2, p3), picks), lambda p: raw_ref.at[me ^ p], sem)
    copies += fetch_halves(wb0, wb1, wb_ref, outer[1], sem, 8)
    finish(copies)

    def project(i, carry):
        await_slot(raw_ref.at[i], sem.at[me ^ i])
        raw = raw_ref[i].astype(F32)
        raw = raw - jnp.mean(raw, axis=-1, keepdims=True)
        scale = lax.rsqrt(jnp.mean(raw * raw, axis=-1, keepdims=True) + norm_eps)
        rows = (raw * scale * wa_ref[2 * width : 2 * width + 1].astype(F32)).astype(BF)
        rows_ref[i] = rows
        start(rows_ref.at[i], rows_out.at[i], out_sem.at[4 + i])
        spot = aligned(i, block)
        cos = cos_ref[:, spot]
        sin = sin_ref[:, spot]
        query = nt(wa_ref[:width], rows)
        key = nt(wa_ref[width : 2 * width], rows)
        for h in range(heads):
            hs = slice(h * HD, (h + 1) * HD)
            q_ref[hs, spot] = spin(query[hs], cos, sin).astype(BF)
            turned = spin(key[hs], cos, sin)
            k_ref[hs, spot] = turned.astype(BF)
            knat_ref[h, spot, :] = turned.T.astype(BF)
        v_ref[:, spot] = nt(wb_ref[:width], rows).astype(BF)
        return carry

    lax.fori_loop(0, count, project, 0)
    saves = [(q_ref, q_out), (k_ref, k_out), (v_ref, v_out)]
    saves = [start(ref, out, out_sem.at[8 + i]) for i, (ref, out) in enumerate(saves)]

    for n in range(1, 5):

        @pl.when(count == n)
        def _(n=n):
            last = lax.broadcasted_iota(jnp.int32, (block, block), 0) + (n - 1) * block < length

            def rows_of(i, carry):
                spot = aligned(i, block)
                for h in range(heads):
                    hs = slice(h * HD, (h + 1) * HD)
                    query = q_ref[hs, spot]
                    tiles = []
                    for j in range(n):
                        tile = nn(knat_ref[h, j * block : (j + 1) * block, :], query) * (SCALE * LOG2E)
                        if j == n - 1:
                            tile = jnp.where(last, tile, -1e30)
                        tiles.append(tile)
                    top = jnp.max(functools.reduce(jnp.maximum, tiles), axis=0, keepdims=True)
                    total = jnp.zeros((1, block), F32)
                    found = jnp.zeros((HD, block), F32)
                    for j, tile in enumerate(tiles):
                        weight = jnp.exp2(tile - top)
                        total = total + jnp.sum(weight, axis=0, keepdims=True)
                        found = found + nn(v_ref[hs, j * block : (j + 1) * block], weight.astype(BF))
                    ctx_ref[hs, spot] = (found / total).astype(BF)
                    lse_ref[h, :, spot] = top + jnp.log2(total)
                out = me ^ i
                held_ref[out] = nn(ctx_ref[:, spot].T, wb_ref[width:]).astype(BF)
                send_block(out, held_ref, outs, out_sem)
                return carry

            lax.fori_loop(0, n, rows_of, 0)

    saves += [start(ref, out, out_sem.at[11 + i]) for i, (ref, out) in enumerate([(ctx_ref, ctx_out), (lse_ref, lse_out)])]

    def blank(i, carry):
        await_slot(raw_ref.at[i], sem.at[me ^ i])
        out = me ^ i
        held_ref[out] = jnp.zeros(held_ref.shape[1:], BF)
        send_block(out, held_ref, outs, out_sem)
        rows_ref[i] = held_ref[out]
        start(rows_ref.at[i], rows_out.at[i], out_sem.at[4 + i])
        return carry

    lax.fori_loop(count, 4, blank, 0)
    finish(saves)
    sent_blocks(rows_ref, [rows_out.at[i] for i in range(4)], out_sem, 4)
    sent_blocks(held_ref, outs, out_sem)


def put_halves(keep_ref, send_ref, rows, value, order):
    size = value.shape[-1] // 8
    for side, ref in enumerate((keep_ref, send_ref)):
        for i in range(4):
            offset = side * order[0] + i // 2 * order[1] + i % 2 * order[2]
            place = EIGHTHS.index(offset)
            ref[rows, i * size : (i + 1) * size] = value[:, place * size : (place + 1) * size].astype(BF)


def attn_bwd_kernel(
    where_ref, p0, p1, p2, p3, wa0, wa1, wb0, wb1, rows_in, q_in, k_in, v_in, ctx_in, lse_in,
    cos_in, sin_in, *rest, seq, old, orders, outer_w,
):
    if old:
        old_in, oldgain_ref, *rest = rest
    (o0, o2, o13), rest = rest[:3], rest[3:]
    outs = (o0, o13.at[0], o2, o13.at[1])
    if old:
        g_outs, g_refs, gain_ref, rest = rest[:4], rest[4:8], rest[8], rest[9:]
    else:
        grad_out, gain_ref, *rest = rest
    (
        grad_ref, wa_ref, wb_ref, rows_ref, q_ref, k_ref, v_ref, ctx_ref, lse_ref, cos_ref, sin_ref,
        back_ref, cb_ref, knat_ref, vnat_ref, d_ref, dk_ref, dv_ref, delta_ref, held_ref, sem, out_sem,
    ) = rest
    me = where_ref[0]
    length = where_ref[1 + seq]
    block = rows_ref.shape[1]
    heads = lse_ref.shape[0]
    width = heads * HD
    count = lax.div(length + block - 1, block)
    early = fetch_halves(wb0, wb1, wb_ref, outer_w[1], sem, 8)
    fetch((p0, p1, p2, p3), lambda p: back_ref.at[me ^ p], sem)
    saved = (ctx_in, k_in, v_in, q_in, lse_in, cos_in, sin_in)
    places = (ctx_ref, k_ref, v_ref, q_ref, lse_ref, cos_ref, sin_ref)
    early += fetch(saved, lambda p: places[p], sem, 12)
    late = fetch((rows_in,), lambda p: rows_ref, sem, 19)
    late += fetch_halves(wa0, wa1, wa_ref, outer_w[0], sem, 4)
    if old:
        late += fetch((old_in,), lambda p: grad_ref, sem, 20)
        gain_ref[...] = oldgain_ref[...]
    else:
        gain_ref[...] = jnp.zeros(gain_ref.shape, F32)
    dk_ref[...] = jnp.zeros(dk_ref.shape, F32)
    dv_ref[...] = jnp.zeros(dv_ref.shape, F32)
    finish(early)

    def prepare(i, carry):
        await_slot(back_ref.at[i], sem.at[me ^ i])
        spot = aligned(i, block)
        low = nt(wb_ref[width:], back_ref[i]).astype(BF)
        cb_ref[:, spot] = low
        inner = low.astype(F32) * ctx_ref[:, spot].astype(F32)
        for h in range(heads):
            hs = slice(h * HD, (h + 1) * HD)
            delta_ref[h, :, spot] = jnp.sum(inner[hs], axis=0, keepdims=True)
            knat_ref[h, spot, :] = k_ref[hs, spot].T
            vnat_ref[h, spot, :] = v_ref[hs, spot].T
        return carry

    lax.fori_loop(0, count, prepare, 0)

    def unspin(value, spot):
        return spin(value * SCALE, cos_ref[:, spot], -sin_ref[:, spot]).astype(BF)

    for n in range(1, 5):

        @pl.when(count == n)
        def _(n=n):
            last = lax.broadcasted_iota(jnp.int32, (block, block), 0) + (n - 1) * block < length

            def rows_of(i, carry):
                spot = aligned(i, block)
                for h in range(heads):
                    hs = slice(h * HD, (h + 1) * HD)
                    query = q_ref[hs, spot]
                    cb = cb_ref[hs, spot]
                    lse = lse_ref[h, :, spot]
                    delta = delta_ref[h, :, spot]
                    dq = jnp.zeros((HD, block), F32)
                    for j in range(n):
                        js = slice(j * block, (j + 1) * block)
                        tile = nn(knat_ref[h, js, :], query) * (SCALE * LOG2E) - lse
                        if j == n - 1:
                            tile = jnp.where(last, tile, -1e30)
                        weight = jnp.exp2(tile)
                        back = nn(vnat_ref[h, js, :], cb)
                        ds = (weight * (back - delta)).astype(BF)
                        dv_ref[hs, js] += nt(cb, weight.astype(BF))
                        dk_ref[hs, js] += nt(query, ds)
                        dq = dq + nn(k_ref[hs, js], ds)
                    d_ref[hs, spot] = unspin(dq, spot)
                return carry

            lax.fori_loop(0, n, rows_of, 0)
            for i in range(n):
                spot = slice(i * block, (i + 1) * block)
                for h in range(heads):
                    hs = slice(h * HD, (h + 1) * HD)
                    d_ref[width + h * HD : width + (h + 1) * HD, spot] = unspin(dk_ref[hs, spot], spot)
                d_ref[2 * width :, spot] = dv_ref[:, spot].astype(BF)
            finish(late)
            full = slice(0, n * block)
            rows = rows_ref[:n].reshape(n * block, -1)
            back = back_ref[:n].reshape(n * block, -1)
            pieces = [(k, d_ref[k * width : (k + 1) * width, full], rows) for k in range(3)]
            pieces.append((3, ctx_ref[:, full], back))
            for k, left, right in pieces:
                at = slice(k * width, (k + 1) * width)
                value = nn(left, right)
                if old:
                    pair = g_refs[k // 2 * 2 : k // 2 * 2 + 2]
                    put_halves(*pair, slice(k % 2 * width, (k % 2 + 1) * width), grad_ref[at] + value, orders[k // 2])
                else:
                    grad_ref[at] = value

    saves = []
    if not old:
        saves = [start(grad_ref, grad_out, out_sem.at[4])]
    else:
        saves = [start(ref, out, out_sem.at[4 + i]) for i, (ref, out) in enumerate(zip(g_refs[:2], g_outs[:2]))]

    def close(i, carry):
        turned = d_ref[:, aligned(i, block)].T
        out = nn(turned[:, : 2 * width], wa_ref[: 2 * width]) + nn(turned[:, 2 * width :], wb_ref[:width])
        held_ref[me ^ i] = out.astype(BF)
        send_block(me ^ i, held_ref, outs, out_sem)
        gain_ref[:1] += jnp.sum(out * rows_ref[i].astype(F32), axis=0, keepdims=True)
        return carry

    lax.fori_loop(0, count, close, 0)

    def blank(i, carry):
        await_slot(back_ref.at[i], sem.at[me ^ i])
        held_ref[me ^ i] = jnp.zeros(held_ref.shape[1:], BF)
        send_block(me ^ i, held_ref, outs, out_sem)
        return carry

    lax.fori_loop(count, 4, blank, 0)
    if old:
        put_halves(g_refs[2], g_refs[3], slice(2 * width, None), gain_ref[...], orders[1])
        saves += [start(ref, out, out_sem.at[6 + i]) for i, (ref, out) in enumerate(zip(g_refs[2:], g_outs[2:]))]
    finish(saves)
    sent_blocks(held_ref, outs, out_sem)


def ffn_kernel(
    where_ref, a0, a1, a2, a3, b0, b1, b2, b3, wu0, wu1, wg0, wg1, wo0, wo1,
    f0, f2, f13, n0, n2, n13, ub_out, gb_out, mixed_out, gain_ref,
    rows_ref, back_ref, fheld_ref, nheld_ref, ub_ref, gb_ref, mixed_ref, wu_ref, wg_ref, wo_ref, sem, out_sem,
    *, seq, outer, picks,
):
    me = where_ref[0]
    length = where_ref[1 + seq]
    block = rows_ref.shape[1]
    fouts = (f0, f13.at[0], f2, f13.at[1])
    nouts = (n0, n13.at[0], n2, n13.at[1])
    copies = fetch_halves(wu0, wu1, wu_ref, outer[0], sem, 8)
    aparts, bparts = picked((a0, a1, a2, a3), picks[:4]), picked((b0, b1, b2, b3), picks[4:])
    start(aparts[0], rows_ref.at[0], sem.at[0])
    copies += fetch_halves(wg0, wg1, wg_ref, outer[1], sem, 12)
    start(bparts[0], back_ref.at[0], sem.at[4])
    copies += fetch_halves(wo0, wo1, wo_ref, outer[2], sem, 16)
    for p in range(1, 4):
        start(aparts[p], rows_ref.at[p], sem.at[p])
        start(bparts[p], back_ref.at[p], sem.at[4 + p])
    gain_ref[...] = jnp.zeros(gain_ref.shape, F32)
    finish(copies)
    kept = ((ub_ref, ub_out), (gb_ref, gb_out), (mixed_ref, mixed_out))

    def step(p, carry):
        valid = (me ^ p) * block < length
        await_slot(rows_ref.at[p], sem.at[p])
        await_slot(back_ref.at[p], sem.at[4 + p])

        @pl.when(valid)
        def _():
            rows = rows_ref[p]
            up = nt(rows, wu_ref[...])
            gate = nt(rows, wg_ref[...])
            mb = nt(back_ref[p], wo_ref[...])
            phi = 0.5 + 0.5 * lax.erf(up * (0.5**0.5))
            act = up * phi
            mixed = (act * gate).astype(BF)
            mixed_ref[p] = mixed
            slope = phi + up * (jnp.exp(-0.5 * up * up) * (0.5 / np.pi) ** 0.5)
            ub = (mb * gate * slope).astype(BF)
            gb = (mb * act).astype(BF)
            ub_ref[p] = ub
            gb_ref[p] = gb
            out = nn(ub, wu_ref[...]) + nn(gb, wg_ref[...])
            nheld_ref[p] = out.astype(BF)
            gain_ref[1:2] += jnp.sum(out * rows.astype(F32), axis=0, keepdims=True)
            fheld_ref[p] = nn(mixed, wo_ref[...]).astype(BF)

        @pl.when(jnp.logical_not(valid))
        def _():
            for ref in (mixed_ref, ub_ref, gb_ref, nheld_ref, fheld_ref):
                ref[p] = jnp.zeros(ref.shape[1:], BF)

        send_block(p, nheld_ref, nouts, out_sem, 4)
        send_block(p, fheld_ref, fouts, out_sem)
        for k, (ref, out) in enumerate(kept):
            start(ref.at[p], out.at[p], out_sem.at[8 + 4 * k + p])
        return carry

    lax.fori_loop(0, 4, step, 0)
    sent_blocks(nheld_ref, nouts, out_sem, 4)
    sent_blocks(fheld_ref, fouts, out_sem)
    for k, (ref, out) in enumerate(kept):
        sent_blocks(ref, [out.at[p] for p in range(4)], out_sem, 8 + 4 * k)


def ffn_grad_kernel(_, *refs, orders, picks):
    parts, saved, refs = picked(refs[:16], picks), refs[16:22], refs[22:]
    outs, (rows_ref, back_ref, saved_ref, *held), refs = refs[:4], refs[4:11], refs[11:]
    g_ref, sem, out_sem = refs
    units = g_ref.shape[1]
    copies = []
    for s in range(2):
        rows = fetch(parts[8 * s : 8 * s + 4], lambda p: rows_ref.at[s, p], sem, 8 * s)
        backs = lambda: fetch(parts[8 * s + 4 : 8 * s + 8], lambda p: back_ref.at[s, p], sem, 8 * s + 4)
        kept = lambda k: fetch((saved[3 * s + k],), lambda p: saved_ref.at[s, k], sem, 16 + 3 * s + k)
        copies += [rows + kept(0), kept(1), kept(2) + backs()]
    sent = []
    for s in range(2):
        rows = rows_ref.at[s]
        for k in range(3):
            finish(copies[3 * s + k])
            other = (back_ref if k == 2 else rows_ref)[s].reshape(-1, rows_ref.shape[-1])
            part = tn(saved_ref[s, k].reshape(-1, units), other)
            if s == 0:
                g_ref[k] = part
                continue
            pair = held[k // 2 * 2 : k // 2 * 2 + 2]
            at = slice(None) if k == 2 else slice(k * units, (k + 1) * units)
            put_halves(*pair, at, g_ref[k] + part, orders[k // 2])
            if k > 0:
                sent += [start(ref, out, out_sem.at[k // 2 * 2 + i]) for i, (ref, out) in enumerate(zip(pair, outs[k // 2 * 2 :][:2]))]
    finish(sent)


SMEM = pl.BlockSpec(memory_space=pltpu.SMEM)
VMEM = pl.BlockSpec(memory_space=pltpu.VMEM)
HBM = pl.BlockSpec(memory_space=pl.ANY)
LIMIT = 60 * 1024 * 1024
PARAMS = pltpu.CompilerParams(vmem_limit_bytes=LIMIT)
GAIN_ROWS = 16


def shape(*dims, kind=BF):
    return jax.ShapeDtypeStruct(dims, kind)


def idle(where):
    return pl.pallas_call(
        lambda in_ref, out_ref: None,
        out_shape=jax.ShapeDtypeStruct(where.shape, where.dtype),
        in_specs=[pl.BlockSpec(memory_space=pl.ANY)],
        out_specs=pl.BlockSpec(memory_space=pl.ANY),
        input_output_aliases={0: 0},
        cost_estimate=pl.CostEstimate(flops=1 << 34, bytes_accessed=1 << 20, transcendentals=0),
        name="idle",
    )(where)


def partials(block, width):
    return (shape(block, width), shape(block, width), shape(2, block, width))


def vmem(array):
    return pltpu.VMEM(array.shape, array.dtype)


def attn_fwd(where, seq, parts, wa, wb, cos, sin):
    arrays, picks = zip(*parts)
    block, width = arrays[0].shape[-2:]
    rows = wb.halves[0].shape[0]
    cols = rows // 2
    heads = cols // HD
    full = 4 * block
    flops = 2 * full * width * cols * 4 + 4 * full * full * cols
    saved = (shape(4, block, width),) + (shape(cols, full),) * 4 + (shape(heads, 1, full, kind=F32),)
    return pl.pallas_call(
        functools.partial(attn_fwd_kernel, seq=seq, outer=(wa.outer, wb.outer), picks=picks),
        out_shape=partials(block, width) + saved,
        in_specs=[SMEM] + [HBM] * 10,
        out_specs=(HBM,) * 9,
        scratch_shapes=[
            pltpu.VMEM((4, block, width), BF),
            pltpu.VMEM(wa.halves[0].shape[:1] + (width,), BF),
            pltpu.VMEM((rows, width), BF),
            vmem(cos),
            vmem(sin),
            *[vmem(array) for array in saved],
            pltpu.VMEM((heads, full, HD), BF),
            pltpu.VMEM((4, block, width), BF),
            pltpu.SemaphoreType.DMA((14,)),
            pltpu.SemaphoreType.DMA((13,)),
        ],
        compiler_params=pltpu.CompilerParams(vmem_limit_bytes=58 << 20),
        cost_estimate=pl.CostEstimate(flops=flops * 3, bytes_accessed=12 << 20, transcendentals=heads * full * full),
        name="attn_fwd",
    )(where, *arrays, *wa.halves, *wb.halves, cos, sin)


def attn_bwd(where, seq, parts, saved, wa, wb, cos, sin, old, orders):
    arrays = [array for array, _ in parts]
    block, width = arrays[0].shape
    rows = wb.halves[0].shape[0]
    cols = rows // 2
    heads = cols // HD
    full = 4 * block
    flops = 4 * full * width * cols * 4 + 10 * full * full * cols
    extra = [] if old is None else list(old)
    grads = shape(4 * cols, width, kind=F32)
    gain = shape(GAIN_ROWS, width, kind=F32)
    halved = (shape(rows, width // 2),) * 2 + (shape(rows + GAIN_ROWS, width // 2),) * 2
    outs = (grads,) if old is None else halved
    return pl.pallas_call(
        functools.partial(
            attn_bwd_kernel,
            seq=seq,
            old=old is not None,
            orders=orders,
            outer_w=(wa.outer, wb.outer),
        ),
        out_shape=partials(block, width) + outs + (() if extra else (gain,)),
        in_specs=[SMEM] + [HBM] * 16 + ([] if old is None else [HBM, VMEM]),
        out_specs=(HBM,) * (3 + len(outs)) + (() if extra else (VMEM,)),
        scratch_shapes=[vmem(array) for array in ((grads,) if old is None else halved + (gain, grads))] + [
            pltpu.VMEM(wa.halves[0].shape[:1] + (width,), BF),
            pltpu.VMEM((rows, width), BF),
            *[vmem(array) for array in saved],
            vmem(cos),
            vmem(sin),
            pltpu.VMEM((4, block, width), BF),
            pltpu.VMEM((cols, full), BF),
            pltpu.VMEM((heads, full, HD), BF),
            pltpu.VMEM((heads, full, HD), BF),
            pltpu.VMEM((3 * cols, full), BF),
            pltpu.VMEM((cols, full), F32),
            pltpu.VMEM((cols, full), F32),
            pltpu.VMEM((heads, 1, full), F32),
            pltpu.VMEM((4, block, width), BF),
            pltpu.SemaphoreType.DMA((21,)),
            pltpu.SemaphoreType.DMA((8,)),
        ],
        compiler_params=pltpu.CompilerParams(vmem_limit_bytes=32 << 20),
        cost_estimate=pl.CostEstimate(flops=flops * 3, bytes_accessed=16 << 20, transcendentals=heads * full * full),
        name="attn_bwd",
    )(where, *arrays, *wa.halves, *wb.halves, *saved, cos, sin, *extra)


def ffn(where, seq, parts, backs, weights):
    arrays, picks = zip(*parts, *backs)
    block, width = arrays[0].shape[-2:]
    units = weights[0].halves[0].shape[0]
    flops = 2 * 4 * block * width * units * 6
    saved = (shape(4, block, units),) * 3
    return pl.pallas_call(
        functools.partial(ffn_kernel, seq=seq, outer=[w.outer for w in weights], picks=picks),
        out_shape=partials(block, width) * 2 + saved + (shape(GAIN_ROWS, width, kind=F32),),
        in_specs=[SMEM] + [HBM] * 14,
        out_specs=(HBM,) * 9 + (VMEM,),
        scratch_shapes=[pltpu.VMEM((4, block, width), BF)] * 4
        + [vmem(array) for array in saved]
        + [pltpu.VMEM((units, width), BF)] * 3
        + [pltpu.SemaphoreType.DMA((20,)), pltpu.SemaphoreType.DMA((20,))],
        compiler_params=pltpu.CompilerParams(vmem_limit_bytes=58 << 20),
        cost_estimate=pl.CostEstimate(flops=flops, bytes_accessed=20 << 20, transcendentals=2 * 4 * block * units),
        name="ffn",
    )(where, *arrays, *[half for w in weights for half in w.halves])


def ffn_grad(where, parts, saved, orders):
    arrays, picks = zip(*parts)
    block, width = arrays[0].shape[-2:]
    units = saved[0].shape[2]
    outs = (shape(2 * units, width // 2),) * 2 + (shape(units, width // 2),) * 2
    return pl.pallas_call(
        functools.partial(ffn_grad_kernel, orders=orders, picks=picks),
        out_shape=outs,
        in_specs=[SMEM] + [HBM] * 22,
        out_specs=(HBM,) * 4,
        scratch_shapes=[pltpu.VMEM((2, 4, block, width), BF)] * 2
        + [pltpu.VMEM((2, 3) + saved[0].shape, BF)]
        + [vmem(array) for array in outs]
        + [pltpu.VMEM((3, units, width), F32), pltpu.SemaphoreType.DMA((22,)), pltpu.SemaphoreType.DMA((4,))],
        compiler_params=pltpu.CompilerParams(vmem_limit_bytes=40 << 20),
        cost_estimate=pl.CostEstimate(flops=2 * 8 * block * width * units * 3, bytes_accessed=24 << 20, transcendentals=0),
        name="ffn_grad",
    )(where, *arrays, *saved)


def norm_parts(values):
    average = jnp.mean(values, axis=-1, keepdims=True)
    centred = values - average
    spread = jnp.mean(centred * centred, axis=-1, keepdims=True)
    scale = lax.rsqrt(spread + norm_eps)
    return centred * scale, scale


def norm_back(grad, gain, normed, scale):
    y = grad * gain
    return scale * (
        y - jnp.mean(y, axis=-1, keepdims=True) - normed * jnp.mean(y * normed, axis=-1, keepdims=True)
    )


def rope_tables(length):
    places = np.arange(length, dtype=np.float32)
    frequency = (rope_base ** (-np.arange(0, HD, 2, dtype=np.float32) / HD)).astype(np.float32)
    angles = (frequency[:, None] * places[None, :]).astype(np.float32)
    return jnp.asarray(np.cos(angles)), jnp.asarray(np.sin(angles))


def per_device(
    tokens, lengths, attn_norm, qkv_weight, attn_out_weight, ffn_norm, ffn_in_weight, ffn_out_weight, out_grad
):
    seqs, local_len, width = tokens.shape
    assert lax.axis_size("mp") == 4 and seqs == 2
    groups = lax.axis_size("dp")
    me = lax.axis_index("mp")
    full_len = 4 * local_len
    cols = qkv_weight.shape[2]
    units = ffn_in_weight.shape[2]
    span = width // groups
    cos, sin = rope_tables(full_len)

    ranks = rank_order(groups)
    order = jnp.asarray(np.array(ranks, np.int32)) ^ lax.axis_index("dp")
    source = (order[:, None] * span + jnp.arange(span, dtype=jnp.int32)[None, :]).reshape(width)
    reorder = (source[None, :] == jnp.arange(width, dtype=jnp.int32)[:, None]).astype(BF)

    def to_own(rows):
        return jnp.dot(rows.reshape(-1, width), reorder, preferred_element_type=F32).astype(BF).reshape(rows.shape)

    def from_own(rows):
        return lax.dot_general(
            rows, reorder, (((1,), (1,)), ((), ())), preferred_element_type=F32
        ).astype(BF)

    far, near = gather_order(4, 2, 1), gather_order(1, 4, 2)
    qkv = jnp.swapaxes(qkv_weight, 1, 2)
    ffn_in = jnp.swapaxes(ffn_in_weight, 1, 2)
    own_gains = jnp.stack([attn_norm, ffn_norm])
    own_gains = jnp.pad(own_gains, ((0, 14), (0, 0)))
    wa = Gather(jnp.concatenate([qkv[:2].reshape(2 * cols, span), own_gains], axis=0), far, "w_qk")
    wb = Gather(jnp.concatenate([qkv[2], attn_out_weight], axis=0), near, "w_vo")
    w_up = Gather(ffn_in[0], far, "w_up")
    w_gate = Gather(ffn_in[1], far, "w_gate")
    w_out = Gather(ffn_out_weight, near, "w_out")

    local = me * local_len + jnp.arange(local_len, dtype=jnp.int32)
    where = jnp.concatenate([me[None], lengths]).astype(jnp.int32)
    valid = [(local < lengths[s]).astype(F32)[:, None] for s in range(seqs)]
    token_low = [to_own(tokens[s]) for s in range(seqs)]
    token = [SeqRows(token_low[s], f"token{s}") for s in range(seqs)]

    _, (where, token[1].across.value, out_grad, w_out.value) = stage(
        [wa, w_up, token[0].across, wb, token[0].beside],
        None,
        where, token[1].across.value, out_grad, w_out.value,
    )

    def prepare():
        return *[(valid[s] * to_own(out_grad[s]).astype(F32)).astype(BF) for s in range(seqs)], idle(where)

    (*back_low, where), (token_low,) = stage(
        [wb, token[1].across, wa, w_out, token[0].diag()], prepare, token_low
    )
    outback = [SeqRows(back_low[s], f"outback{s}") for s in range(seqs)]
    _, (where, w_gate.value) = stage(
        [wb, wa, outback[0].across, token[1].beside, token[1].diag()], None, where, w_gate.value
    )
    ffn_gain = join([half[2 * cols + 1 : 2 * cols + 2] for half in wa.halves]).astype(F32)
    attn_gain = join([half[2 * cols : 2 * cols + 1] for half in wa.halves]).astype(F32)

    done, (where,) = stage(
        [outback[1].across, w_up, w_gate, outback[0].beside, outback[1].beside],
        lambda: attn_fwd(where, 0, token[0].parts(), wa, wb, cos, sin),
        where,
    )
    attn = [Sums(*done[:3], "attn0")]
    saved = [done[3:]]
    stage_turn = lambda sums, *others: stage([sums.turn, *others], lambda: (), where)
    _, (where,) = stage_turn(attn[0], outback[0].diag())
    done, (where,) = stage(
        [attn[0].away(), w_up, w_gate, w_out, outback[1].diag()],
        lambda: attn_fwd(where, 1, token[1].parts(), wa, wb, cos, sin),
        where,
    )
    attn.append(Sums(*done[:3], "attn1"))
    saved.append(done[3:])

    def second_norm(s):
        rows = token_low[s].astype(F32) + attn[s].total()
        normed, scale = norm_parts(rows)
        return rows, normed, scale, (normed * ffn_gain).astype(BF)

    hidden, second, two = [None, None], [None, None], [None, None]

    (done,), (where,) = stage([attn[1].turn], lambda: (second_norm(0),), where)
    hidden[0], second[0] = done[0], done[1:3]
    two[0] = SeqRows(done[3], "two0")
    _, (where,) = stage([two[0].across, attn[1].away(), w_out, w_gate, two[0].beside], None, where)
    (done,), (where,) = stage([two[0].diag()], lambda: (second_norm(1),), where)
    hidden[1], second[1] = done[0], done[1:3]
    two[1] = SeqRows(done[3], "two1")
    weights = (w_up, w_gate, w_out)
    done, (where,) = stage(
        [two[1].across, two[1].beside],
        lambda: ffn(where, 0, two[0].parts(), outback[0].parts(), weights),
        where,
    )
    ff, twoback = [Sums(*done[:3], "ff0")], [Sums(*done[3:6], "twoback0")]
    ffn_saved, ffn_gains = list(done[6:9]), done[9]
    _, (where,) = stage_turn(twoback[0], two[1].diag())
    done, (where,) = stage(
        [twoback[0].away(), ff[0].turn],
        lambda: ffn(where, 1, two[1].parts(), outback[1].parts(), weights),
        where,
    )
    ff.append(Sums(*done[:3], "ff1"))
    twoback.append(Sums(*done[3:6], "twoback1"))
    ffn_saved += done[6:9]
    ffn_gains = ffn_gains + done[9]

    def second_back(s):
        rows = back_low[s].astype(F32) + norm_back(twoback[s].total(), ffn_gain, *second[s])
        return rows, rows.astype(BF)

    hidden_back, hidback = [None, None], [None, None]
    (done,), (where,) = stage([twoback[1].turn], lambda: (second_back(0),), where)
    hidden_back[0] = done[0]
    hidback[0] = SeqRows(done[1], "hidback0")
    orders = (scatter_order(2, 4, 1), scatter_order(1, 2, 4))

    def weight_grads():
        grads = ffn_grad(
            where, [p for s in range(seqs) for p in two[s].parts() + outback[s].parts()], ffn_saved, orders
        )
        return grads


    def weight_grads():
        parts = [p for s in range(seqs) for p in two[s].parts() + outback[s].parts()]
        grads = ffn_grad(where, parts, ffn_saved, orders)
        turned = exchange(ff[1].turn.value, "mp", 1, ff[1].turn.name)
        terms = (ff[0].far, ff[0].turn.got, ff[1].far, turned)
        terms = lax.optimization_barrier((terms, grads[0]))[0]
        sums = [(terms[k].astype(F32) + terms[k + 1][1].astype(F32)).astype(BF) for k in (0, 2)]
        return *grads, turned, *sums

    done, (where,) = stage(
        [twoback[1].away(), hidback[0].across, hidback[0].beside], weight_grads, where
    )
    *done, ff[1].turn.got, away0, away1 = done
    ff[0].last, ff[1].last = (Move(a, "mp", 2, f"ff{s}") for s, a in enumerate((away0, away1)))
    g_in = Scatter(*done[:2], orders[0], "g_in")
    g_out = Scatter(*done[2:4], orders[1], "g_out")
    (done,), (where,) = stage([hidback[0].diag()], lambda: (second_back(1),), where)
    hidden_back[1] = done[0]
    hidback[1] = SeqRows(done[1], "hidback1")

    orders = (scatter_order(1, 2, 4), scatter_order(2, 4, 1))
    done, (where,) = stage(
        [g_in, g_out, hidback[1].across, ff[0].last, hidback[1].beside],
        lambda: attn_bwd(where, 0, hidback[0].parts(), saved[0], wa, wb, cos, sin, None, orders),
        where,
    )
    oneback = [Sums(*done[:3], "oneback0")]
    sums = [done[3], done[4] + ffn_gains]
    _, (where,) = stage_turn(oneback[0], hidback[1].diag())
    done, (where, token_low) = stage(
        [g_in, oneback[0].away(), ff[1].last, g_out],
        lambda: attn_bwd(where, 1, hidback[1].parts(), saved[1], wa, wb, cos, sin, sums, orders),
        where, token_low,
    )
    oneback.append(Sums(*done[:3], "oneback1"))
    g_qk = Scatter(*done[3:5], orders[0], "g_qk")
    g_vo = Scatter(*done[5:7], orders[1], "g_vo")
    def close(s):
        return (hidden_back[s] + norm_back(oneback[s].total(), attn_gain, *norm_parts(token_low[s].astype(F32)))).astype(BF)

    def ready():
        rows = [(valid[s] * (hidden[s] + ff[s].total())).astype(BF) for s in range(seqs)]
        return from_own(jnp.concatenate(rows, axis=0)), close(0)

    (output, input_grad), (where,) = stage([g_vo, g_qk, g_out, oneback[1].turn], ready, where)
    _, (where,) = stage([g_vo, oneback[1].away(), g_qk, g_in], None, where)
    stage([g_vo, g_qk], None, where)
    grad_qk, grad_vo = g_qk.end(), g_vo.end()
    gain_back = grad_vo[2 * cols : 2 * cols + 2]
    ones, twos, threes = (exchange(gain_back, "mp", k, "gain") for k in (1, 2, 3))
    gain_back = (gain_back + ones) + (twos + threes)
    input_grad = from_own(jnp.concatenate([input_grad, close(1)], axis=0))
    grad_qkv = jnp.concatenate([grad_qk, grad_vo[:cols]], axis=0).reshape(3, cols, span)
    return (
        output.reshape(seqs, local_len, width),
        input_grad.reshape(seqs, local_len, width),
        gain_back[0] / attn_norm.astype(F32),
        jnp.swapaxes(grad_qkv, 1, 2),
        grad_vo[cols : 2 * cols],
        gain_back[1] / ffn_norm.astype(F32),
        jnp.swapaxes(g_in.end().reshape(2, units, span), 1, 2),
        g_out.end(),
    )


def solution(mesh):
    in_specs = (
        P("dp", "mp", None),
        P("dp"),
        P("dp"),
        P(None, "dp", "mp"),
        P("mp", "dp"),
        P("dp"),
        P(None, "dp", "mp"),
        P("mp", "dp"),
        P("dp", "mp", None),
    )
    out_specs = (
        P("dp", "mp", None),
        P("dp", "mp", None),
        P("dp"),
        P(None, "dp", "mp"),
        P("mp", "dp"),
        P("dp"),
        P(None, "dp", "mp"),
        P("mp", "dp"),
    )
    return jax.shard_map(
        per_device, mesh=mesh, in_specs=in_specs, out_specs=out_specs, check_vma=False
    )
```

```python
import functools

import jax
import jax.numpy as jnp
import numpy as np
from jax import lax
from jax.experimental import pallas as pl
from jax.experimental.pallas import tpu as pltpu
from jax.sharding import PartitionSpec as P

HD = 64
norm_eps = 1e-05
rope_base = 160000.0
SCALE = HD ** (-0.5)
LOG2E = 1.4426950408889634
BF = jnp.bfloat16
F32 = jnp.float32


EIGHTHS = [0, 4, 2, 6, 1, 5, 3, 7]


def exchange(value, axis, bit, name):
    size = lax.axis_size(axis)
    with jax.named_scope(f"{name}_{axis}{bit}"):
        return lax.ppermute(value, axis, [(i, i ^ bit) for i in range(size)])


def bits_of(size):
    assert size & (size - 1) == 0 and size >= 8
    return [1 << i for i in reversed(range(size.bit_length() - 1))]


def rank_order(size):
    order = [0]
    for bit in bits_of(size):
        order = order + [o ^ bit for o in order]
    return order


def gather_order(*low):
    return bits_of(lax.axis_size("dp"))[:-3] + list(low)


def scatter_order(*low):
    return list(low) + bits_of(lax.axis_size("dp"))[:-3][::-1]


def cut(array, parts):
    size = array.shape[-1] // parts
    return [array[..., i * size : (i + 1) * size] for i in range(parts)]


def join(pieces):
    return pieces[0] if len(pieces) == 1 else jnp.concatenate(pieces, axis=-1)


class Move:
    def __init__(self, value, axis, bit, name):
        self.value, self.axis, self.bit, self.name = value, axis, bit, name

    def take(self, got):
        self.got = got


class Gather:
    def __init__(self, shard, order, name):
        self.value, self.order, self.name, self.axis = shard, list(order), name, "dp"
        self.held = []
        while len(self.order) > 3:
            self.take(exchange(self.value, "dp", self.bit, self.name))

    @property
    def bit(self):
        return self.order[0]

    def take(self, got):
        bit = self.order.pop(0)
        outer = 2 ** sum(1 for other in self.held if other < bit)
        self.held.append(bit)
        if self.order:
            pairs = zip(cut(self.value, outer), cut(got, outer))
            self.value = join([piece for pair in pairs for piece in pair])
        else:
            self.outer = outer
            self.halves = (self.value, got)


class Scatter:
    def __init__(self, keep, send, order, name):
        self.keep, self.value, self.left, self.name, self.axis = keep, send, list(order), name, "dp"

    @property
    def bit(self):
        return self.left[0]

    def take(self, got):
        self.left.pop(0)
        if self.left:
            half = got.shape[-1] // 2
            sides = [(a[..., :half], a[..., half:]) for a in (self.keep, got)]
            self.keep, self.value = ((a.astype(F32) + b.astype(F32)).astype(BF) for a, b in zip(*sides))
        else:
            self.total = self.keep.astype(F32) + got.astype(F32)

    def end(self):
        while self.left:
            self.take(exchange(self.value, "dp", self.bit, self.name))
        return self.total


def stage(moves, work=None, *carry):
    got = [exchange(m.value, m.axis, m.bit, m.name) for m in moves]
    if work is None:
        carry = (idle(carry[0]), *carry[1:])
        done = ()
    else:
        done = work()
    got, done, carry = lax.optimization_barrier((got, tuple(done), carry))
    for m, g in zip(moves, got):
        m.take(g)
    return done, carry


class SeqRows:
    def __init__(self, own, name):
        self.own, self.name = own, name
        self.beside = Move(own, "mp", 1, name)
        self.across = Move(own, "mp", 2, name)

    def diag(self):
        self.last = Move(self.across.got, "mp", 1, self.name + "_diag")
        return self.last

    def parts(self):
        return tuple((a, None) for a in (self.own, self.beside.got, self.across.got, self.last.got))


class Sums:
    def __init__(self, keep, far, turn, name):
        self.keep, self.far, self.name = keep, far, name
        self.turn = Move(turn, "mp", 1, name + "_turn")

    def away(self):
        total = self.far.astype(F32) + self.turn.got[1].astype(F32)
        self.last = Move(total.astype(BF), "mp", 2, self.name)
        return self.last

    def total(self):
        return self.keep.astype(F32) + self.turn.got[0].astype(F32) + self.last.got.astype(F32)


def nt(a, b):
    return lax.dot_general(a, b, (((1,), (1,)), ((), ())), preferred_element_type=F32)


def nn(a, b):
    return lax.dot_general(a, b, (((1,), (0,)), ((), ())), preferred_element_type=F32)


def tn(a, b):
    return lax.dot_general(a, b, (((0,), (0,)), ((), ())), preferred_element_type=F32)


def aligned(index, step):
    return pl.ds(pl.multiple_of(index * step, step), step)


def picked(refs, picks):
    return [ref if pick is None else ref.at[pick] for ref, pick in zip(refs, picks)]


def start(source, into, sem):
    copy = pltpu.make_async_copy(source, into, sem)
    copy.start()
    return copy


def fetch(parts, place, sem, base=0):
    return [start(part, place(p), sem.at[base + p]) for p, part in enumerate(parts)]


def finish(copies):
    for copy in copies:
        copy.wait()


def await_slot(ref, sem):
    pltpu.make_async_copy(ref, ref, sem).wait()


def fetch_halves(own, got, into, outer, sem, base):
    size = own.shape[-1] // outer
    return [
        start(
            (own, got)[i % 2].at[:, i // 2 * size : (i // 2 + 1) * size],
            into.at[:, i * size : (i + 1) * size],
            sem.at[base + i],
        )
        for i in range(2 * outer)
    ]


def send_block(spot, held_ref, outs, sem, base=0):
    for k, out in enumerate(outs):

        @pl.when(spot == k)
        def _(k=k, out=out):
            start(held_ref.at[k], out, sem.at[base + k])


def sent_blocks(held_ref, outs, sem, base=0):
    finish([pltpu.make_async_copy(held_ref.at[k], out, sem.at[base + k]) for k, out in enumerate(outs)])


def spin(value, cos, sin):
    a, b = value[: HD // 2], value[HD // 2 :]
    return jnp.concatenate([a * cos - b * sin, b * cos + a * sin], axis=0)


def attn_fwd_kernel(
    where_ref, p0, p1, p2, p3, wa0, wa1, wb0, wb1, cos_in, sin_in,
    o0, o2, o13, rows_out, q_out, k_out, v_out, ctx_out, lse_out,
    raw_ref, wa_ref, wb_ref, cos_ref, sin_ref, rows_ref, q_ref, k_ref, v_ref, ctx_ref, lse_ref,
    knat_ref, held_ref, sem, out_sem, *, seq, outer, picks,
):
    me = where_ref[0]
    length = where_ref[1 + seq]
    outs = (o0, o13.at[0], o2, o13.at[1])
    block = rows_ref.shape[1]
    heads = lse_ref.shape[0]
    width = heads * HD
    count = lax.div(length + block - 1, block)
    copies = fetch_halves(wa0, wa1, wa_ref, outer[0], sem, 4)
    copies += fetch((cos_in, sin_in), lambda p: (cos_ref, sin_ref)[p], sem, 12)
    fetch(picked((p0, p1, p2, p3), picks), lambda p: raw_ref.at[me ^ p], sem)
    copies += fetch_halves(wb0, wb1, wb_ref, outer[1], sem, 8)
    finish(copies)

    def project(i, carry):
        await_slot(raw_ref.at[i], sem.at[me ^ i])
        raw = raw_ref[i].astype(F32)
        raw = raw - jnp.mean(raw, axis=-1, keepdims=True)
        scale = lax.rsqrt(jnp.mean(raw * raw, axis=-1, keepdims=True) + norm_eps)
        rows = (raw * scale * wa_ref[2 * width : 2 * width + 1].astype(F32)).astype(BF)
        rows_ref[i] = rows
        start(rows_ref.at[i], rows_out.at[i], out_sem.at[4 + i])
        spot = aligned(i, block)
        cos = cos_ref[:, spot]
        sin = sin_ref[:, spot]
        query = nt(wa_ref[:width], rows)
        key = nt(wa_ref[width : 2 * width], rows)
        for h in range(heads):
            hs = slice(h * HD, (h + 1) * HD)
            q_ref[hs, spot] = spin(query[hs], cos, sin).astype(BF)
            turned = spin(key[hs], cos, sin)
            k_ref[hs, spot] = turned.astype(BF)
            knat_ref[h, spot, :] = turned.T.astype(BF)
        v_ref[:, spot] = nt(wb_ref[:width], rows).astype(BF)
        return carry

    lax.fori_loop(0, count, project, 0)
    saves = [(q_ref, q_out), (k_ref, k_out), (v_ref, v_out)]
    saves = [start(ref, out, out_sem.at[8 + i]) for i, (ref, out) in enumerate(saves)]

    for n in range(1, 5):

        @pl.when(count == n)
        def _(n=n):
            last = lax.broadcasted_iota(jnp.int32, (block, block), 0) + (n - 1) * block < length

            def rows_of(i, carry):
                spot = aligned(i, block)
                for h in range(heads):
                    hs = slice(h * HD, (h + 1) * HD)
                    query = q_ref[hs, spot]
                    tiles = []
                    for j in range(n):
                        tile = nn(knat_ref[h, j * block : (j + 1) * block, :], query) * (SCALE * LOG2E)
                        if j == n - 1:
                            tile = jnp.where(last, tile, -1e30)
                        tiles.append(tile)
                    top = jnp.max(functools.reduce(jnp.maximum, tiles), axis=0, keepdims=True)
                    total = jnp.zeros((1, block), F32)
                    found = jnp.zeros((HD, block), F32)
                    for j, tile in enumerate(tiles):
                        weight = jnp.exp2(tile - top)
                        total = total + jnp.sum(weight, axis=0, keepdims=True)
                        found = found + nn(v_ref[hs, j * block : (j + 1) * block], weight.astype(BF))
                    ctx_ref[hs, spot] = (found / total).astype(BF)
                    lse_ref[h, :, spot] = top + jnp.log2(total)
                out = me ^ i
                held_ref[out] = nn(ctx_ref[:, spot].T, wb_ref[width:]).astype(BF)
                send_block(out, held_ref, outs, out_sem)
                return carry

            lax.fori_loop(0, n, rows_of, 0)

    saves += [start(ref, out, out_sem.at[11 + i]) for i, (ref, out) in enumerate([(ctx_ref, ctx_out), (lse_ref, lse_out)])]

    def blank(i, carry):
        await_slot(raw_ref.at[i], sem.at[me ^ i])
        out = me ^ i
        held_ref[out] = jnp.zeros(held_ref.shape[1:], BF)
        send_block(out, held_ref, outs, out_sem)
        rows_ref[i] = held_ref[out]
        start(rows_ref.at[i], rows_out.at[i], out_sem.at[4 + i])
        return carry

    lax.fori_loop(count, 4, blank, 0)
    finish(saves)
    sent_blocks(rows_ref, [rows_out.at[i] for i in range(4)], out_sem, 4)
    sent_blocks(held_ref, outs, out_sem)


def put_halves(keep_ref, send_ref, rows, value, order):
    size = value.shape[-1] // 8
    for side, ref in enumerate((keep_ref, send_ref)):
        for i in range(4):
            offset = side * order[0] + i // 2 * order[1] + i % 2 * order[2]
            place = EIGHTHS.index(offset)
            ref[rows, i * size : (i + 1) * size] = value[:, place * size : (place + 1) * size].astype(BF)


def attn_bwd_kernel(
    where_ref, p0, p1, p2, p3, wa0, wa1, wb0, wb1, rows_in, q_in, k_in, v_in, ctx_in, lse_in,
    cos_in, sin_in, *rest, seq, old, orders, outer_w,
):
    if old:
        old_in, oldgain_ref, *rest = rest
    (o0, o2, o13), rest = rest[:3], rest[3:]
    outs = (o0, o13.at[0], o2, o13.at[1])
    if old:
        g_outs, g_refs, gain_ref, rest = rest[:4], rest[4:8], rest[8], rest[9:]
    else:
        grad_out, gain_ref, *rest = rest
    (
        grad_ref, wa_ref, wb_ref, rows_ref, q_ref, k_ref, v_ref, ctx_ref, lse_ref, cos_ref, sin_ref,
        back_ref, cb_ref, knat_ref, vnat_ref, d_ref, dk_ref, dv_ref, delta_ref, held_ref, sem, out_sem,
    ) = rest
    me = where_ref[0]
    length = where_ref[1 + seq]
    block = rows_ref.shape[1]
    heads = lse_ref.shape[0]
    width = heads * HD
    count = lax.div(length + block - 1, block)
    early = fetch_halves(wb0, wb1, wb_ref, outer_w[1], sem, 8)
    fetch((p0, p1, p2, p3), lambda p: back_ref.at[me ^ p], sem)
    saved = (ctx_in, k_in, v_in, q_in, lse_in, cos_in, sin_in)
    places = (ctx_ref, k_ref, v_ref, q_ref, lse_ref, cos_ref, sin_ref)
    early += fetch(saved, lambda p: places[p], sem, 12)
    late = fetch((rows_in,), lambda p: rows_ref, sem, 19)
    late += fetch_halves(wa0, wa1, wa_ref, outer_w[0], sem, 4)
    if old:
        late += fetch((old_in,), lambda p: grad_ref, sem, 20)
        gain_ref[...] = oldgain_ref[...]
    else:
        gain_ref[...] = jnp.zeros(gain_ref.shape, F32)
    dk_ref[...] = jnp.zeros(dk_ref.shape, F32)
    dv_ref[...] = jnp.zeros(dv_ref.shape, F32)
    finish(early)

    def prepare(i, carry):
        await_slot(back_ref.at[i], sem.at[me ^ i])
        spot = aligned(i, block)
        low = nt(wb_ref[width:], back_ref[i]).astype(BF)
        cb_ref[:, spot] = low
        inner = low.astype(F32) * ctx_ref[:, spot].astype(F32)
        for h in range(heads):
            hs = slice(h * HD, (h + 1) * HD)
            delta_ref[h, :, spot] = jnp.sum(inner[hs], axis=0, keepdims=True)
            knat_ref[h, spot, :] = k_ref[hs, spot].T
            vnat_ref[h, spot, :] = v_ref[hs, spot].T
        return carry

    lax.fori_loop(0, count, prepare, 0)

    def unspin(value, spot):
        return spin(value * SCALE, cos_ref[:, spot], -sin_ref[:, spot]).astype(BF)

    for n in range(1, 5):

        @pl.when(count == n)
        def _(n=n):
            last = lax.broadcasted_iota(jnp.int32, (block, block), 0) + (n - 1) * block < length

            def rows_of(i, carry):
                spot = aligned(i, block)
                for h in range(heads):
                    hs = slice(h * HD, (h + 1) * HD)
                    query = q_ref[hs, spot]
                    cb = cb_ref[hs, spot]
                    lse = lse_ref[h, :, spot]
                    delta = delta_ref[h, :, spot]
                    dq = jnp.zeros((HD, block), F32)
                    for j in range(n):
                        js = slice(j * block, (j + 1) * block)
                        tile = nn(knat_ref[h, js, :], query) * (SCALE * LOG2E) - lse
                        if j == n - 1:
                            tile = jnp.where(last, tile, -1e30)
                        weight = jnp.exp2(tile)
                        back = nn(vnat_ref[h, js, :], cb)
                        ds = (weight * (back - delta)).astype(BF)
                        dv_ref[hs, js] += nt(cb, weight.astype(BF))
                        dk_ref[hs, js] += nt(query, ds)
                        dq = dq + nn(k_ref[hs, js], ds)
                    d_ref[hs, spot] = unspin(dq, spot)
                return carry

            lax.fori_loop(0, n, rows_of, 0)
            for i in range(n):
                spot = slice(i * block, (i + 1) * block)
                for h in range(heads):
                    hs = slice(h * HD, (h + 1) * HD)
                    d_ref[width + h * HD : width + (h + 1) * HD, spot] = unspin(dk_ref[hs, spot], spot)
                d_ref[2 * width :, spot] = dv_ref[:, spot].astype(BF)
            finish(late)
            full = slice(0, n * block)
            rows = rows_ref[:n].reshape(n * block, -1)
            back = back_ref[:n].reshape(n * block, -1)
            pieces = [(k, d_ref[k * width : (k + 1) * width, full], rows) for k in range(3)]
            pieces.append((3, ctx_ref[:, full], back))
            for k, left, right in pieces:
                at = slice(k * width, (k + 1) * width)
                value = nn(left, right)
                if old:
                    pair = g_refs[k // 2 * 2 : k // 2 * 2 + 2]
                    put_halves(*pair, slice(k % 2 * width, (k % 2 + 1) * width), grad_ref[at] + value, orders[k // 2])
                else:
                    grad_ref[at] = value

    saves = []
    if not old:
        saves = [start(grad_ref, grad_out, out_sem.at[4])]
    else:
        saves = [start(ref, out, out_sem.at[4 + i]) for i, (ref, out) in enumerate(zip(g_refs[:2], g_outs[:2]))]

    def close(i, carry):
        turned = d_ref[:, aligned(i, block)].T
        out = nn(turned[:, : 2 * width], wa_ref[: 2 * width]) + nn(turned[:, 2 * width :], wb_ref[:width])
        held_ref[me ^ i] = out.astype(BF)
        send_block(me ^ i, held_ref, outs, out_sem)
        gain_ref[:1] += jnp.sum(out * rows_ref[i].astype(F32), axis=0, keepdims=True)
        return carry

    lax.fori_loop(0, count, close, 0)

    def blank(i, carry):
        await_slot(back_ref.at[i], sem.at[me ^ i])
        held_ref[me ^ i] = jnp.zeros(held_ref.shape[1:], BF)
        send_block(me ^ i, held_ref, outs, out_sem)
        return carry

    lax.fori_loop(count, 4, blank, 0)
    if old:
        put_halves(g_refs[2], g_refs[3], slice(2 * width, None), gain_ref[...], orders[1])
        saves += [start(ref, out, out_sem.at[6 + i]) for i, (ref, out) in enumerate(zip(g_refs[2:], g_outs[2:]))]
    finish(saves)
    sent_blocks(held_ref, outs, out_sem)


def ffn_kernel(
    where_ref, a0, a1, a2, a3, b0, b1, b2, b3, wu0, wu1, wg0, wg1, wo0, wo1,
    f0, f2, f13, n0, n2, n13, ub_out, gb_out, mixed_out, gain_ref,
    rows_ref, back_ref, fheld_ref, nheld_ref, ub_ref, gb_ref, mixed_ref, wu_ref, wg_ref, wo_ref, sem, out_sem,
    *, seq, outer, picks,
):
    me = where_ref[0]
    length = where_ref[1 + seq]
    block = rows_ref.shape[1]
    fouts = (f0, f13.at[0], f2, f13.at[1])
    nouts = (n0, n13.at[0], n2, n13.at[1])
    copies = fetch_halves(wu0, wu1, wu_ref, outer[0], sem, 8)
    aparts, bparts = picked((a0, a1, a2, a3), picks[:4]), picked((b0, b1, b2, b3), picks[4:])
    start(aparts[0], rows_ref.at[0], sem.at[0])
    copies += fetch_halves(wg0, wg1, wg_ref, outer[1], sem, 12)
    start(bparts[0], back_ref.at[0], sem.at[4])
    copies += fetch_halves(wo0, wo1, wo_ref, outer[2], sem, 16)
    for p in range(1, 4):
        start(aparts[p], rows_ref.at[p], sem.at[p])
        start(bparts[p], back_ref.at[p], sem.at[4 + p])
    gain_ref[...] = jnp.zeros(gain_ref.shape, F32)
    finish(copies)
    kept = ((ub_ref, ub_out), (gb_ref, gb_out), (mixed_ref, mixed_out))

    def step(p, carry):
        valid = (me ^ p) * block < length
        await_slot(rows_ref.at[p], sem.at[p])
        await_slot(back_ref.at[p], sem.at[4 + p])

        @pl.when(valid)
        def _():
            rows = rows_ref[p]
            up = nt(rows, wu_ref[...])
            gate = nt(rows, wg_ref[...])
            mb = nt(back_ref[p], wo_ref[...])
            phi = 0.5 + 0.5 * lax.erf(up * (0.5**0.5))
            act = up * phi
            mixed = (act * gate).astype(BF)
            mixed_ref[p] = mixed
            slope = phi + up * (jnp.exp(-0.5 * up * up) * (0.5 / np.pi) ** 0.5)
            ub = (mb * gate * slope).astype(BF)
            gb = (mb * act).astype(BF)
            ub_ref[p] = ub
            gb_ref[p] = gb
            out = nn(ub, wu_ref[...]) + nn(gb, wg_ref[...])
            nheld_ref[p] = out.astype(BF)
            gain_ref[1:2] += jnp.sum(out * rows.astype(F32), axis=0, keepdims=True)
            fheld_ref[p] = nn(mixed, wo_ref[...]).astype(BF)

        @pl.when(jnp.logical_not(valid))
        def _():
            for ref in (mixed_ref, ub_ref, gb_ref, nheld_ref, fheld_ref):
                ref[p] = jnp.zeros(ref.shape[1:], BF)

        send_block(p, nheld_ref, nouts, out_sem, 4)
        send_block(p, fheld_ref, fouts, out_sem)
        for k, (ref, out) in enumerate(kept):
            start(ref.at[p], out.at[p], out_sem.at[8 + 4 * k + p])
        return carry

    lax.fori_loop(0, 4, step, 0)
    sent_blocks(nheld_ref, nouts, out_sem, 4)
    sent_blocks(fheld_ref, fouts, out_sem)
    for k, (ref, out) in enumerate(kept):
        sent_blocks(ref, [out.at[p] for p in range(4)], out_sem, 8 + 4 * k)


def ffn_grad_kernel(_, *refs, orders, picks):
    parts, saved, refs = picked(refs[:16], picks), refs[16:22], refs[22:]
    outs, (rows_ref, back_ref, saved_ref, *held), refs = refs[:4], refs[4:11], refs[11:]
    g_ref, sem, out_sem = refs
    units = g_ref.shape[1]
    copies = []
    for s in range(2):
        rows = fetch(parts[8 * s : 8 * s + 4], lambda p: rows_ref.at[s, p], sem, 8 * s)
        backs = lambda: fetch(parts[8 * s + 4 : 8 * s + 8], lambda p: back_ref.at[s, p], sem, 8 * s + 4)
        kept = lambda k: fetch((saved[3 * s + k],), lambda p: saved_ref.at[s, k], sem, 16 + 3 * s + k)
        copies += [rows + kept(0), kept(1), kept(2) + backs()]
    sent = []
    for s in range(2):
        rows = rows_ref.at[s]
        for k in range(3):
            finish(copies[3 * s + k])
            other = (back_ref if k == 2 else rows_ref)[s].reshape(-1, rows_ref.shape[-1])
            part = tn(saved_ref[s, k].reshape(-1, units), other)
            if s == 0:
                g_ref[k] = part
                continue
            pair = held[k // 2 * 2 : k // 2 * 2 + 2]
            at = slice(None) if k == 2 else slice(k * units, (k + 1) * units)
            put_halves(*pair, at, g_ref[k] + part, orders[k // 2])
            if k > 0:
                sent += [start(ref, out, out_sem.at[k // 2 * 2 + i]) for i, (ref, out) in enumerate(zip(pair, outs[k // 2 * 2 :][:2]))]
    finish(sent)


SMEM = pl.BlockSpec(memory_space=pltpu.SMEM)
VMEM = pl.BlockSpec(memory_space=pltpu.VMEM)
HBM = pl.BlockSpec(memory_space=pl.ANY)
LIMIT = 60 * 1024 * 1024
PARAMS = pltpu.CompilerParams(vmem_limit_bytes=LIMIT)
GAIN_ROWS = 16


def shape(*dims, kind=BF):
    return jax.ShapeDtypeStruct(dims, kind)


def idle(where):
    return pl.pallas_call(
        lambda in_ref, out_ref: None,
        out_shape=jax.ShapeDtypeStruct(where.shape, where.dtype),
        in_specs=[pl.BlockSpec(memory_space=pl.ANY)],
        out_specs=pl.BlockSpec(memory_space=pl.ANY),
        input_output_aliases={0: 0},
        cost_estimate=pl.CostEstimate(flops=1 << 34, bytes_accessed=1 << 20, transcendentals=0),
        name="idle",
    )(where)


def partials(block, width):
    return (shape(block, width), shape(block, width), shape(2, block, width))


def vmem(array):
    return pltpu.VMEM(array.shape, array.dtype)


def attn_fwd(where, seq, parts, wa, wb, cos, sin):
    arrays, picks = zip(*parts)
    block, width = arrays[0].shape[-2:]
    rows = wb.halves[0].shape[0]
    cols = rows // 2
    heads = cols // HD
    full = 4 * block
    flops = 2 * full * width * cols * 4 + 4 * full * full * cols
    saved = (shape(4, block, width),) + (shape(cols, full),) * 4 + (shape(heads, 1, full, kind=F32),)
    return pl.pallas_call(
        functools.partial(attn_fwd_kernel, seq=seq, outer=(wa.outer, wb.outer), picks=picks),
        out_shape=partials(block, width) + saved,
        in_specs=[SMEM] + [HBM] * 10,
        out_specs=(HBM,) * 9,
        scratch_shapes=[
            pltpu.VMEM((4, block, width), BF),
            pltpu.VMEM(wa.halves[0].shape[:1] + (width,), BF),
            pltpu.VMEM((rows, width), BF),
            vmem(cos),
            vmem(sin),
            *[vmem(array) for array in saved],
            pltpu.VMEM((heads, full, HD), BF),
            pltpu.VMEM((4, block, width), BF),
            pltpu.SemaphoreType.DMA((14,)),
            pltpu.SemaphoreType.DMA((13,)),
        ],
        compiler_params=pltpu.CompilerParams(vmem_limit_bytes=58 << 20),
        cost_estimate=pl.CostEstimate(flops=flops * 3, bytes_accessed=12 << 20, transcendentals=heads * full * full),
        name="attn_fwd",
    )(where, *arrays, *wa.halves, *wb.halves, cos, sin)


def attn_bwd(where, seq, parts, saved, wa, wb, cos, sin, old, orders):
    arrays = [array for array, _ in parts]
    block, width = arrays[0].shape
    rows = wb.halves[0].shape[0]
    cols = rows // 2
    heads = cols // HD
    full = 4 * block
    flops = 4 * full * width * cols * 4 + 10 * full * full * cols
    extra = [] if old is None else list(old)
    grads = shape(4 * cols, width, kind=F32)
    gain = shape(GAIN_ROWS, width, kind=F32)
    halved = (shape(rows, width // 2),) * 2 + (shape(rows + GAIN_ROWS, width // 2),) * 2
    outs = (grads,) if old is None else halved
    return pl.pallas_call(
        functools.partial(
            attn_bwd_kernel,
            seq=seq,
            old=old is not None,
            orders=orders,
            outer_w=(wa.outer, wb.outer),
        ),
        out_shape=partials(block, width) + outs + (() if extra else (gain,)),
        in_specs=[SMEM] + [HBM] * 16 + ([] if old is None else [HBM, VMEM]),
        out_specs=(HBM,) * (3 + len(outs)) + (() if extra else (VMEM,)),
        scratch_shapes=[vmem(array) for array in ((grads,) if old is None else halved + (gain, grads))] + [
            pltpu.VMEM(wa.halves[0].shape[:1] + (width,), BF),
            pltpu.VMEM((rows, width), BF),
            *[vmem(array) for array in saved],
            vmem(cos),
            vmem(sin),
            pltpu.VMEM((4, block, width), BF),
            pltpu.VMEM((cols, full), BF),
            pltpu.VMEM((heads, full, HD), BF),
            pltpu.VMEM((heads, full, HD), BF),
            pltpu.VMEM((3 * cols, full), BF),
            pltpu.VMEM((cols, full), F32),
            pltpu.VMEM((cols, full), F32),
            pltpu.VMEM((heads, 1, full), F32),
            pltpu.VMEM((4, block, width), BF),
            pltpu.SemaphoreType.DMA((21,)),
            pltpu.SemaphoreType.DMA((8,)),
        ],
        compiler_params=pltpu.CompilerParams(vmem_limit_bytes=32 << 20),
        cost_estimate=pl.CostEstimate(flops=flops * 3, bytes_accessed=16 << 20, transcendentals=heads * full * full),
        name="attn_bwd",
    )(where, *arrays, *wa.halves, *wb.halves, *saved, cos, sin, *extra)


def ffn(where, seq, parts, backs, weights):
    arrays, picks = zip(*parts, *backs)
    block, width = arrays[0].shape[-2:]
    units = weights[0].halves[0].shape[0]
    flops = 2 * 4 * block * width * units * 6
    saved = (shape(4, block, units),) * 3
    return pl.pallas_call(
        functools.partial(ffn_kernel, seq=seq, outer=[w.outer for w in weights], picks=picks),
        out_shape=partials(block, width) * 2 + saved + (shape(GAIN_ROWS, width, kind=F32),),
        in_specs=[SMEM] + [HBM] * 14,
        out_specs=(HBM,) * 9 + (VMEM,),
        scratch_shapes=[pltpu.VMEM((4, block, width), BF)] * 4
        + [vmem(array) for array in saved]
        + [pltpu.VMEM((units, width), BF)] * 3
        + [pltpu.SemaphoreType.DMA((20,)), pltpu.SemaphoreType.DMA((20,))],
        compiler_params=pltpu.CompilerParams(vmem_limit_bytes=58 << 20),
        cost_estimate=pl.CostEstimate(flops=flops, bytes_accessed=20 << 20, transcendentals=2 * 4 * block * units),
        name="ffn",
    )(where, *arrays, *[half for w in weights for half in w.halves])


def ffn_grad(where, parts, saved, orders):
    arrays, picks = zip(*parts)
    block, width = arrays[0].shape[-2:]
    units = saved[0].shape[2]
    outs = (shape(2 * units, width // 2),) * 2 + (shape(units, width // 2),) * 2
    return pl.pallas_call(
        functools.partial(ffn_grad_kernel, orders=orders, picks=picks),
        out_shape=outs,
        in_specs=[SMEM] + [HBM] * 22,
        out_specs=(HBM,) * 4,
        scratch_shapes=[pltpu.VMEM((2, 4, block, width), BF)] * 2
        + [pltpu.VMEM((2, 3) + saved[0].shape, BF)]
        + [vmem(array) for array in outs]
        + [pltpu.VMEM((3, units, width), F32), pltpu.SemaphoreType.DMA((22,)), pltpu.SemaphoreType.DMA((4,))],
        compiler_params=pltpu.CompilerParams(vmem_limit_bytes=40 << 20),
        cost_estimate=pl.CostEstimate(flops=2 * 8 * block * width * units * 3, bytes_accessed=24 << 20, transcendentals=0),
        name="ffn_grad",
    )(where, *arrays, *saved)


def norm_parts(values):
    average = jnp.mean(values, axis=-1, keepdims=True)
    centred = values - average
    spread = jnp.mean(centred * centred, axis=-1, keepdims=True)
    scale = lax.rsqrt(spread + norm_eps)
    return centred * scale, scale


def norm_back(grad, gain, normed, scale):
    y = grad * gain
    return scale * (
        y - jnp.mean(y, axis=-1, keepdims=True) - normed * jnp.mean(y * normed, axis=-1, keepdims=True)
    )


def rope_tables(length):
    places = np.arange(length, dtype=np.float32)
    frequency = (rope_base ** (-np.arange(0, HD, 2, dtype=np.float32) / HD)).astype(np.float32)
    angles = (frequency[:, None] * places[None, :]).astype(np.float32)
    return jnp.asarray(np.cos(angles)), jnp.asarray(np.sin(angles))


def per_device(
    tokens, lengths, attn_norm, qkv_weight, attn_out_weight, ffn_norm, ffn_in_weight, ffn_out_weight, out_grad
):
    seqs, local_len, width = tokens.shape
    assert lax.axis_size("mp") == 4 and seqs == 2
    groups = lax.axis_size("dp")
    me = lax.axis_index("mp")
    full_len = 4 * local_len
    cols = qkv_weight.shape[2]
    units = ffn_in_weight.shape[2]
    span = width // groups
    cos, sin = rope_tables(full_len)

    ranks = rank_order(groups)
    order = jnp.asarray(np.array(ranks, np.int32)) ^ lax.axis_index("dp")
    source = (order[:, None] * span + jnp.arange(span, dtype=jnp.int32)[None, :]).reshape(width)
    reorder = (source[None, :] == jnp.arange(width, dtype=jnp.int32)[:, None]).astype(BF)

    def to_own(rows):
        return jnp.dot(rows.reshape(-1, width), reorder, preferred_element_type=F32).astype(BF).reshape(rows.shape)

    def from_own(rows):
        return lax.dot_general(
            rows, reorder, (((1,), (1,)), ((), ())), preferred_element_type=F32
        ).astype(BF)

    far, near = gather_order(4, 2, 1), gather_order(1, 4, 2)
    qkv = jnp.swapaxes(qkv_weight, 1, 2)
    ffn_in = jnp.swapaxes(ffn_in_weight, 1, 2)
    own_gains = jnp.stack([attn_norm, ffn_norm])
    own_gains = jnp.pad(own_gains, ((0, 14), (0, 0)))
    wa = Gather(jnp.concatenate([qkv[:2].reshape(2 * cols, span), own_gains], axis=0), far, "w_qk")
    wb = Gather(jnp.concatenate([qkv[2], attn_out_weight], axis=0), near, "w_vo")
    w_up = Gather(ffn_in[0], far, "w_up")
    w_gate = Gather(ffn_in[1], far, "w_gate")
    w_out = Gather(ffn_out_weight, near, "w_out")

    local = me * local_len + jnp.arange(local_len, dtype=jnp.int32)
    where = jnp.concatenate([me[None], lengths]).astype(jnp.int32)
    valid = [(local < lengths[s]).astype(F32)[:, None] for s in range(seqs)]
    token_low = [to_own(tokens[s]) for s in range(seqs)]
    token = [SeqRows(token_low[s], f"token{s}") for s in range(seqs)]

    _, (where, token[1].across.value, out_grad, w_out.value) = stage(
        [wa, w_up, token[0].across, wb, token[0].beside],
        None,
        where, token[1].across.value, out_grad, w_out.value,
    )

    def prepare():
        return *[(valid[s] * to_own(out_grad[s]).astype(F32)).astype(BF) for s in range(seqs)], idle(where)

    (*back_low, where), (token_low,) = stage(
        [wb, token[1].across, wa, w_out, token[0].diag()], prepare, token_low
    )
    outback = [SeqRows(back_low[s], f"outback{s}") for s in range(seqs)]
    _, (where, w_gate.value) = stage(
        [wb, wa, outback[0].across, token[1].beside, token[1].diag()], None, where, w_gate.value
    )
    ffn_gain = join([half[2 * cols + 1 : 2 * cols + 2] for half in wa.halves]).astype(F32)
    attn_gain = join([half[2 * cols : 2 * cols + 1] for half in wa.halves]).astype(F32)

    done, (where,) = stage(
        [outback[1].across, w_up, w_gate, outback[0].beside, outback[1].beside],
        lambda: attn_fwd(where, 0, token[0].parts(), wa, wb, cos, sin),
        where,
    )
    attn = [Sums(*done[:3], "attn0")]
    saved = [done[3:]]
    stage_turn = lambda sums, *others: stage([sums.turn, *others], lambda: (), where)
    _, (where,) = stage_turn(attn[0])
    done, (where,) = stage(
        [attn[0].away(), w_up, w_gate, w_out],
        lambda: attn_fwd(where, 1, token[1].parts(), wa, wb, cos, sin),
        where,
    )
    attn.append(Sums(*done[:3], "attn1"))
    saved.append(done[3:])

    def second_norm(s):
        rows = token_low[s].astype(F32) + attn[s].total()
        normed, scale = norm_parts(rows)
        return rows, normed, scale, (normed * ffn_gain).astype(BF)

    hidden, second, two = [None, None], [None, None], [None, None]

    (done,), (where,) = stage([attn[1].turn], lambda: (second_norm(0),), where)
    hidden[0], second[0] = done[0], done[1:3]
    two[0] = SeqRows(done[3], "two0")
    _, (where,) = stage([two[0].across, attn[1].away(), w_out, w_gate, two[0].beside, outback[0].diag(), outback[1].diag()], None, where)
    (done,), (where,) = stage([two[0].diag()], lambda: (second_norm(1),), where)
    hidden[1], second[1] = done[0], done[1:3]
    two[1] = SeqRows(done[3], "two1")
    weights = (w_up, w_gate, w_out)
    done, (where,) = stage(
        [two[1].across, two[1].beside],
        lambda: ffn(where, 0, two[0].parts(), outback[0].parts(), weights),
        where,
    )
    ff, twoback = [Sums(*done[:3], "ff0")], [Sums(*done[3:6], "twoback0")]
    ffn_saved, ffn_gains = list(done[6:9]), done[9]
    _, (where,) = stage_turn(twoback[0], two[1].diag())
    done, (where,) = stage(
        [twoback[0].away(), ff[0].turn],
        lambda: ffn(where, 1, two[1].parts(), outback[1].parts(), weights),
        where,
    )
    ff.append(Sums(*done[:3], "ff1"))
    twoback.append(Sums(*done[3:6], "twoback1"))
    ffn_saved += done[6:9]
    ffn_gains = ffn_gains + done[9]

    def second_back(s):
        rows = back_low[s].astype(F32) + norm_back(twoback[s].total(), ffn_gain, *second[s])
        return rows, rows.astype(BF)

    hidden_back, hidback = [None, None], [None, None]
    (done,), (where,) = stage([twoback[1].turn], lambda: (second_back(0),), where)
    hidden_back[0] = done[0]
    hidback[0] = SeqRows(done[1], "hidback0")
    orders = (scatter_order(2, 4, 1), scatter_order(1, 2, 4))

    def weight_grads():
        grads = ffn_grad(
            where, [p for s in range(seqs) for p in two[s].parts() + outback[s].parts()], ffn_saved, orders
        )
        return grads


    def weight_grads():
        parts = [p for s in range(seqs) for p in two[s].parts() + outback[s].parts()]
        grads = ffn_grad(where, parts, ffn_saved, orders)
        turned = exchange(ff[1].turn.value, "mp", 1, ff[1].turn.name)
        terms = (ff[0].far, ff[0].turn.got, ff[1].far, turned)
        terms = lax.optimization_barrier((terms, grads[0]))[0]
        sums = [(terms[k].astype(F32) + terms[k + 1][1].astype(F32)).astype(BF) for k in (0, 2)]
        return *grads, turned, *sums

    done, (where,) = stage(
        [twoback[1].away(), hidback[0].across, hidback[0].beside], weight_grads, where
    )
    *done, ff[1].turn.got, away0, away1 = done
    ff[0].last, ff[1].last = (Move(a, "mp", 2, f"ff{s}") for s, a in enumerate((away0, away1)))
    g_in = Scatter(*done[:2], orders[0], "g_in")
    g_out = Scatter(*done[2:4], orders[1], "g_out")
    (done,), (where,) = stage([hidback[0].diag()], lambda: (second_back(1),), where)
    hidden_back[1] = done[0]
    hidback[1] = SeqRows(done[1], "hidback1")

    orders = (scatter_order(1, 2, 4), scatter_order(2, 4, 1))
    done, (where,) = stage(
        [g_in, g_out, hidback[1].across, ff[0].last, hidback[1].beside],
        lambda: attn_bwd(where, 0, hidback[0].parts(), saved[0], wa, wb, cos, sin, None, orders),
        where,
    )
    oneback = [Sums(*done[:3], "oneback0")]
    sums = [done[3], done[4] + ffn_gains]
    _, (where,) = stage_turn(oneback[0], hidback[1].diag())
    done, (where, token_low) = stage(
        [g_in, oneback[0].away(), ff[1].last, g_out],
        lambda: attn_bwd(where, 1, hidback[1].parts(), saved[1], wa, wb, cos, sin, sums, orders),
        where, token_low,
    )
    oneback.append(Sums(*done[:3], "oneback1"))
    g_qk = Scatter(*done[3:5], orders[0], "g_qk")
    g_vo = Scatter(*done[5:7], orders[1], "g_vo")
    def close(s):
        return (hidden_back[s] + norm_back(oneback[s].total(), attn_gain, *norm_parts(token_low[s].astype(F32)))).astype(BF)

    def ready():
        rows = [(valid[s] * (hidden[s] + ff[s].total())).astype(BF) for s in range(seqs)]
        return from_own(jnp.concatenate(rows, axis=0)), close(0)

    (output, input_grad), (where,) = stage([g_vo, g_qk, g_out, oneback[1].turn], ready, where)
    _, (where,) = stage([g_vo, oneback[1].away(), g_qk, g_in], None, where)
    stage([g_vo, g_qk], None, where)
    grad_qk, grad_vo = g_qk.end(), g_vo.end()
    gain_back = grad_vo[2 * cols : 2 * cols + 2]
    ones, twos, threes = (exchange(gain_back, "mp", k, "gain") for k in (1, 2, 3))
    gain_back = (gain_back + ones) + (twos + threes)
    input_grad = from_own(jnp.concatenate([input_grad, close(1)], axis=0))
    grad_qkv = jnp.concatenate([grad_qk, grad_vo[:cols]], axis=0).reshape(3, cols, span)
    return (
        output.reshape(seqs, local_len, width),
        input_grad.reshape(seqs, local_len, width),
        gain_back[0] / attn_norm.astype(F32),
        jnp.swapaxes(grad_qkv, 1, 2),
        grad_vo[cols : 2 * cols],
        gain_back[1] / ffn_norm.astype(F32),
        jnp.swapaxes(g_in.end().reshape(2, units, span), 1, 2),
        g_out.end(),
    )


def solution(mesh):
    in_specs = (
        P("dp", "mp", None),
        P("dp"),
        P("dp"),
        P(None, "dp", "mp"),
        P("mp", "dp"),
        P("dp"),
        P(None, "dp", "mp"),
        P("mp", "dp"),
        P("dp", "mp", None),
    )
    out_specs = (
        P("dp", "mp", None),
        P("dp", "mp", None),
        P("dp"),
        P(None, "dp", "mp"),
        P("mp", "dp"),
        P("dp"),
        P(None, "dp", "mp"),
        P("mp", "dp"),
    )
    return jax.shard_map(
        per_device, mesh=mesh, in_specs=in_specs, out_specs=out_specs, check_vma=False
    )
```
